512 devices in a mesh: gx: 32 (over x, z), gy: 16 (over y, core).
Axes of the slice: x: 4, y: 8, z: 8, core: 2. Of those that a mesh axis runs over, the one named last changes fastest.
Arguments:
- rhs: float32 [128, 128, 512], P('gx', 'gy'), may hold values from -6 to 6
- alpha: float32 [128, 128, 512], P('gx', 'gy'), may hold values from 0.0001 to 4
- beta_x: float32 [128, 128, 512], P('gx', 'gy'), may hold values from 0.5 to 2
- beta_y: float32 [128, 128, 512], P('gx', 'gy'), may hold values from 0.5 to 2
- beta_z: float32 [128, 128, 512], P('gx', 'gy'), may hold values from 0.5 to 2
Outputs:
- fine_solution: float32 [128, 128, 512], P('gx', 'gy')
- coarse_correction: float32 [32, 32, 128], P('gx', 'gy')
The draws below stay inside these ranges and needn't reach their ends.
All inputs are finite; a program needn't handle non-finite values.
Results may differ from the reference program's by a relative error of at most 0.00002.
Values sent between devices are 32-bit elements; how exact they have to be, the bound alone decides.
No kernel may reach another device: no remote copies, remote signals or barrier semaphores. Data moves between devices by JAX's collectives and lax.ppermute only.
A program may use at most 64 MiB of HBM per device.

```python
import math
import jax
import jax.numpy as jnp
from jax import lax

SWEEPS = 4
COARSE_SWEEPS = 8
NX = 128
NY = 128
NZ = 512


def draw_rhs(key, part):
    shape = (NX, NY, NZ)
    values = jnp.clip(2.0 * jax.random.normal(key, shape, jnp.float32), -6.0, 6.0)
    return values.astype(jnp.float32)


def draw_alpha(key, part):
    shape = (NX, NY, NZ)
    key_low, key_high, key_pick = jax.random.split(key, 3)
    background = jnp.exp(jax.random.uniform(key_low, shape, jnp.float32, math.log(0.0001), math.log(0.001)))
    stiff = jnp.exp(jax.random.uniform(key_high, shape, jnp.float32, 0.0, math.log(4.0)))
    picked = jax.random.uniform(key_pick, shape, jnp.float32) < 1.0 / 2048.0
    return jnp.where(picked, stiff, background).astype(jnp.float32)


def steps_of(own_key, dims, pieces, smallest, top_value):
    factor_of, own = 1.0, jax.random.fold_in(own_key, 6)
    for dim, blocks in pieces:
        steps = jnp.exp(jax.random.uniform(jax.random.fold_in(own, dim), (blocks,), jnp.float32, smallest / len(pieces), top_value / len(pieces)))
        factor_of = factor_of * jnp.repeat(steps, dims[dim] // blocks).reshape([-1 if axis == dim else 1 for axis in range(len(dims))])
    return factor_of


def setup_inputs(seed: int = 0) -> dict:
    seeds = jax.random.split(jax.random.key(seed), 6)
    return {
        "rhs": draw_rhs(jax.random.fold_in(seeds[5], 71), 0),
        "alpha": draw_alpha(jax.random.fold_in(seeds[5], 71), 0),
        "beta_x": jnp.clip(jnp.exp(math.log(2.0) - 1.3862944 * jax.random.uniform(seeds[2], (NX, NY, NZ), jnp.float32) ** steps_of(seeds[2], (NX, NY, NZ), ((0, 32), (1, 16)), -0.2, 0.2)), 0.5, 2.0),
        "beta_y": jnp.clip(jnp.exp(math.log(2.0) - 1.3862944 * jax.random.uniform(seeds[3], (NX, NY, NZ), jnp.float32) ** steps_of(seeds[3], (NX, NY, NZ), ((0, 32), (1, 16)), -0.2, 0.2)), 0.5, 2.0),
        "beta_z": jnp.clip(jnp.exp(math.log(2.0) - 1.3862944 * jax.random.uniform(seeds[4], (NX, NY, NZ), jnp.float32) ** steps_of(seeds[4], (NX, NY, NZ), ((0, 32), (1, 16)), -0.2, 0.2)), 0.5, 2.0),
    }


def upper_faces(beta, axis_pos):
    rest = lax.slice_in_dim(beta, 1, beta.shape[axis_pos], axis=axis_pos)
    zero_layer = jnp.zeros_like(lax.slice_in_dim(beta, 0, 1, axis=axis_pos))
    return jnp.concatenate([rest, zero_layer], axis=axis_pos)


def coarsen_face(faces, axis_pos, upper):
    size_x, size_y, size_z = faces.shape
    blocks = faces.reshape(size_x // 2, 2, size_y // 2, 2, size_z // 2, 2)
    taken = 2 * axis_pos + 1
    picked = jnp.take(blocks, upper, axis=taken)
    others = tuple(pair - 1 if pair > taken else pair for pair in (1, 3, 5) if pair != taken)
    return jnp.mean(picked, axis=others) * 0.25


def coarsen_all(faces):
    return tuple(coarsen_face(faces[number], number // 2, number % 2) for number in range(6))


def restrict(field):
    size_x, size_y, size_z = field.shape
    return jnp.mean(field.reshape(size_x // 2, 2, size_y // 2, 2, size_z // 2, 2), axis=(1, 3, 5))


def prolong(field):
    return jnp.repeat(jnp.repeat(jnp.repeat(field, 2, 0), 2, 1), 2, 2)


def beside_sum(padded, faces):
    total = faces[0] * padded[:-2, 1:-1, 1:-1] + faces[1] * padded[2:, 1:-1, 1:-1]
    total = total + faces[2] * padded[1:-1, :-2, 1:-1] + faces[3] * padded[1:-1, 2:, 1:-1]
    total = total + faces[4] * padded[1:-1, 1:-1, :-2] + faces[5] * padded[1:-1, 1:-1, 2:]
    return total


def diagonal_of(cell_coef, faces):
    total = cell_coef
    for face in faces:
        total = total + face
    return total


def red_cells(shape, offset_x, offset_y):
    index_x = jnp.arange(shape[0], dtype=jnp.int32) + offset_x
    index_y = jnp.arange(shape[1], dtype=jnp.int32) + offset_y
    index_z = jnp.arange(shape[2], dtype=jnp.int32)
    return (index_x[:, None, None] + index_y[None, :, None] + index_z[None, None, :]) % 2 == 0


def smooth(field, source, inverse, faces, red_mask, count):
    for sweep_index in range(count):
        for colour in (True, False):
            beside = beside_sum(jnp.pad(field, 1), faces)
            field = jnp.where(red_mask == colour, (source + beside) * inverse, field)
    return field


def residual_of(field, source, diagonal, faces):
    return source - (diagonal * field - beside_sum(jnp.pad(field, 1), faces))


def reference(rhs, alpha, beta_x, beta_y, beta_z):
    faces_fine = (beta_x, upper_faces(beta_x, 0), beta_y, upper_faces(beta_y, 1), beta_z, upper_faces(beta_z, 2))
    diagonal_fine = diagonal_of(alpha, faces_fine)
    smoothed = smooth(jnp.zeros_like(rhs), rhs, 1.0 / diagonal_fine, faces_fine, red_cells(rhs.shape, 0, 0), SWEEPS)
    source_mid = restrict(residual_of(smoothed, rhs, diagonal_fine, faces_fine))
    coef_mid = restrict(alpha)
    faces_mid = coarsen_all(faces_fine)
    diagonal_mid = diagonal_of(coef_mid, faces_mid)
    level_mid = smooth(jnp.zeros_like(source_mid), source_mid, 1.0 / diagonal_mid, faces_mid, red_cells(source_mid.shape, 0, 0), SWEEPS)
    source_low = restrict(residual_of(level_mid, source_mid, diagonal_mid, faces_mid))
    coef_low = restrict(coef_mid)
    faces_low = coarsen_all(faces_mid)
    inverse_low = 1.0 / diagonal_of(coef_low, faces_low)
    coarse = smooth(jnp.zeros_like(source_low), source_low, inverse_low, faces_low, red_cells(source_low.shape, 0, 0), COARSE_SWEEPS)
    corrected = level_mid + prolong(coarse)
    return smoothed + prolong(corrected), coarse
```

```python
import jax
import jax.numpy as jnp
from jax import lax
from jax.experimental import pallas as pl
from jax.experimental.pallas import tpu as pltpu
from jax.sharding import PartitionSpec as P

F32 = jnp.float32
RHS, ALPHA, BX, BY, BZ = range(5)


def shifted(values, axis, name, steps):
    count = lax.axis_size(name)
    lead, last = max(0, -steps), min(count, count - steps)
    return lax.ppermute(values, name, [(i, i + steps) for i in range(lead, last)])


def call(kernel, outs, scratch=(), smem=()):
    def run(*args):
        specs = [
            pl.BlockSpec(memory_space=pltpu.SMEM if i in smem else pltpu.VMEM)
            for i in range(len(args))
        ]
        shapes = [jax.ShapeDtypeStruct(s, F32) for s in outs]
        return pl.pallas_call(
            kernel,
            out_shape=shapes,
            in_specs=specs,
            out_specs=[pl.BlockSpec(memory_space=pltpu.VMEM)] * len(outs),
            scratch_shapes=[pltpu.VMEM(s, F32) for s in scratch],
        )(*args)

    return run


def iotas(shape):
    return lax.broadcasted_iota(jnp.int32, shape, 0), lax.broadcasted_iota(jnp.int32, shape, 1)


def even_mask(shape):
    row, lane = iotas(shape)
    return ((row + lane) & 1) == 0


def half(x):
    return pltpu.roll(x, 4, 0)


def prev_row(x):
    return pltpu.roll(x, 1, 0)


def next_row(x):
    return pltpu.roll(x, x.shape[0] - 1, 0)


def prev_lane(x):
    return pltpu.roll(x, 1, 1)


def next_lane(x):
    return pltpu.roll(x, x.shape[1] - 1, 1)


def exact_dot(a, b):
    return jnp.dot(a, b, precision=lax.Precision.HIGHEST, preferred_element_type=F32)


def one_hot(shape, test):
    row, col = iotas(shape)
    return jnp.where(test(row, col), 1.0, 0.0).astype(F32)


def low_rows(shape):
    row, _ = iotas(shape)
    return (row & 7) < 4


S_R, S_B, WP, WO_R, WO_B, YM_R, YM_B, YP_R, YP_B, ZM_R, ZM_B, ZP_R, ZP_B, I_R, I_B, D_R, D_B = range(17)


def beside(co, src, p, red, q0):
    v = src[p + 1]
    before, after = src[p], src[p + 2]
    other = jnp.where(q0, before, after) if red else jnp.where(q0, after, before)
    wo, ym, yp, zm, zp = (
        (WO_R, YM_R, YP_R, ZM_R, ZP_R) if red else (WO_B, YM_B, YP_B, ZM_B, ZP_B)
    )
    total = co[WP, p] * v + co[wo, p] * other
    total = total + (co[ym, p] * prev_row(v) + co[yp, p] * next_row(v))
    return total + (co[zm, p] * prev_lane(v) + co[zp, p] * next_lane(v))


def relax(co, dst, src, pairs, red, q0):
    s, inv = (S_R, I_R) if red else (S_B, I_B)
    for p in pairs:
        dst[p + 1] = (co[s, p] + beside(co, src, p, red, q0)) * co[inv, p]


def first_red(co, dst, pairs):
    for p in pairs:
        dst[p + 1] = co[S_R, p] * co[I_R, p]


def residual(co, r, b, p, q0):
    red = co[S_R, p] - (co[D_R, p] * r[p + 1] - beside(co, b, p, True, q0))
    black = co[S_B, p] - (co[D_B, p] * b[p + 1] - beside(co, r, p, False, q0))
    return red, black


def put_faces(co, p, q0, bx, by, bz):
    b0, b1, b2 = bx
    wo_r, wo_b = jnp.where(q0, b0, b2), jnp.where(q0, b2, b0)
    y_r, y_b = jnp.where(q0, by[0], by[1]), jnp.where(q0, by[1], by[0])
    z_r, z_b = jnp.where(q0, bz[0], bz[1]), jnp.where(q0, bz[1], bz[0])
    yp_r, yp_b = next_row(y_b), next_row(y_r)
    row, lane = iotas(q0.shape)
    first, last = lane == 0, lane == q0.shape[1] - 1
    zp_r, zp_b = jnp.where(last, 0.0, next_lane(z_b)), jnp.where(last, 0.0, next_lane(z_r))
    co[WP, p], co[WO_R, p], co[WO_B, p] = b1, wo_r, wo_b
    co[YM_R, p], co[YM_B, p] = y_r, y_b
    co[ZM_R, p], co[ZM_B, p] = jnp.where(first, 0.0, z_r), jnp.where(first, 0.0, z_b)
    co[ZP_R, p], co[ZP_B, p] = zp_r, zp_b
    return (b1 + wo_r, b1 + wo_b), (y_r, y_b), (yp_r, yp_b), (z_r + zp_r, z_b + zp_b)


def pack_rows_kernel(n_extra, left, own, right, to_low, to_high):
    arrays, planes = own.shape[0], own.shape[1]
    keep = low_rows((8, own.shape[3]))
    for a in range(arrays):
        for k, block in enumerate((left, own, right)):
            for x in range(0, planes, 2):
                t = a * (3 * planes // 2) + (k * planes + x) // 2
                e0, e1 = block[a, x], block[a, x + 1]
                to_low[t] = jnp.where(keep, e0, half(e1))
                to_high[t] = jnp.where(keep, half(e1), e0)
    if n_extra:
        base = arrays * 3 * planes // 2
        for x in range(0, planes, 2):
            e0, e1 = next_row(own[BY, x]), next_row(own[BY, x + 1])
            to_low[base + x // 2] = jnp.where(keep, e0, half(e1))


def halo_tile(from_low, from_high, t, odd, keep):
    high, low = from_high[t], from_low[t]
    if odd:
        high, low = half(high), half(low)
    return jnp.where(keep, high, low)


def fine_setup(co, left, own, right, beyond, from_low, from_high, q0):
    keep = low_rows((8, own.shape[3]))
    q0t = q0[:8]
    blocks = (left, own, right)

    def plane(a, x):
        return jnp.concatenate(
            [blocks[x // 4][a, x % 4], halo_tile(from_low, from_high, a * 6 + x // 2, x % 2, keep)], 0
        )

    bx0 = plane(BX, 0)
    for p in range(6):
        e0, e1 = plane(RHS, 2 * p), plane(RHS, 2 * p + 1)
        co[S_R, p], co[S_B, p] = jnp.where(q0, e0, e1), jnp.where(q0, e1, e0)
        b1 = plane(BX, 2 * p + 1)
        if p < 5:
            b2 = plane(BX, 2 * p + 2)
        else:
            b2 = jnp.concatenate([beyond[...], jnp.zeros_like(beyond[...])], 0)
        by = plane(BY, 2 * p), plane(BY, 2 * p + 1)
        bz = plane(BZ, 2 * p), plane(BZ, 2 * p + 1)
        fx, fy, fyp, fz = put_faces(co, p, q0, (bx0, b1, b2), by, bz)
        bx0 = b2
        yp_r, yp_b = fyp
        if p in (2, 3):
            up = from_high[30 + p - 2]
            u0, u1 = up, half(up)
            up_r, up_b = jnp.where(q0t, u0, u1), jnp.where(q0t, u1, u0)
            yp_r = jnp.concatenate([yp_r[:8], jnp.where(keep, up_r, yp_r[8:])], 0)
            yp_b = jnp.concatenate([yp_b[:8], jnp.where(keep, up_b, yp_b[8:])], 0)
        co[YP_R, p], co[YP_B, p] = yp_r, yp_b
        e0, e1 = plane(ALPHA, 2 * p), plane(ALPHA, 2 * p + 1)
        a_r, a_b = jnp.where(q0, e0, e1), jnp.where(q0, e1, e0)
        d_r = a_r + ((fx[0] + fz[0]) + (fy[0] + yp_r))
        d_b = a_b + ((fx[1] + fz[1]) + (fy[1] + yp_b))
        co[D_R, p], co[D_B, p] = d_r, d_b
        co[I_R, p] = jnp.where(a_r > 0.0, 1.0 / jnp.where(a_r > 0.0, d_r, 1.0), 0.0)
        co[I_B, p] = jnp.where(a_b > 0.0, 1.0 / jnp.where(a_b > 0.0, d_b, 1.0), 0.0)


def clear_guards(r, b, n):
    for ref in (r, b):
        ref[0] = jnp.zeros_like(ref[0])
        ref[n + 1] = jnp.zeros_like(ref[n + 1])


def fine_first_kernel(left, own, right, beyond, from_low, from_high, red_out, co, r, b):
    q0 = even_mask(r.shape[1:])
    clear_guards(r, b, 6)
    fine_setup(co, left, own, right, beyond, from_low, from_high, q0)
    first_red(co, r, range(6))
    relax(co, b, r, range(6), False, q0)
    relax(co, r, b, range(1, 5), True, q0)
    relax(co, b, r, range(1, 5), False, q0)
    relax(co, r, b, range(2, 4), True, q0)
    red_out[0, 0] = r[3][:8]
    red_out[0, 1] = r[4][:8]


def fine_second_kernel(
    left, own, right, beyond, from_low, from_high,
    red_left, red_own, red_right, red_low, red_high,
    fine_out, mid_out, own_out, co, r, b,
):
    size_z = own.shape[3]
    mid_z = size_z // 2
    q0 = even_mask(r.shape[1:])
    keep = low_rows((8, size_z))
    clear_guards(r, b, 6)
    fine_setup(co, left, own, right, beyond, from_low, from_high, q0)
    reds = (red_left, red_own, red_right)
    for p in range(6):
        tile = halo_tile(red_low, red_high, p // 2, p % 2, keep)
        r[p + 1] = jnp.concatenate([reds[p // 2][0, p % 2], tile], 0)
    relax(co, b, r, range(6), False, q0)
    relax(co, r, b, range(1, 5), True, q0)
    relax(co, b, r, range(1, 5), False, q0)
    sums = []
    for p in (2, 3):
        red, black = residual(co, r, b, p, q0)
        sums.append((red + black)[:8])
        fine_out[0, p - 2] = r[p + 1][:8]
        fine_out[1, p - 2] = b[p + 1][:8]
    z_sum = one_hot((size_z, mid_z), lambda i, j: (i >> 1) == j)
    z_even = one_hot((size_z, mid_z), lambda i, j: i == 2 * j)
    y_sum = one_hot((8, 16), lambda i, j: (j >> 1) == i)
    y_even = one_hot((8, 16), lambda i, j: j == 2 * i)
    zeros8 = jnp.zeros((8, size_z), F32)
    alphas = [own[ALPHA, 2 * i] + own[ALPHA, 2 * i + 1] for i in range(2)]
    bys = [own[BY, 2 * i] + own[BY, 2 * i + 1] for i in range(2)]
    by_next = []
    for i in range(2):
        t = BY * 6 + 2 + i
        h = from_high[t]
        by_next.append(h + half(h))
    bzs = [own[BZ, 2 * i] + own[BZ, 2 * i + 1] for i in range(2)]
    bxs = [own[BX, 0], own[BX, 2], right[BX, 0]]
    stacked = jnp.concatenate([*sums, *alphas, *bys, *by_next, *bxs, zeros8], 0)
    along_z = exact_dot(stacked, z_sum)
    bz_z = exact_dot(jnp.concatenate(bzs, 0), z_even)
    source = exact_dot(y_sum, along_z[0:16]) * 0.125
    alpha = exact_dot(y_sum, along_z[16:32]) * 0.125
    y_lower = exact_dot(y_even, along_z[32:48]) * 0.0625
    y_next = one_hot((8, 16), lambda i, j: ((i & 3) < 3) & (j == 2 * i + 2))
    y_last = one_hot((8, 16), lambda i, j: ((i & 3) == 3) & (j == 8 * (i >> 2)))
    y_upper = (exact_dot(y_next, along_z[32:48]) + exact_dot(y_last, along_z[48:64])) * 0.0625
    x_lower = exact_dot(y_sum, along_z[64:80]) * 0.0625
    x_upper = exact_dot(y_sum, along_z[72:88]) * 0.0625
    z_lower = exact_dot(y_sum, bz_z) * 0.0625
    _, lane = iotas(z_lower.shape)
    z_upper = jnp.where(lane == mid_z - 1, 0.0, next_lane(z_lower))
    diagonal = alpha + ((x_lower + x_upper) + (y_lower + y_upper) + (z_lower + z_upper))
    mid_out[0] = source
    mid_out[1] = 1.0 / diagonal
    mid_out[2] = x_lower
    mid_out[3] = y_lower
    mid_out[4] = z_lower
    own_out[0] = diagonal
    own_out[1] = alpha


def mid_setup(co, cat, low, high, q0):
    size_z = q0.shape[1]
    keep = low_rows((8, size_z))
    zero = jnp.zeros((8, size_z), F32)

    def planes(p, a):
        c, h, w = cat[p, a], high[p, a], low[p, a]
        e0 = jnp.concatenate([jnp.where(keep, c, half(h)), jnp.where(keep, zero, half(w))], 0)
        e1 = jnp.concatenate([jnp.where(keep, half(c), h), jnp.where(keep, zero, w)], 0)
        return e0, e1

    b0, b1 = planes(0, 2)
    for p in range(5):
        e0, e1 = planes(p, 0)
        co[S_R, p], co[S_B, p] = jnp.where(q0, e0, e1), jnp.where(q0, e1, e0)
        e0, e1 = planes(p, 1)
        co[I_R, p], co[I_B, p] = jnp.where(q0, e0, e1), jnp.where(q0, e1, e0)
        n0, n1 = planes(p + 1, 2) if p < 4 else (jnp.zeros_like(b0), b1)
        _, _, fyp, _ = put_faces(co, p, q0, (b0, b1, n0), planes(p, 3), planes(p, 4))
        co[YP_R, p], co[YP_B, p] = fyp
        b0, b1 = n0, n1


def mid_first_kernel(cat, low, high, red_out, co, r, b):
    q0 = even_mask(r.shape[1:])
    clear_guards(r, b, 5)
    mid_setup(co, cat, low, high, q0)
    first_red(co, r, range(5))
    relax(co, b, r, range(5), False, q0)
    relax(co, r, b, range(1, 4), True, q0)
    relax(co, b, r, range(1, 4), False, q0)
    relax(co, r, b, range(2, 3), True, q0)
    red_out[0] = r[3][:8]


def mid_second_kernel(cat, low, high, reds, reds_low, reds_high, own, level_out, low_out, co, r, b):
    size_z = r.shape[2]
    low_z = size_z // 2
    q0 = even_mask(r.shape[1:])
    keep = low_rows((8, size_z))
    clear_guards(r, b, 5)
    mid_setup(co, cat, low, high, q0)
    for p in range(5):
        tile0 = jnp.where(keep, reds[p], half(reds_high[p]))
        tile1 = jnp.where(keep, 0.0, half(reds_low[p]))
        r[p + 1] = jnp.concatenate([tile0, tile1], 0)
    d0, d1 = own[0], half(own[0])
    d0, d1 = jnp.concatenate([d0, d0], 0), jnp.concatenate([d1, d1], 0)
    co[D_R, 2], co[D_B, 2] = jnp.where(q0, d0, d1), jnp.where(q0, d1, d0)
    relax(co, b, r, range(5), False, q0)
    relax(co, r, b, range(1, 4), True, q0)
    relax(co, b, r, range(1, 4), False, q0)
    red, black = residual(co, r, b, 2, q0)
    level_out[0] = r[3][:8]
    level_out[1] = b[3][:8]
    z_sum = one_hot((size_z, low_z), lambda i, j: (i >> 1) == j)
    z_even = one_hot((size_z, low_z), lambda i, j: i == 2 * j)
    res = (red + black)[:8]
    mine = cat[2]
    alpha, bx, by, bz = own[1], mine[2], mine[3], mine[4]
    along_z = exact_dot(jnp.concatenate([res, alpha, bx, by], 0), z_sum)
    bz_z = exact_dot(bz, z_even)

    def rows(out_row, test):
        return one_hot((16, 8), lambda i, j: ((i >> 1) == out_row) & test(i & 1, j))

    total = exact_dot(rows(0, lambda i, j: (j < 4) & ((j >> 1) == i)), along_z[0:8]) * 0.125
    total += exact_dot(rows(1, lambda i, j: ((j & 3) >> 1) == i), along_z[8:16]) * 0.125
    total += exact_dot(rows(2, lambda i, j: (j < 4) & ((j >> 1) == i)), along_z[16:24]) * 0.0625
    total += exact_dot(rows(3, lambda i, j: (j & 3) == 2 * i), along_z[24:32]) * 0.0625
    total += exact_dot(rows(4, lambda i, j: ((j & 3) >> 1) == i), bz_z) * 0.0625
    for j in range(low_out.shape[0]):
        low_out[j] = total


WINDOW = 40


def window_kernel(width, index, gathered, out):
    blocks, rows, size_z = gathered.shape
    size_y = 2 * blocks
    flat = gathered[...].reshape(blocks * rows, size_z)

    def test(i, j):
        k, y = i // size_y, i % size_y
        return j == (y // 2) * rows + 2 * k + y % 2

    planes = exact_dot(one_hot((5 * size_y, blocks * rows), test), flat)
    start = index[0] * width - 16
    planes = pltpu.roll(planes, lax.rem(2 * size_z - start, size_z), 1)
    _, lane = iotas(planes.shape)
    inside = (lane < WINDOW) & (lane + start >= 0) & (lane + start < size_z)
    planes = jnp.where(inside, planes, 0.0)
    parts = [planes[k * size_y : (k + 1) * size_y] for k in range(5)]
    tile0 = parts[0] + pltpu.roll(parts[1], WINDOW, 1) + pltpu.roll(parts[2], 2 * WINDOW, 1)
    tile1 = parts[3] + pltpu.roll(parts[4], WINDOW, 1)
    for g in range(out.shape[0]):
        out[g, :size_y] = tile0
        out[g, size_y:] = tile1


def coarse_kernel(width, sweeps, index, gathered, out, co, r, b):
    size_x, size_y = gathered.shape[0], gathered.shape[1] // 2
    lanes = gathered.shape[2]
    pairs = size_x // 2
    shape = (size_y, lanes)
    q0 = even_mask(shape)
    row, lane = iotas(shape)
    r[...] = jnp.zeros_like(r)
    b[...] = jnp.zeros_like(b)

    def setup(p, carry):
        x = 2 * p
        t0, t1 = gathered[x], gathered[x + 1]
        f0, g0, f1, g1 = t0[:size_y], t0[size_y:], t1[:size_y], t1[size_y:]
        after = gathered[jnp.minimum(x + 2, size_x - 1)][:size_y]
        after = jnp.where(x + 2 < size_x, after, 0.0)

        def at(tile, k):
            return jnp.where(lane < WINDOW, pltpu.roll(tile, (lanes - k * WINDOW) % lanes, 1) if k else tile, 0.0)

        s0, s1 = at(f0, 0), at(f1, 0)
        a0, a1 = at(f0, 1), at(f1, 1)
        co[S_R, p], co[S_B, p] = jnp.where(q0, s0, s1), jnp.where(q0, s1, s0)
        a_r, a_b = jnp.where(q0, a0, a1), jnp.where(q0, a1, a0)
        fx, fy, fyp, fz = put_faces(
            co, p, q0, (at(f0, 2), at(f1, 2), at(after, 2)), (at(g0, 0), at(g1, 0)), (at(g0, 1), at(g1, 1))
        )
        yp_r = jnp.where(row == size_y - 1, 0.0, fyp[0])
        yp_b = jnp.where(row == size_y - 1, 0.0, fyp[1])
        co[YP_R, p], co[YP_B, p] = yp_r, yp_b
        co[YM_R, p], co[YM_B, p] = jnp.where(row == 0, 0.0, fy[0]), jnp.where(row == 0, 0.0, fy[1])
        d_r = a_r + ((fx[0] + fz[0]) + (fy[0] + yp_r))
        d_b = a_b + ((fx[1] + fz[1]) + (fy[1] + yp_b))
        co[I_R, p] = jnp.where(a_r > 0.0, 1.0 / jnp.where(a_r > 0.0, d_r, 1.0), 0.0)
        co[I_B, p] = jnp.where(a_b > 0.0, 1.0 / jnp.where(a_b > 0.0, d_b, 1.0), 0.0)
        return carry

    lax.fori_loop(0, pairs, setup, 0)

    def sweep(step, carry):
        relax(co, r, b, range(pairs), True, q0)
        relax(co, b, r, range(pairs), False, q0)
        return carry

    lax.fori_loop(0, sweeps, sweep, 0)
    gx, gy = index[1], index[0]
    pair = gx // 2 + 1
    pick = ((row + lane + gx) & 1) == 0
    plane = jnp.where(pick, r[pair], b[pair])
    start = gy * width - 16
    plane = pltpu.roll(plane, lax.rem(start + lanes, lanes), 1)
    plane = jnp.where((lane >= gy * width) & (lane < (gy + 1) * width), plane, 0.0)
    for j in range(out.shape[0]):
        first = 8 * (2 * j // 8)
        out[j] = plane[first : first + 8]


def finish_kernel(index, pieces, level, fine, fine_out, coarse_out):
    total = pieces[0]
    for j in range(1, pieces.shape[0]):
        total = total + pieces[j]
    start = lax.rem(2 * index[0], 8)
    coarse_out[0] = exact_dot(one_hot((8, 8), lambda i, j: j == i + start), total)[:2]
    low_z, mid_z, size_z = pieces.shape[2], level.shape[2], fine.shape[3]
    up = exact_dot(one_hot((8, 8), lambda i, j: (j == start + (i >> 1)) & (i < 4)), total)
    up = exact_dot(up, one_hot((low_z, mid_z), lambda i, j: (j >> 1) == i))
    red, black = level[0] + up, level[1] + up
    q0 = even_mask((8, mid_z))
    mid = jnp.concatenate([jnp.where(q0, red, black), jnp.where(q0, black, red)], 0)
    wide = exact_dot(mid, one_hot((mid_z, size_z), lambda i, j: (j >> 1) == i))
    spread = one_hot((16, 16), lambda i, j: j == 8 * (i >> 3) + ((i & 7) >> 1))
    wide = exact_dot(spread, wide)
    q0 = even_mask((8, size_z))
    for i in range(2):
        add = wide[8 * i : 8 * i + 8]
        red, black = fine[0, i] + add, fine[1, i] + add
        fine_out[2 * i] = jnp.where(q0, red, black)
        fine_out[2 * i + 1] = jnp.where(q0, black, red)


def on_device(rhs, alpha, beta_x, beta_y, beta_z):
    size_z = rhs.shape[2]
    mid_z, low_z = size_z // 2, size_z // 4
    count_x, count_y = lax.axis_size("gx"), lax.axis_size("gy")
    index = jnp.stack([lax.axis_index("gy"), lax.axis_index("gx")]).astype(jnp.int32)
    own = jnp.stack([rhs, alpha, beta_x, beta_y, beta_z])
    beyond = shifted(beta_x[0], 0, "gx", -2)
    left, right = shifted(own, 1, "gx", 1), shifted(own, 1, "gx", -1)
    to_low, to_high = call(
        lambda *refs: pack_rows_kernel(2, *refs), [(32, 8, size_z), (30, 8, size_z)]
    )(left, own, right)
    from_high, from_low = shifted(to_low, 2, "gy", -1), shifted(to_high, 2, "gy", 1)
    fine_args = (left, own, right, beyond, from_low, from_high)
    scratch = [(17, 6, 16, size_z), (8, 16, size_z), (8, 16, size_z)]
    (red,) = call(fine_first_kernel, [(1, 2, 8, size_z)], scratch)(*fine_args)
    red_left, red_right = shifted(red, 1, "gx", 1), shifted(red, 1, "gx", -1)
    to_low, to_high = call(
        lambda *refs: pack_rows_kernel(0, *refs), [(3, 8, size_z), (3, 8, size_z)]
    )(red_left, red, red_right)
    red_high, red_low = shifted(to_low, 2, "gy", -1), shifted(to_high, 2, "gy", 1)
    fine, mid, mid_own = call(
        fine_second_kernel, [(2, 2, 8, size_z), (5, 8, mid_z), (2, 8, mid_z)], scratch
    )(*fine_args, red_left, red, red_right, red_low, red_high)

    cat = jnp.stack([shifted(mid, 0, "gx", 2), shifted(mid, 0, "gx", 1), mid, shifted(mid, 0, "gx", -1), shifted(mid, 0, "gx", -2)])
    mid_args = (cat, shifted(cat, 0, "gy", 1), shifted(cat, 0, "gy", -1))
    scratch = [(17, 5, 16, mid_z), (7, 16, mid_z), (7, 16, mid_z)]
    (red,) = call(mid_first_kernel, [(1, 8, mid_z)], scratch)(*mid_args)
    reds = jnp.concatenate([shifted(red, 0, "gx", 2), shifted(red, 0, "gx", 1), red, shifted(red, 0, "gx", -1), shifted(red, 0, "gx", -2)])
    level, low = call(
        mid_second_kernel, [(2, 8, mid_z), (count_y, 16, low_z)], scratch
    )(*mid_args, reds, shifted(reds, 0, "gy", 1), shifted(reds, 0, "gy", -1), mid_own)

    low = lax.all_to_all(low, "gy", 0, 0, tiled=True)
    size_y = 2 * count_y
    width = low_z // count_y
    (low,) = call(
        lambda *refs: window_kernel(width, *refs), [(count_x, 2 * size_y, low_z)], smem=(0,)
    )(index, low)
    low = lax.all_to_all(low, "gx", 0, 0, tiled=True)
    pairs = count_x // 2
    (pieces,) = call(
        lambda *refs: coarse_kernel(width, 8, *refs),
        [(count_y, 8, low_z)],
        [(17, pairs, size_y, low_z), (pairs + 2, size_y, low_z), (pairs + 2, size_y, low_z)],
        smem=(0,),
    )(index, low)
    pieces = lax.all_to_all(pieces, "gy", 0, 0, tiled=True)
    fine_solution, coarse = call(
        finish_kernel, [rhs.shape, (1, 2, low_z)], smem=(0,)
    )(index, pieces, level, fine)
    return fine_solution, coarse


def solution(mesh):
    placed = P("gx", "gy", None)
    return jax.shard_map(
        on_device,
        mesh=mesh,
        in_specs=(placed,) * 5,
        out_specs=(placed, placed),
        check_vma=False,
    )
```

```python
import jax
import jax.numpy as jnp
from jax import lax
from jax.experimental import pallas as pl
from jax.experimental.pallas import tpu as pltpu
from jax.sharding import PartitionSpec as P

F32 = jnp.float32
RHS, ALPHA, BX, BY, BZ = range(5)
VMEM_BYTES = 20 * 2**20
RING = 8


def shifted(values, axis, name, steps):
    count = lax.axis_size(name)
    lead, last = max(0, -steps), min(count, count - steps)
    return lax.ppermute(values, name, [(i, i + steps) for i in range(lead, last)])


def call(kernel, outs, scratch=(), smem=()):
    def run(*args):
        specs = [
            pl.BlockSpec(memory_space=pltpu.SMEM if i in smem else pltpu.VMEM)
            for i in range(len(args))
        ]
        shapes = [jax.ShapeDtypeStruct(s, F32) for s in outs]
        return pl.pallas_call(
            kernel,
            out_shape=shapes,
            in_specs=specs,
            out_specs=[pl.BlockSpec(memory_space=pltpu.VMEM)] * len(outs),
            scratch_shapes=[pltpu.VMEM(s, F32) for s in scratch],
            compiler_params=pltpu.CompilerParams(vmem_limit_bytes=VMEM_BYTES),
        )(*args)

    return run


def iotas(shape):
    return lax.broadcasted_iota(jnp.int32, shape, 0), lax.broadcasted_iota(jnp.int32, shape, 1)


def even_mask(shape):
    row, lane = iotas(shape)
    return ((row + lane) & 1) == 0


def half(x):
    return pltpu.roll(x, 4, 0)


def prev_row(x):
    return pltpu.roll(x, 1, 0)


def next_row(x):
    return pltpu.roll(x, x.shape[0] - 1, 0)


def prev_lane(x):
    return pltpu.roll(x, 1, 1)


def next_lane(x):
    return pltpu.roll(x, x.shape[1] - 1, 1)


def exact_dot(a, b):
    return jnp.dot(a, b, precision=lax.Precision.HIGHEST, preferred_element_type=F32)


def one_hot(shape, test):
    row, col = iotas(shape)
    return jnp.where(test(row, col), 1.0, 0.0).astype(F32)


def low_rows(shape):
    row, _ = iotas(shape)
    return (row & 7) < 4


S_R, S_B, WP, WO_R, WO_B, YM_R, YM_B, YP_R, YP_B, ZM_R, ZM_B, ZP_R, ZP_B, I_R, I_B, D_R, D_B = range(17)


def beside(co, src, p, red, q0):
    v = src[p + 1]
    before, after = src[p], src[p + 2]
    other = jnp.where(q0, before, after) if red else jnp.where(q0, after, before)
    wo, ym, yp, zm, zp = (
        (WO_R, YM_R, YP_R, ZM_R, ZP_R) if red else (WO_B, YM_B, YP_B, ZM_B, ZP_B)
    )
    total = co[WP, p] * v + co[wo, p] * other
    total = total + (co[ym, p] * prev_row(v) + co[yp, p] * next_row(v))
    return total + (co[zm, p] * prev_lane(v) + co[zp, p] * next_lane(v))


def relax(co, dst, src, pairs, red, q0):
    s, inv = (S_R, I_R) if red else (S_B, I_B)
    for p in pairs:
        dst[p + 1] = (co[s, p] + beside(co, src, p, red, q0)) * co[inv, p]


def first_red(co, dst, pairs):
    for p in pairs:
        dst[p + 1] = co[S_R, p] * co[I_R, p]


def residual(co, r, b, p, q0):
    red = co[S_R, p] - (co[D_R, p] * r[p + 1] - beside(co, b, p, True, q0))
    black = co[S_B, p] - (co[D_B, p] * b[p + 1] - beside(co, r, p, False, q0))
    return red, black


def put_faces(co, p, q0, bx, by, bz):
    b0, b1, b2 = bx
    wo_r, wo_b = jnp.where(q0, b0, b2), jnp.where(q0, b2, b0)
    y_r, y_b = jnp.where(q0, by[0], by[1]), jnp.where(q0, by[1], by[0])
    z_r, z_b = jnp.where(q0, bz[0], bz[1]), jnp.where(q0, bz[1], bz[0])
    yp_r, yp_b = next_row(y_b), next_row(y_r)
    row, lane = iotas(q0.shape)
    first, last = lane == 0, lane == q0.shape[1] - 1
    zp_r, zp_b = jnp.where(last, 0.0, next_lane(z_b)), jnp.where(last, 0.0, next_lane(z_r))
    co[WP, p], co[WO_R, p], co[WO_B, p] = b1, wo_r, wo_b
    co[YM_R, p], co[YM_B, p] = y_r, y_b
    co[ZM_R, p], co[ZM_B, p] = jnp.where(first, 0.0, z_r), jnp.where(first, 0.0, z_b)
    co[ZP_R, p], co[ZP_B, p] = zp_r, zp_b
    return (b1 + wo_r, b1 + wo_b), (y_r, y_b), (yp_r, yp_b), (z_r + zp_r, z_b + zp_b)


def pack_rows_kernel(n_extra, left, own, right, to_low, to_high):
    arrays, planes = own.shape[0], own.shape[1]
    keep = low_rows((8, own.shape[3]))
    for a in range(arrays):
        for k, block in enumerate((left, own, right)):
            for x in range(0, planes, 2):
                t = a * (3 * planes // 2) + (k * planes + x) // 2
                e0, e1 = block[a, x], block[a, x + 1]
                to_low[t] = jnp.where(keep, e0, half(e1))
                to_high[t] = jnp.where(keep, half(e1), e0)
    if n_extra:
        base = arrays * 3 * planes // 2
        for x in range(0, planes, 2):
            e0, e1 = next_row(own[BY, x]), next_row(own[BY, x + 1])
            to_low[base + x // 2] = jnp.where(keep, e0, half(e1))


def halo_tile(from_low, from_high, t, odd, keep):
    high, low = from_high[t], from_low[t]
    if odd:
        high, low = half(high), half(low)
    return jnp.where(keep, high, low)


def fine_setup(co, left, own, right, beyond, from_low, from_high, q0):
    keep = low_rows((8, own.shape[3]))
    q0t = q0[:8]
    blocks = (left, own, right)

    def plane(a, x):
        return jnp.concatenate(
            [blocks[x // 4][a, x % 4], halo_tile(from_low, from_high, a * 6 + x // 2, x % 2, keep)], 0
        )

    bx0 = plane(BX, 0)
    for p in range(6):
        e0, e1 = plane(RHS, 2 * p), plane(RHS, 2 * p + 1)
        co[S_R, p], co[S_B, p] = jnp.where(q0, e0, e1), jnp.where(q0, e1, e0)
        b1 = plane(BX, 2 * p + 1)
        if p < 5:
            b2 = plane(BX, 2 * p + 2)
        else:
            b2 = jnp.concatenate([beyond[...], jnp.zeros_like(beyond[...])], 0)
        by = plane(BY, 2 * p), plane(BY, 2 * p + 1)
        bz = plane(BZ, 2 * p), plane(BZ, 2 * p + 1)
        fx, fy, fyp, fz = put_faces(co, p, q0, (bx0, b1, b2), by, bz)
        bx0 = b2
        yp_r, yp_b = fyp
        if p in (2, 3):
            up = from_high[30 + p - 2]
            u0, u1 = up, half(up)
            up_r, up_b = jnp.where(q0t, u0, u1), jnp.where(q0t, u1, u0)
            yp_r = jnp.concatenate([yp_r[:8], jnp.where(keep, up_r, yp_r[8:])], 0)
            yp_b = jnp.concatenate([yp_b[:8], jnp.where(keep, up_b, yp_b[8:])], 0)
        co[YP_R, p], co[YP_B, p] = yp_r, yp_b
        e0, e1 = plane(ALPHA, 2 * p), plane(ALPHA, 2 * p + 1)
        a_r, a_b = jnp.where(q0, e0, e1), jnp.where(q0, e1, e0)
        d_r = a_r + ((fx[0] + fz[0]) + (fy[0] + yp_r))
        d_b = a_b + ((fx[1] + fz[1]) + (fy[1] + yp_b))
        co[D_R, p], co[D_B, p] = d_r, d_b
        co[I_R, p] = jnp.where(a_r > 0.0, 1.0 / jnp.where(a_r > 0.0, d_r, 1.0), 0.0)
        co[I_B, p] = jnp.where(a_b > 0.0, 1.0 / jnp.where(a_b > 0.0, d_b, 1.0), 0.0)


def clear_guards(r, b, n):
    for ref in (r, b):
        ref[0] = jnp.zeros_like(ref[0])
        ref[n + 1] = jnp.zeros_like(ref[n + 1])


def fine_first_kernel(left, own, right, beyond, from_low, from_high, red_out, co, r, b):
    q0 = even_mask(r.shape[1:])
    clear_guards(r, b, 6)
    fine_setup(co, left, own, right, beyond, from_low, from_high, q0)
    first_red(co, r, range(6))
    relax(co, b, r, range(6), False, q0)
    relax(co, r, b, range(1, 5), True, q0)
    relax(co, b, r, range(1, 5), False, q0)
    relax(co, r, b, range(2, 4), True, q0)
    red_out[0, 0] = r[3][:8]
    red_out[0, 1] = r[4][:8]


def fine_second_kernel(
    left, own, right, beyond, from_low, from_high,
    red_left, red_own, red_right, red_low, red_high,
    fine_out, mid_out, own_out, co, r, b,
):
    size_z = own.shape[3]
    mid_z = size_z // 2
    q0 = even_mask(r.shape[1:])
    keep = low_rows((8, size_z))
    clear_guards(r, b, 6)
    fine_setup(co, left, own, right, beyond, from_low, from_high, q0)
    reds = (red_left, red_own, red_right)
    for p in range(6):
        tile = halo_tile(red_low, red_high, p // 2, p % 2, keep)
        r[p + 1] = jnp.concatenate([reds[p // 2][0, p % 2], tile], 0)
    relax(co, b, r, range(6), False, q0)
    relax(co, r, b, range(1, 5), True, q0)
    relax(co, b, r, range(1, 5), False, q0)
    sums = []
    for p in (2, 3):
        red, black = residual(co, r, b, p, q0)
        sums.append((red + black)[:8])
        fine_out[0, p - 2] = r[p + 1][:8]
        fine_out[1, p - 2] = b[p + 1][:8]
    z_sum = one_hot((size_z, mid_z), lambda i, j: (i >> 1) == j)
    z_even = one_hot((size_z, mid_z), lambda i, j: i == 2 * j)
    y_sum = one_hot((8, 16), lambda i, j: (j >> 1) == i)
    y_even = one_hot((8, 16), lambda i, j: j == 2 * i)
    zeros8 = jnp.zeros((8, size_z), F32)
    alphas = [own[ALPHA, 2 * i] + own[ALPHA, 2 * i + 1] for i in range(2)]
    bys = [own[BY, 2 * i] + own[BY, 2 * i + 1] for i in range(2)]
    by_next = []
    for i in range(2):
        t = BY * 6 + 2 + i
        h = from_high[t]
        by_next.append(h + half(h))
    bzs = [own[BZ, 2 * i] + own[BZ, 2 * i + 1] for i in range(2)]
    bxs = [own[BX, 0], own[BX, 2], right[BX, 0]]
    stacked = jnp.concatenate([*sums, *alphas, *bys, *by_next, *bxs, zeros8], 0)
    along_z = exact_dot(stacked, z_sum)
    bz_z = exact_dot(jnp.concatenate(bzs, 0), z_even)
    source = exact_dot(y_sum, along_z[0:16]) * 0.125
    alpha = exact_dot(y_sum, along_z[16:32]) * 0.125
    y_lower = exact_dot(y_even, along_z[32:48]) * 0.0625
    y_next = one_hot((8, 16), lambda i, j: ((i & 3) < 3) & (j == 2 * i + 2))
    y_last = one_hot((8, 16), lambda i, j: ((i & 3) == 3) & (j == 8 * (i >> 2)))
    y_upper = (exact_dot(y_next, along_z[32:48]) + exact_dot(y_last, along_z[48:64])) * 0.0625
    x_lower = exact_dot(y_sum, along_z[64:80]) * 0.0625
    x_upper = exact_dot(y_sum, along_z[72:88]) * 0.0625
    z_lower = exact_dot(y_sum, bz_z) * 0.0625
    _, lane = iotas(z_lower.shape)
    z_upper = jnp.where(lane == mid_z - 1, 0.0, next_lane(z_lower))
    diagonal = alpha + ((x_lower + x_upper) + (y_lower + y_upper) + (z_lower + z_upper))
    mid_out[0] = source
    mid_out[1] = 1.0 / diagonal
    mid_out[2] = x_lower
    mid_out[3] = y_lower
    mid_out[4] = z_lower
    own_out[0] = diagonal
    own_out[1] = alpha


def mid_setup(co, cat, low, high, q0):
    size_z = q0.shape[1]
    keep = low_rows((8, size_z))
    zero = jnp.zeros((8, size_z), F32)

    def planes(p, a):
        c, h, w = cat[p, a], high[p, a], low[p, a]
        e0 = jnp.concatenate([jnp.where(keep, c, half(h)), jnp.where(keep, zero, half(w))], 0)
        e1 = jnp.concatenate([jnp.where(keep, half(c), h), jnp.where(keep, zero, w)], 0)
        return e0, e1

    b0, b1 = planes(0, 2)
    for p in range(5):
        e0, e1 = planes(p, 0)
        co[S_R, p], co[S_B, p] = jnp.where(q0, e0, e1), jnp.where(q0, e1, e0)
        e0, e1 = planes(p, 1)
        co[I_R, p], co[I_B, p] = jnp.where(q0, e0, e1), jnp.where(q0, e1, e0)
        n0, n1 = planes(p + 1, 2) if p < 4 else (jnp.zeros_like(b0), b1)
        _, _, fyp, _ = put_faces(co, p, q0, (b0, b1, n0), planes(p, 3), planes(p, 4))
        co[YP_R, p], co[YP_B, p] = fyp
        b0, b1 = n0, n1


def mid_first_kernel(cat, low, high, red_out, co, r, b):
    q0 = even_mask(r.shape[1:])
    clear_guards(r, b, 5)
    mid_setup(co, cat, low, high, q0)
    first_red(co, r, range(5))
    relax(co, b, r, range(5), False, q0)
    relax(co, r, b, range(1, 4), True, q0)
    relax(co, b, r, range(1, 4), False, q0)
    relax(co, r, b, range(2, 3), True, q0)
    red_out[0] = r[3][:8]


def mid_second_kernel(cat, low, high, reds, reds_low, reds_high, own, level_out, low_out, co, r, b):
    size_z = r.shape[2]
    low_z = size_z // 2
    q0 = even_mask(r.shape[1:])
    keep = low_rows((8, size_z))
    clear_guards(r, b, 5)
    mid_setup(co, cat, low, high, q0)
    for p in range(5):
        tile0 = jnp.where(keep, reds[p], half(reds_high[p]))
        tile1 = jnp.where(keep, 0.0, half(reds_low[p]))
        r[p + 1] = jnp.concatenate([tile0, tile1], 0)
    d0, d1 = own[0], half(own[0])
    d0, d1 = jnp.concatenate([d0, d0], 0), jnp.concatenate([d1, d1], 0)
    co[D_R, 2], co[D_B, 2] = jnp.where(q0, d0, d1), jnp.where(q0, d1, d0)
    relax(co, b, r, range(5), False, q0)
    relax(co, r, b, range(1, 4), True, q0)
    relax(co, b, r, range(1, 4), False, q0)
    red, black = residual(co, r, b, 2, q0)
    level_out[0] = r[3][:8]
    level_out[1] = b[3][:8]
    z_sum = one_hot((size_z, low_z), lambda i, j: (i >> 1) == j)
    z_even = one_hot((size_z, low_z), lambda i, j: i == 2 * j)
    res = (red + black)[:8]
    mine = cat[2]
    alpha, bx, by, bz = own[1], mine[2], mine[3], mine[4]
    along_z = exact_dot(jnp.concatenate([res, alpha, bx, by], 0), z_sum)
    bz_z = exact_dot(bz, z_even)

    def rows(out_row, test):
        return one_hot((16, 8), lambda i, j: ((i >> 1) == out_row) & test(i & 1, j))

    total = exact_dot(rows(0, lambda i, j: (j < 4) & ((j >> 1) == i)), along_z[0:8]) * 0.125
    total += exact_dot(rows(1, lambda i, j: ((j & 3) >> 1) == i), along_z[8:16]) * 0.125
    total += exact_dot(rows(2, lambda i, j: (j < 4) & ((j >> 1) == i)), along_z[16:24]) * 0.0625
    total += exact_dot(rows(3, lambda i, j: (j & 3) == 2 * i), along_z[24:32]) * 0.0625
    total += exact_dot(rows(4, lambda i, j: ((j & 3) >> 1) == i), bz_z) * 0.0625
    for j in range(low_out.shape[0]):
        low_out[j] = total


WINDOW = 40


def window_kernel(width, index, gathered, out):
    blocks, rows, size_z = gathered.shape
    size_y = 2 * blocks
    flat = gathered[...].reshape(blocks * rows, size_z)

    def test(i, j):
        k, y = i // size_y, i % size_y
        return j == (y // 2) * rows + 2 * k + y % 2

    planes = exact_dot(one_hot((5 * size_y, blocks * rows), test), flat)
    start = index[0] * width - 16
    planes = pltpu.roll(planes, lax.rem(2 * size_z - start, size_z), 1)
    _, lane = iotas(planes.shape)
    inside = (lane < WINDOW) & (lane + start >= 0) & (lane + start < size_z)
    planes = jnp.where(inside, planes, 0.0)
    parts = [planes[k * size_y : (k + 1) * size_y] for k in range(5)]
    tile0 = parts[0] + pltpu.roll(parts[1], WINDOW, 1) + pltpu.roll(parts[2], 2 * WINDOW, 1)
    tile1 = parts[3] + pltpu.roll(parts[4], WINDOW, 1)
    for g in range(out.shape[0]):
        out[g, :size_y] = tile0
        out[g, size_y:] = tile1


def coarse_kernel(width, sweeps, index, gathered, out, co, r, b):
    size_x, size_y = gathered.shape[0], gathered.shape[1] // 2
    lanes = gathered.shape[2]
    pairs = size_x // 2
    shape = (size_y, lanes)
    q0 = even_mask(shape)
    row, lane = iotas(shape)
    r[...] = jnp.zeros_like(r)
    b[...] = jnp.zeros_like(b)

    def setup(p, carry):
        x = 2 * p
        t0, t1 = gathered[x], gathered[x + 1]
        f0, g0, f1, g1 = t0[:size_y], t0[size_y:], t1[:size_y], t1[size_y:]
        after = gathered[jnp.minimum(x + 2, size_x - 1)][:size_y]
        after = jnp.where(x + 2 < size_x, after, 0.0)

        def at(tile, k):
            return jnp.where(lane < WINDOW, pltpu.roll(tile, (lanes - k * WINDOW) % lanes, 1) if k else tile, 0.0)

        s0, s1 = at(f0, 0), at(f1, 0)
        a0, a1 = at(f0, 1), at(f1, 1)
        co[S_R, p], co[S_B, p] = jnp.where(q0, s0, s1), jnp.where(q0, s1, s0)
        a_r, a_b = jnp.where(q0, a0, a1), jnp.where(q0, a1, a0)
        fx, fy, fyp, fz = put_faces(
            co, p, q0, (at(f0, 2), at(f1, 2), at(after, 2)), (at(g0, 0), at(g1, 0)), (at(g0, 1), at(g1, 1))
        )
        yp_r = jnp.where(row == size_y - 1, 0.0, fyp[0])
        yp_b = jnp.where(row == size_y - 1, 0.0, fyp[1])
        co[YP_R, p], co[YP_B, p] = yp_r, yp_b
        co[YM_R, p], co[YM_B, p] = jnp.where(row == 0, 0.0, fy[0]), jnp.where(row == 0, 0.0, fy[1])
        d_r = a_r + ((fx[0] + fz[0]) + (fy[0] + yp_r))
        d_b = a_b + ((fx[1] + fz[1]) + (fy[1] + yp_b))
        co[I_R, p] = jnp.where(a_r > 0.0, 1.0 / jnp.where(a_r > 0.0, d_r, 1.0), 0.0)
        co[I_B, p] = jnp.where(a_b > 0.0, 1.0 / jnp.where(a_b > 0.0, d_b, 1.0), 0.0)
        return carry

    lax.fori_loop(0, pairs, setup, 0)

    def sweep(step, carry):
        relax(co, r, b, range(pairs), True, q0)
        relax(co, b, r, range(pairs), False, q0)
        return carry

    lax.fori_loop(0, sweeps, sweep, 0)
    gx, gy = index[1], index[0]
    pair = gx // 2 + 1
    pick = ((row + lane + gx) & 1) == 0
    plane = jnp.where(pick, r[pair], b[pair])
    start = gy * width - 16
    plane = pltpu.roll(plane, lax.rem(start + lanes, lanes), 1)
    plane = jnp.where((lane >= gy * width) & (lane < (gy + 1) * width), plane, 0.0)
    for j in range(out.shape[0]):
        first = 8 * (2 * j // 8)
        out[j] = plane[first : first + 8]


def finish_kernel(index, pieces, level, fine, fine_out, coarse_out):
    total = pieces[0]
    for j in range(1, pieces.shape[0]):
        total = total + pieces[j]
    start = lax.rem(2 * index[0], 8)
    coarse_out[0] = exact_dot(one_hot((8, 8), lambda i, j: j == i + start), total)[:2]
    low_z, mid_z, size_z = pieces.shape[2], level.shape[2], fine.shape[3]
    up = exact_dot(one_hot((8, 8), lambda i, j: (j == start + (i >> 1)) & (i < 4)), total)
    up = exact_dot(up, one_hot((low_z, mid_z), lambda i, j: (j >> 1) == i))
    red, black = level[0] + up, level[1] + up
    q0 = even_mask((8, mid_z))
    mid = jnp.concatenate([jnp.where(q0, red, black), jnp.where(q0, black, red)], 0)
    wide = exact_dot(mid, one_hot((mid_z, size_z), lambda i, j: (j >> 1) == i))
    spread = one_hot((16, 16), lambda i, j: j == 8 * (i >> 3) + ((i & 7) >> 1))
    wide = exact_dot(spread, wide)
    q0 = even_mask((8, size_z))
    for i in range(2):
        add = wide[8 * i : 8 * i + 8]
        red, black = fine[0, i] + add, fine[1, i] + add
        fine_out[2 * i] = jnp.where(q0, red, black)
        fine_out[2 * i + 1] = jnp.where(q0, black, red)


def on_device(rhs, alpha, beta_x, beta_y, beta_z):
    size_z = rhs.shape[2]
    mid_z, low_z = size_z // 2, size_z // 4
    count_x, count_y = lax.axis_size("gx"), lax.axis_size("gy")
    index = jnp.stack([lax.axis_index("gy"), lax.axis_index("gx")]).astype(jnp.int32)
    own = jnp.stack([rhs, alpha, beta_x, beta_y, beta_z])
    beyond = shifted(beta_x[0], 0, "gx", -2)
    left, right = shifted(own, 1, "gx", 1), shifted(own, 1, "gx", -1)
    to_low, to_high = call(
        lambda *refs: pack_rows_kernel(2, *refs), [(32, 8, size_z), (30, 8, size_z)]
    )(left, own, right)
    from_high, from_low = shifted(to_low, 2, "gy", -1), shifted(to_high, 2, "gy", 1)
    fine_args = (left, own, right, beyond, from_low, from_high)
    scratch = [(17, 6, 16, size_z), (8, 16, size_z), (8, 16, size_z)]
    (red,) = call(fine_first_kernel, [(1, 2, 8, size_z)], scratch)(*fine_args)
    red_left, red_right = shifted(red, 1, "gx", 1), shifted(red, 1, "gx", -1)
    to_low, to_high = call(
        lambda *refs: pack_rows_kernel(0, *refs), [(3, 8, size_z), (3, 8, size_z)]
    )(red_left, red, red_right)
    red_high, red_low = shifted(to_low, 2, "gy", -1), shifted(to_high, 2, "gy", 1)
    fine, mid, mid_own = call(
        fine_second_kernel, [(2, 2, 8, size_z), (5, 8, mid_z), (2, 8, mid_z)], scratch
    )(*fine_args, red_left, red, red_right, red_low, red_high)

    cat = jnp.stack([shifted(mid, 0, "gx", 2), shifted(mid, 0, "gx", 1), mid, shifted(mid, 0, "gx", -1), shifted(mid, 0, "gx", -2)])
    mid_args = (cat, shifted(cat, 0, "gy", 1), shifted(cat, 0, "gy", -1))
    scratch = [(17, 5, 16, mid_z), (7, 16, mid_z), (7, 16, mid_z)]
    (red,) = call(mid_first_kernel, [(1, 8, mid_z)], scratch)(*mid_args)
    reds = jnp.concatenate([shifted(red, 0, "gx", 2), shifted(red, 0, "gx", 1), red, shifted(red, 0, "gx", -1), shifted(red, 0, "gx", -2)])
    level, low = call(
        mid_second_kernel, [(2, 8, mid_z), (count_y, 16, low_z)], scratch
    )(*mid_args, reds, shifted(reds, 0, "gy", 1), shifted(reds, 0, "gy", -1), mid_own)

    low = lax.all_to_all(low, "gy", 0, 0, tiled=True)
    size_y = 2 * count_y
    width = low_z // count_y
    (low,) = call(
        lambda *refs: window_kernel(width, *refs), [(RING, 2 * size_y, low_z)], smem=(0,)
    )(index, low)
    groups = count_x // RING
    rings = [[RING * i + j for j in range(RING)] for i in range(groups)]
    low = lax.all_to_all(low, "gx", 0, 0, tiled=True, axis_index_groups=rings)
    low = jnp.broadcast_to(low[None], (groups, *low.shape)).reshape(-1, *low.shape[1:])
    low = lax.all_to_all(low, "gx", 0, 0, tiled=True, axis_index_groups=[list(c) for c in zip(*rings)])
    pairs = count_x // 2
    (pieces,) = call(
        lambda *refs: coarse_kernel(width, 8, *refs),
        [(count_y, 8, low_z)],
        [(17, pairs, size_y, low_z), (pairs + 2, size_y, low_z), (pairs + 2, size_y, low_z)],
        smem=(0,),
    )(index, low)
    pieces = lax.all_to_all(pieces, "gy", 0, 0, tiled=True)
    fine_solution, coarse = call(
        finish_kernel, [rhs.shape, (1, 2, low_z)], smem=(0,)
    )(index, pieces, level, fine)
    return fine_solution, coarse


def solution(mesh):
    placed = P("gx", "gy", None)
    return jax.shard_map(
        on_device,
        mesh=mesh,
        in_specs=(placed,) * 5,
        out_specs=(placed, placed),
        check_vma=False,
    )
```

```python
import jax
import jax.numpy as jnp
from jax import lax
from jax.experimental import pallas as pl
from jax.experimental.pallas import tpu as pltpu
from jax.sharding import PartitionSpec as P

F32 = jnp.float32
RHS, ALPHA, BX, BY, BZ = range(5)
VMEM_BYTES = 20 * 2**20
RING = 8


def shifted(values, axis, name, steps):
    count = lax.axis_size(name)
    lead, last = max(0, -steps), min(count, count - steps)
    return lax.ppermute(values, name, [(i, i + steps) for i in range(lead, last)])


def call(kernel, outs, scratch=(), smem=()):
    def run(*args):
        specs = [
            pl.BlockSpec(memory_space=pltpu.SMEM if i in smem else pltpu.VMEM)
            for i in range(len(args))
        ]
        shapes = [jax.ShapeDtypeStruct(s, F32) for s in outs]
        return pl.pallas_call(
            kernel,
            out_shape=shapes,
            in_specs=specs,
            out_specs=[pl.BlockSpec(memory_space=pltpu.VMEM)] * len(outs),
            scratch_shapes=[pltpu.VMEM(s, F32) for s in scratch],
            compiler_params=pltpu.CompilerParams(vmem_limit_bytes=VMEM_BYTES),
        )(*args)

    return run


def iotas(shape):
    return lax.broadcasted_iota(jnp.int32, shape, 0), lax.broadcasted_iota(jnp.int32, shape, 1)


def even_mask(shape):
    row, lane = iotas(shape)
    return ((row + lane) & 1) == 0


def half(x):
    return pltpu.roll(x, 4, 0)


def prev_row(x):
    return pltpu.roll(x, 1, 0)


def next_row(x):
    return pltpu.roll(x, x.shape[0] - 1, 0)


def prev_lane(x):
    return pltpu.roll(x, 1, 1)


def next_lane(x):
    return pltpu.roll(x, x.shape[1] - 1, 1)


def exact_dot(a, b):
    return jnp.dot(a, b, precision=lax.Precision.HIGHEST, preferred_element_type=F32)


def one_hot(shape, test):
    row, col = iotas(shape)
    return jnp.where(test(row, col), 1.0, 0.0).astype(F32)


def low_rows(shape):
    row, _ = iotas(shape)
    return (row & 7) < 4


def inverse_of(diagonal, cell):
    inside = cell > 0.0
    return jnp.where(inside, 1.0 / jnp.where(inside, diagonal, 1.0), 0.0)


def halves(q0, e0, e1):
    return jnp.where(q0, e0, e1), jnp.where(q0, e1, e0)


def clear_guards(r, b, n):
    for ref in (r, b):
        ref[0] = jnp.zeros_like(ref[0])
        ref[n + 1] = jnp.zeros_like(ref[n + 1])


S_R, S_B, WP, WO_R, WO_B, YM_R, YM_B, YP_R, YP_B, ZM_R, ZM_B, ZP_R, ZP_B, I_R, I_B, D_R, D_B = range(17)


def beside(co, src, p, red, q0):
    v = src[p + 1]
    before, after = src[p], src[p + 2]
    other = jnp.where(q0, before, after) if red else jnp.where(q0, after, before)
    wo, ym, yp, zm, zp = (
        (WO_R, YM_R, YP_R, ZM_R, ZP_R) if red else (WO_B, YM_B, YP_B, ZM_B, ZP_B)
    )
    total = co[WP, p] * v + co[wo, p] * other
    total = total + (co[ym, p] * prev_row(v) + co[yp, p] * next_row(v))
    return total + (co[zm, p] * prev_lane(v) + co[zp, p] * next_lane(v))


def relax(co, dst, src, pairs, red, q0):
    s, inv = (S_R, I_R) if red else (S_B, I_B)
    for p in pairs:
        dst[p + 1] = (co[s, p] + beside(co, src, p, red, q0)) * co[inv, p]


def first_red(co, dst, pairs):
    for p in pairs:
        dst[p + 1] = co[S_R, p] * co[I_R, p]


def residual(co, r, b, p, q0):
    red = co[S_R, p] - (co[D_R, p] * r[p + 1] - beside(co, b, p, True, q0))
    black = co[S_B, p] - (co[D_B, p] * b[p + 1] - beside(co, r, p, False, q0))
    return red, black


def put_faces(co, p, q0, bx, by, bz):
    b0, b1, b2 = bx
    wo_r, wo_b = halves(q0, b0, b2)
    y_r, y_b = halves(q0, *by)
    z_r, z_b = halves(q0, *bz)
    yp_r, yp_b = next_row(y_b), next_row(y_r)
    zp_r, zp_b = next_lane(z_b), next_lane(z_r)
    co[WP, p], co[WO_R, p], co[WO_B, p] = b1, wo_r, wo_b
    co[YM_R, p], co[YM_B, p], co[YP_R, p], co[YP_B, p] = y_r, y_b, yp_r, yp_b
    co[ZM_R, p], co[ZM_B, p], co[ZP_R, p], co[ZP_B, p] = z_r, z_b, zp_r, zp_b
    return (b1 + wo_r, b1 + wo_b), (y_r, y_b), (yp_r, yp_b), (z_r + zp_r, z_b + zp_b)


def smooth_cone(co, r, b, own, halo, q0):
    def pairs(reach):
        extra = min(halo, (reach + 1) // 2)
        return range(halo - extra, halo + own + extra)

    first_red(co, r, pairs(8))
    for step in range(2, 9):
        red = step % 2 == 1
        relax(co, r if red else b, b if red else r, pairs(9 - step), red, q0)


def to_windows_kernel(rhs, alpha, beta_x, beta_y, beta_z, out):
    _, lane = iotas((8, 128))
    zero = jnp.zeros((8, 128), F32)
    for a, ref in enumerate((rhs, alpha, beta_x, beta_y, beta_z)):
        for x in range(4):
            tiles = [ref[x, :, 128 * c : 128 * c + 128] for c in range(4)]
            up = [pltpu.roll(t, 32, 1) for t in tiles]
            down = [pltpu.roll(t, 96, 1) for t in tiles]
            for c in range(4):
                out[2 * c, a, x] = jnp.where(lane < 32, up[c - 1] if c else zero, up[c])
                out[2 * c + 1, a, x] = jnp.where(lane < 96, down[c], down[c + 1] if c < 3 else zero)


def x_messages_kernel(own, to_low, to_high, first_by):
    for s in range(2):
        for a in range(5):
            for x in range(4):
                t = (s * 5 + a) * 4 + x
                to_low[t] = own[s, a, x]
                to_high[t] = own[6 + s, a, x]
    to_low[40] = own[2, BX, 0]
    for x in range(32):
        first_by[x : x + 1] = own[x // 4, BY, x % 4][:1]


def y_message_kernel(low, own, high, out, beyond):
    for a in range(5):
        for x in range(4):
            for s in range(2):
                t = (s * 5 + a) * 4 + x
                out[s, a, x] = low[t]
                out[10 + s, a, x] = high[t]
            for s in range(8):
                out[2 + s, a, x] = own[s, a, x]
    beyond[...] = high[40]


def fine_kernel(mine, low, high, beyond_x, beyond_y, fine_out, mid_first, mid_last, own_out, co, r, b):
    q0 = even_mask((24, 128))
    row, lane = iotas((24, 128))
    clear_guards(r, b, 24)
    zero = jnp.zeros((8, 128), F32)

    def plane(a, x):
        return jnp.concatenate([ref[x // 4, a, x % 4] for ref in (mine, high, low)], 0)

    bx0 = plane(BX, 0)
    for p in range(24):
        x = 2 * p
        co[S_R, p], co[S_B, p] = halves(q0, plane(RHS, x), plane(RHS, x + 1))
        bx1 = plane(BX, x + 1)
        bx2 = plane(BX, x + 2) if p < 23 else jnp.concatenate([beyond_x[...], zero, zero], 0)
        by = plane(BY, x), plane(BY, x + 1)
        bz = plane(BZ, x), plane(BZ, x + 1)
        fx, fy, fyp, fz = put_faces(co, p, q0, (bx0, bx1, bx2), by, bz)
        bx0 = bx2
        yp_r, yp_b = fyp
        if 4 <= p < 20:
            e0, e1 = beyond_y[x - 8 : x - 7], beyond_y[x - 7 : x - 6]
            up_r, up_b = halves(q0[15:16], e0, e1)
            yp_r = jnp.where(row == 15, up_r, yp_r)
            yp_b = jnp.where(row == 15, up_b, yp_b)
            co[YP_R, p], co[YP_B, p] = yp_r, yp_b
        a_r, a_b = halves(q0, plane(ALPHA, x), plane(ALPHA, x + 1))
        d_r = a_r + ((fx[0] + fz[0]) + (fy[0] + yp_r))
        d_b = a_b + ((fx[1] + fz[1]) + (fy[1] + yp_b))
        co[D_R, p], co[D_B, p] = d_r, d_b
        co[I_R, p], co[I_B, p] = inverse_of(d_r, a_r), inverse_of(d_b, a_b)
    smooth_cone(co, r, b, 16, 4, q0)
    sums, alphas, bys, nexts, bxs, bzs = [], [], [], [], [], []
    for j in range(16):
        p = j + 4
        red, black = residual(co, r, b, p, q0)
        sums.append((red + black)[:8])
        fine_out[0, j] = r[p + 1][:8]
        fine_out[1, j] = b[p + 1][:8]
        s, x = (2 * p) // 4, (2 * p) % 4
        alphas.append(mine[s, ALPHA, x] + mine[s, ALPHA, x + 1])
        bys.append(mine[s, BY, x] + mine[s, BY, x + 1])
        nexts.append(high[s, BY, x] + high[s, BY, x + 1])
        bzs.append(mine[s, BZ, x] + mine[s, BZ, x + 1])
        bxs.append(mine[s, BX, x])
    bxs.append(mine[10, BX, 0])
    z_sum = one_hot((128, 128), lambda i, j: (i >> 1) == j)
    z_even = one_hot((128, 128), lambda i, j: i == 2 * j)
    y_sum = one_hot((64, 128), lambda i, j: (j >> 1) == i)
    y_even = one_hot((64, 128), lambda i, j: j == 2 * i)
    y_next = one_hot((64, 128), lambda i, j: ((i & 3) < 3) & (j == 2 * i + 2))
    y_last = one_hot((64, 128), lambda i, j: ((i & 3) == 3) & (j == 8 * (i >> 2)))
    along = exact_dot(jnp.concatenate(sums + alphas + bys + nexts + bxs, 0), z_sum)
    bz_z = exact_dot(jnp.concatenate(bzs, 0), z_even)
    source = exact_dot(y_sum, along[0:128]) * 0.125
    alpha = exact_dot(y_sum, along[128:256]) * 0.125
    y_lower = exact_dot(y_even, along[256:384]) * 0.0625
    y_upper = (exact_dot(y_next, along[256:384]) + exact_dot(y_last, along[384:512])) * 0.0625
    x_lower = exact_dot(y_sum, along[512:640]) * 0.0625
    x_upper = exact_dot(y_sum, along[520:648]) * 0.0625
    z_lower = exact_dot(y_sum, bz_z) * 0.0625
    z_upper = next_lane(z_lower)
    diagonal = alpha + ((x_lower + x_upper) + (y_lower + y_upper) + (z_lower + z_upper))
    arrays = (source, inverse_of(diagonal, alpha), x_lower, y_lower, z_lower)
    _, lane = iotas((8, 128))

    def tile(value, t):
        return jnp.where(lane < 64, value[16 * t : 16 * t + 8], pltpu.roll(value[16 * t + 8 : 16 * t + 16], 64, 1))

    for t in range(4):
        for a, value in enumerate(arrays):
            (mid_first if t < 2 else mid_last)[t % 2, a] = tile(value, t)
        own_out[t, 0] = tile(diagonal, t)
        own_out[t, 1] = tile(alpha, t)


def mid_message_kernel(low, first, last, high, near, far):
    tiles = [ref[s] for ref in (low, first, last, high) for s in range(2)]
    for s in range(8):
        near[s] = tiles[s]
        if 0 < s < 7:
            far[s - 1] = tiles[s]


def mid_kernel(mine, low1, high1, low2, high2, own, level_out, low_out, co, r, b):
    q0 = even_mask((24, 128))
    _, lane = iotas((8, 128))
    keep = low_rows((8, 128))
    zero = jnp.zeros((8, 128), F32)
    clear_guards(r, b, 16)

    def part(tile, p):
        return jnp.where(lane < 64, pltpu.roll(tile, 64, 1) if p % 2 else tile, 0.0)

    def planes(p, a):
        t = p // 2
        c, h1, w1 = part(mine[t, a], p), part(high1[t, a], p), part(low1[t, a], p)
        inner = 0 < t < 7
        h2 = part(high2[t - 1, a], p) if inner else zero
        w2 = part(low2[t - 1, a], p) if inner else zero
        e0 = [jnp.where(keep, c, half(h1)), jnp.where(keep, h2, 0.0), jnp.where(keep, w2, half(w1))]
        e1 = [jnp.where(keep, half(c), h1), jnp.where(keep, half(h2), 0.0), jnp.where(keep, half(w2), w1)]
        return jnp.concatenate(e0, 0), jnp.concatenate(e1, 0)

    bx0, bx1 = planes(0, 2)
    for p in range(16):
        co[S_R, p], co[S_B, p] = halves(q0, *planes(p, 0))
        co[I_R, p], co[I_B, p] = halves(q0, *planes(p, 1))
        n0, n1 = planes(p + 1, 2) if p < 15 else (jnp.zeros_like(bx0), bx1)
        put_faces(co, p, q0, (bx0, bx1, n0), planes(p, 3), planes(p, 4))
        bx0, bx1 = n0, n1
        if 4 <= p < 12:
            d = part(own[p // 2 - 2, 0], p)
            d = jnp.concatenate([d, d, d], 0), jnp.concatenate([half(d)] * 3, 0)
            co[D_R, p], co[D_B, p] = halves(q0, *d)
    smooth_cone(co, r, b, 8, 4, q0)
    sums = jnp.zeros((32, 128), F32)
    bz_z = zero
    for k in range(8):
        p = k + 4
        red, black = residual(co, r, b, p, q0)
        level_out[0, k] = r[p + 1][:8]
        level_out[1, k] = b[p + 1][:8]
        mid = [part(mine[p // 2, a], p) for a in (2, 3, 4)]
        stack = jnp.concatenate([(red + black)[:8], part(own[p // 2 - 2, 1], p), mid[0], mid[1]], 0)
        sums += exact_dot(stack, one_hot((128, 128), lambda i, j: ((i >> 1) == j - 16 * k + 8) & ((j >> 4) == k)))
        bz_z += exact_dot(mid[2], one_hot((128, 128), lambda i, j: (i == 2 * (j - 16 * k + 8)) & ((j >> 4) == k)))

    def rows(out_row, test):
        return one_hot((16, 8), lambda i, j: ((i >> 1) == out_row) & test(i & 1, j))

    total = exact_dot(rows(0, lambda i, j: (j < 4) & ((j >> 1) == i)), sums[0:8]) * 0.125
    total += exact_dot(rows(1, lambda i, j: ((j & 3) >> 1) == i), sums[8:16]) * 0.125
    total += exact_dot(rows(2, lambda i, j: (j < 4) & ((j >> 1) == i)), sums[16:24]) * 0.0625
    total += exact_dot(rows(3, lambda i, j: (j & 3) == 2 * i), sums[24:32]) * 0.0625
    total += exact_dot(rows(4, lambda i, j: ((j & 3) >> 1) == i), bz_z) * 0.0625
    for j in range(low_out.shape[0]):
        low_out[j] = total


def whole_y_kernel(gathered, out):
    flat = gathered[...].reshape(256, 128)

    def test(i, j):
        k, y = i >> 5, i & 31
        return j == (y >> 1) * 16 + 2 * k + (y & 1)

    out[...] = exact_dot(one_hot((160, 256), test), flat)


def copies_kernel(left, own, right, out):
    for g in range(out.shape[0]):
        for s, ref in enumerate((left, own, right)):
            out[g, s] = ref[...]


def coarse_kernel(sweeps, index, gathered, level, fine, out, co, r, b):
    shape = (32, 128)
    q0 = even_mask(shape)
    row, lane = iotas(shape)
    r[...] = jnp.zeros_like(r)
    b[...] = jnp.zeros_like(b)

    def plane(a, i):
        total = jnp.zeros(shape, F32)
        for side in range(2):
            x = i + 16 * side
            for s in range(3):
                target = 64 * side + 16 * s
                block = gathered[x // 8, s, 32 * a : 32 * a + 32]
                shift = (target - 16 * (x % 8)) % 128
                moved = pltpu.roll(block, shift, 1) if shift else block
                total = jnp.where((lane >> 4) == target // 16, moved, total)
        return total

    first_bx = plane(2, 0)
    bx0 = first_bx
    for p in range(8):
        x = 2 * p
        co[S_R, p], co[S_B, p] = halves(q0, plane(0, x), plane(0, x + 1))
        bx1 = plane(2, x + 1)
        bx2 = plane(2, x + 2) if p < 7 else jnp.where(lane < 64, pltpu.roll(first_bx, 64, 1), 0.0)
        by, bz = (plane(3, x), plane(3, x + 1)), (plane(4, x), plane(4, x + 1))
        fx, fy, fyp, fz = put_faces(co, p, q0, (bx0, bx1, bx2), by, bz)
        bx0 = bx2
        yp_r, yp_b = jnp.where(row == 31, 0.0, fyp[0]), jnp.where(row == 31, 0.0, fyp[1])
        co[YP_R, p], co[YP_B, p] = yp_r, yp_b
        co[YM_R, p], co[YM_B, p] = jnp.where(row == 0, 0.0, fy[0]), jnp.where(row == 0, 0.0, fy[1])
        a_r, a_b = halves(q0, plane(1, x), plane(1, x + 1))
        d_r = a_r + ((fx[0] + fz[0]) + (fy[0] + yp_r))
        d_b = a_b + ((fx[1] + fz[1]) + (fy[1] + yp_b))
        co[I_R, p], co[I_B, p] = inverse_of(d_r, a_r), inverse_of(d_b, a_b)

    def join(ref):
        ref[0] = jnp.where(lane < 64, 0.0, pltpu.roll(ref[8], 64, 1))
        ref[9] = jnp.where(lane < 64, pltpu.roll(ref[1], 64, 1), 0.0)

    def sweep(step, carry):
        relax(co, r, b, range(8), True, q0)
        join(r)
        relax(co, b, r, range(8), False, q0)
        join(b)
        return carry

    lax.fori_loop(0, sweeps, sweep, 0)

    gy, gx = index[0], index[1]
    ring, place = gx // RING, lax.rem(gx, RING)
    side, base = ring // 2, 4 * lax.rem(ring, 2)
    own = []
    for k in range(8):
        red, black = r[base + k // 2 + 1], b[base + k // 2 + 1]
        value = jnp.where(q0, red, black) if k % 2 == 0 else jnp.where(q0, black, red)
        value = pltpu.roll(value, lax.rem(32 - 2 * gy, 32), 0)
        own.append(pltpu.roll(value, 64 * side, 1)[:8])
    q0 = even_mask((8, 128))
    row, lane = iotas((8, 128))
    up = exact_dot(jnp.concatenate(own, 0), one_hot((128, 128), lambda i, j: (j >> 1) + 8 == i))
    spread = one_hot((64, 64), lambda i, j: ((i >> 3) == (j >> 3)) & (((i & 3) >> 1) == (j & 7)))
    up = exact_dot(spread, up)
    mid = []
    for k in range(8):
        add = up[8 * k : 8 * k + 8]
        mid.extend(halves(q0, level[0, k] + add, level[1, k] + add))
        mine = pltpu.roll(own[k], lax.rem(16 * place + 112, 128), 1)
        out[k, 2] = jnp.where(((lane >> 4) == place) & (row < 2), mine, 0.0)
    wide = exact_dot(jnp.concatenate(mid, 0), one_hot((128, 128), lambda i, j: (j >> 1) == i))
    spread = one_hot((128, 128), lambda i, j: ((i >> 3) == (j >> 3)) & (((i & 7) >> 1) == (j & 7)))
    wide = exact_dot(spread, wide)
    for j in range(16):
        add = wide[8 * j : 8 * j + 8]
        e0, e1 = halves(q0, fine[0, j] + add, fine[1, j] + add)
        out[j // 2, j % 2] = jnp.where(lane < 64, pltpu.roll(e0, 96, 1), pltpu.roll(e1, 32, 1))


def finish_kernel(pieces, fine_out, coarse_out):
    _, lane = iotas((8, 128))
    for t in range(2):
        for c in range(4):
            a, b = pieces[2 * c, t], pieces[2 * c + 1, t]
            span = slice(128 * c, 128 * c + 128)
            fine_out[2 * t, :, span] = jnp.where(lane < 64, a, pltpu.roll(b, 64, 1))
            fine_out[2 * t + 1, :, span] = jnp.where(lane < 64, pltpu.roll(a, 64, 1), b)
    total = pieces[0, 2]
    for j in range(1, RING):
        total = total + pieces[j, 2]
    coarse_out[0] = total[:2]


def in_rings(values, steps):
    count = lax.axis_size("gx")
    pairs = [(i, i + steps) for i in range(count) if 0 <= i % RING + steps < RING]
    return lax.ppermute(values, "gx", pairs)


def on_device(rhs, alpha, beta_x, beta_y, beta_z):
    count_x, count_y = lax.axis_size("gx"), lax.axis_size("gy")
    groups = count_x // RING
    rings = [[RING * i + j for j in range(RING)] for i in range(groups)]
    across = [list(c) for c in zip(*rings)]
    index = jnp.stack([lax.axis_index("gy"), lax.axis_index("gx")]).astype(jnp.int32)

    (own,) = call(to_windows_kernel, [(RING, 5, 4, 8, 128)])(rhs, alpha, beta_x, beta_y, beta_z)
    own = lax.all_to_all(own, "gx", 0, 0, tiled=True, axis_index_groups=rings)
    to_low, to_high, first_by = call(
        x_messages_kernel, [(41, 8, 128), (40, 8, 128), (32, 128)]
    )(own)
    low, high = shifted(to_high, 1, "gx", RING), shifted(to_low, 1, "gx", -RING)
    mine, beyond_x = call(
        y_message_kernel, [(12, 5, 4, 8, 128), (8, 128)]
    )(low, own, high)
    low, high = shifted(mine, 1, "gy", 1), shifted(mine, 1, "gy", -1)
    beyond_y = shifted(first_by, 0, "gy", -2)
    fine, mid_first, mid_last, mid_own = call(
        fine_kernel,
        [(2, 16, 8, 128), (2, 5, 8, 128), (2, 5, 8, 128), (4, 2, 8, 128)],
        [(17, 24, 24, 128), (26, 24, 128), (26, 24, 128)],
    )(mine, low, high, beyond_x, beyond_y)

    low, high = shifted(mid_last, 0, "gx", RING), shifted(mid_first, 0, "gx", -RING)
    near, far = call(
        mid_message_kernel, [(8, 5, 8, 128), (6, 5, 8, 128)]
    )(low, mid_first, mid_last, high)
    level, low = call(
        mid_kernel,
        [(2, 8, 8, 128), (count_y, 16, 128)],
        [(17, 16, 24, 128), (18, 24, 128), (18, 24, 128)],
    )(
        near, shifted(near, 0, "gy", 1), shifted(near, 0, "gy", -1),
        shifted(far, 0, "gy", 2), shifted(far, 0, "gy", -2), mid_own,
    )

    low = lax.all_to_all(low, "gy", 0, 0, tiled=True)
    (low,) = call(whole_y_kernel, [(160, 128)])(low)
    (low,) = call(copies_kernel, [(groups, 3, 160, 128)])(in_rings(low, 1), low, in_rings(low, -1))
    low = lax.all_to_all(low, "gx", 0, 0, tiled=True, axis_index_groups=across)
    (pieces,) = call(
        lambda *refs: coarse_kernel(8, *refs),
        [(RING, 3, 8, 128)],
        [(17, 8, 32, 128), (10, 32, 128), (10, 32, 128)],
        smem=(0,),
    )(index, low, level, fine)
    pieces = lax.all_to_all(pieces, "gx", 0, 0, tiled=True, axis_index_groups=rings)
    fine_solution, coarse = call(finish_kernel, [rhs.shape, (1, 2, 128)])(pieces)
    return fine_solution, coarse


def solution(mesh):
    placed = P("gx", "gy", None)
    return jax.shard_map(
        on_device,
        mesh=mesh,
        in_specs=(placed,) * 5,
        out_specs=(placed, placed),
        check_vma=False,
    )
```

```python
import jax
import jax.numpy as jnp
from jax import lax
from jax.experimental import pallas as pl
from jax.experimental.pallas import tpu as pltpu
from jax.sharding import PartitionSpec as P

F32 = jnp.float32
RHS, ALPHA, BX, BY, BZ = range(5)
VMEM_BYTES = 20 * 2**20
ALL_VMEM = 62 * 2**20
RING = 8


def shifted(values, axis, name, steps):
    count = lax.axis_size(name)
    lead, last = max(0, -steps), min(count, count - steps)
    return lax.ppermute(values, name, [(i, i + steps) for i in range(lead, last)])


def call(kernel, outs, scratch=(), copied=False):
    def run(*args):
        space = pltpu.HBM if copied else pltpu.VMEM
        buffers = [pltpu.VMEM(a.shape, F32) for a in args] if copied else []
        sems = [pltpu.SemaphoreType.DMA] * len(args) if copied else []
        return pl.pallas_call(
            kernel,
            out_shape=[jax.ShapeDtypeStruct(s, F32) for s in outs],
            in_specs=[pl.BlockSpec(memory_space=space)] * len(args),
            out_specs=[pl.BlockSpec(memory_space=pltpu.VMEM)] * len(outs),
            scratch_shapes=[pltpu.VMEM(s, F32) for s in scratch] + buffers + sems,
            compiler_params=pltpu.CompilerParams(vmem_limit_bytes=ALL_VMEM if copied else VMEM_BYTES),
        )(*args)

    return run


def iotas(shape):
    return lax.broadcasted_iota(jnp.int32, shape, 0), lax.broadcasted_iota(jnp.int32, shape, 1)


def even_mask(shape):
    row, lane = iotas(shape)
    return ((row + lane) & 1) == 0


def half(x):
    return pltpu.roll(x, 4, 0)


def prev_row(x):
    return pltpu.roll(x, 1, 0)


def next_row(x):
    return pltpu.roll(x, x.shape[0] - 1, 0)


def prev_lane(x):
    return pltpu.roll(x, 1, 1)


def next_lane(x):
    return pltpu.roll(x, x.shape[1] - 1, 1)


def exact_dot(a, b):
    return jnp.dot(a, b, precision=lax.Precision.HIGHEST, preferred_element_type=F32)


def one_hot(shape, test):
    row, col = iotas(shape)
    return jnp.where(test(row, col), 1.0, 0.0).astype(F32)


def low_rows(shape):
    row, _ = iotas(shape)
    return (row & 7) < 4


def inverse_of(diagonal, cell):
    inside = cell > 0.0
    return jnp.where(inside, 1.0 / jnp.where(inside, diagonal, 1.0), 0.0)


def halves(q0, e0, e1):
    return jnp.where(q0, e0, e1), jnp.where(q0, e1, e0)


def clear_guards(r, b, n):
    for ref in (r, b):
        ref[0] = jnp.zeros_like(ref[0])
        ref[n + 1] = jnp.zeros_like(ref[n + 1])


S_R, S_B, WP, WO_R, WO_B, YM_R, YM_B, YP_R, YP_B, ZM_R, ZM_B, ZP_R, ZP_B, I_R, I_B, D_R, D_B = range(17)


def beside(co, src, p, red, q0):
    v = src[p + 1]
    before, after = src[p], src[p + 2]
    other = jnp.where(q0, before, after) if red else jnp.where(q0, after, before)
    wo, ym, yp, zm, zp = (
        (WO_R, YM_R, YP_R, ZM_R, ZP_R) if red else (WO_B, YM_B, YP_B, ZM_B, ZP_B)
    )
    total = co[WP, p] * v + co[wo, p] * other
    total = total + (co[ym, p] * prev_row(v) + co[yp, p] * next_row(v))
    return total + (co[zm, p] * prev_lane(v) + co[zp, p] * next_lane(v))


def relax(co, dst, src, pairs, red, q0):
    s, inv = (S_R, I_R) if red else (S_B, I_B)
    for p in pairs:
        dst[p + 1] = (co[s, p] + beside(co, src, p, red, q0)) * co[inv, p]


def first_red(co, dst, pairs):
    for p in pairs:
        dst[p + 1] = co[S_R, p] * co[I_R, p]


def residual(co, r, b, p, q0):
    red = co[S_R, p] - (co[D_R, p] * r[p + 1] - beside(co, b, p, True, q0))
    black = co[S_B, p] - (co[D_B, p] * b[p + 1] - beside(co, r, p, False, q0))
    return red, black


def put_faces(co, p, q0, bx, by, bz):
    b0, b1, b2 = bx
    wo_r, wo_b = halves(q0, b0, b2)
    y_r, y_b = halves(q0, *by)
    z_r, z_b = halves(q0, *bz)
    yp_r, yp_b = next_row(y_b), next_row(y_r)
    zp_r, zp_b = next_lane(z_b), next_lane(z_r)
    co[WP, p], co[WO_R, p], co[WO_B, p] = b1, wo_r, wo_b
    co[YM_R, p], co[YM_B, p], co[YP_R, p], co[YP_B, p] = y_r, y_b, yp_r, yp_b
    co[ZM_R, p], co[ZM_B, p], co[ZP_R, p], co[ZP_B, p] = z_r, z_b, zp_r, zp_b
    return (b1 + wo_r, b1 + wo_b), (y_r, y_b), (yp_r, yp_b), (z_r + zp_r, z_b + zp_b)


def smooth_cone(co, r, b, own, halo, q0):
    def pairs(reach):
        extra = min(halo, (reach + 1) // 2)
        return range(halo - extra, halo + own + extra)

    first_red(co, r, pairs(8))
    for step in range(2, 9):
        red = step % 2 == 1
        relax(co, r if red else b, b if red else r, pairs(9 - step), red, q0)


def to_windows_kernel(*refs):
    args, out, buffers, sems = refs[:5], refs[5], refs[6:11], refs[11:]
    copies = [pltpu.make_async_copy(*c) for c in zip(args, buffers, sems)]
    for c in copies:
        c.start()
    _, lane = iotas((8, 128))
    zero = jnp.zeros((8, 128), F32)
    for a, ref in enumerate(buffers):
        copies[a].wait()
        for x in range(4):
            tiles = [ref[x, :, 128 * c : 128 * c + 128] for c in range(4)]
            up = [pltpu.roll(t, 32, 1) for t in tiles]
            down = [pltpu.roll(t, 96, 1) for t in tiles]
            for c in range(4):
                out[2 * c, a, x] = jnp.where(lane < 32, up[c - 1] if c else zero, up[c])
                out[2 * c + 1, a, x] = jnp.where(lane < 96, down[c], down[c + 1] if c < 3 else zero)


def flat(s, a, x):
    return (s * 5 + a) * 4 + x


def x_messages_kernel(own, to_low, to_high, first_by):
    for a in range(5):
        for x in range(4):
            for s in range(2):
                to_low[flat(s, a, x)] = own[s, a, x]
                to_high[flat(s, a, x)] = own[6 + s, a, x]
    to_low[40] = own[2, BX, 0]
    for x in range(32):
        first_by[x : x + 1] = own[x // 4, BY, x % 4][:1]


def corner_messages_kernel(low, high, to_low, to_high):
    keep = low_rows((8, 128))
    for a in range(5):
        for x in range(4):
            for ref in (to_low, to_high):
                ref[flat(0, a, x)] = low[flat(1, a, x)]
                ref[flat(1, a, x)] = high[flat(0, a, x)]
            outer_low, outer_high = low[flat(0, a, x)], high[flat(1, a, x)]
            to_low[flat(2, a, x)] = jnp.where(keep, outer_low, half(outer_high))
            to_high[flat(2, a, x)] = jnp.where(keep, half(outer_low), outer_high)


def fine_kernel(
    own, x_low, x_high, y_low, y_high, corner_low, corner_high, beyond_y,
    fine_out, mid_first, mid_last, own_out, co, r, b,
):
    q0 = even_mask((24, 128))
    row, lane = iotas((24, 128))
    clear_guards(r, b, 24)
    zero = jnp.zeros((8, 128), F32)

    def plane(a, x):
        block, i = x // 4, x % 4
        if 2 <= block < 10:
            tiles = [ref[block - 2, a, i] for ref in (own, y_high, y_low)]
        elif block in (1, 10):
            side = int(block == 10)
            tiles = [(x_high if side else x_low)[flat(1 - side, a, i)]]
            tiles += [ref[flat(side, a, i)] for ref in (corner_high, corner_low)]
        else:
            up, down = corner_high[flat(2, a, i)], corner_low[flat(2, a, i)]
            if block == 0:
                tiles = [x_low[flat(0, a, i)], up, half(down)]
            else:
                tiles = [x_high[flat(1, a, i)], half(up), down]
        return jnp.concatenate(tiles, 0)

    bx0 = plane(BX, 0)
    for p in range(24):
        x = 2 * p
        co[S_R, p], co[S_B, p] = halves(q0, plane(RHS, x), plane(RHS, x + 1))
        bx1 = plane(BX, x + 1)
        bx2 = plane(BX, x + 2) if p < 23 else jnp.concatenate([x_high[40], zero, zero], 0)
        by = plane(BY, x), plane(BY, x + 1)
        bz = plane(BZ, x), plane(BZ, x + 1)
        fx, fy, fyp, fz = put_faces(co, p, q0, (bx0, bx1, bx2), by, bz)
        bx0 = bx2
        yp_r, yp_b = fyp
        if 4 <= p < 20:
            e0, e1 = beyond_y[x - 8 : x - 7], beyond_y[x - 7 : x - 6]
            up_r, up_b = halves(q0[15:16], e0, e1)
            yp_r = jnp.where(row == 15, up_r, yp_r)
            yp_b = jnp.where(row == 15, up_b, yp_b)
            co[YP_R, p], co[YP_B, p] = yp_r, yp_b
        a_r, a_b = halves(q0, plane(ALPHA, x), plane(ALPHA, x + 1))
        d_r = a_r + ((fx[0] + fz[0]) + (fy[0] + yp_r))
        d_b = a_b + ((fx[1] + fz[1]) + (fy[1] + yp_b))
        co[D_R, p], co[D_B, p] = d_r, d_b
        co[I_R, p], co[I_B, p] = inverse_of(d_r, a_r), inverse_of(d_b, a_b)
    smooth_cone(co, r, b, 16, 4, q0)
    sums, alphas, bys, nexts, bxs, bzs = [], [], [], [], [], []
    for j in range(16):
        p = j + 4
        red, black = residual(co, r, b, p, q0)
        sums.append((red + black)[:8])
        fine_out[0, j] = r[p + 1][:8]
        fine_out[1, j] = b[p + 1][:8]
        s, x = j // 2, 2 * (j % 2)
        alphas.append(own[s, ALPHA, x] + own[s, ALPHA, x + 1])
        bys.append(own[s, BY, x] + own[s, BY, x + 1])
        nexts.append(y_high[s, BY, x] + y_high[s, BY, x + 1])
        bzs.append(own[s, BZ, x] + own[s, BZ, x + 1])
        bxs.append(own[s, BX, x])
    bxs.append(x_high[flat(0, BX, 0)])
    z_sum = one_hot((128, 128), lambda i, j: (i >> 1) == j)
    z_even = one_hot((128, 128), lambda i, j: i == 2 * j)
    y_sum = one_hot((64, 128), lambda i, j: (j >> 1) == i)
    y_even = one_hot((64, 128), lambda i, j: j == 2 * i)
    y_next = one_hot((64, 128), lambda i, j: ((i & 3) < 3) & (j == 2 * i + 2))
    y_last = one_hot((64, 128), lambda i, j: ((i & 3) == 3) & (j == 8 * (i >> 2)))
    along = exact_dot(jnp.concatenate(sums + alphas + bys + nexts + bxs, 0), z_sum)
    bz_z = exact_dot(jnp.concatenate(bzs, 0), z_even)
    source = exact_dot(y_sum, along[0:128]) * 0.125
    alpha = exact_dot(y_sum, along[128:256]) * 0.125
    y_lower = exact_dot(y_even, along[256:384]) * 0.0625
    y_upper = (exact_dot(y_next, along[256:384]) + exact_dot(y_last, along[384:512])) * 0.0625
    x_lower = exact_dot(y_sum, along[512:640]) * 0.0625
    x_upper = exact_dot(y_sum, along[520:648]) * 0.0625
    z_lower = exact_dot(y_sum, bz_z) * 0.0625
    z_upper = next_lane(z_lower)
    diagonal = alpha + ((x_lower + x_upper) + (y_lower + y_upper) + (z_lower + z_upper))
    arrays = (source, inverse_of(diagonal, alpha), x_lower, y_lower, z_lower)
    _, lane = iotas((8, 128))

    def tile(value, t):
        return jnp.where(lane < 64, value[16 * t : 16 * t + 8], pltpu.roll(value[16 * t + 8 : 16 * t + 16], 64, 1))

    for t in range(4):
        for a, value in enumerate(arrays):
            (mid_first if t < 2 else mid_last)[t % 2, a] = tile(value, t)
        own_out[t, 0] = tile(diagonal, t)
        own_out[t, 1] = tile(alpha, t)


def mid_message_kernel(low, first, last, high, near, far):
    tiles = [ref[s] for ref in (low, first, last, high) for s in range(2)]
    for s in range(8):
        near[s] = tiles[s]
        if 0 < s < 7:
            far[s - 1] = tiles[s]


def mid_kernel(mine, low1, high1, low2, high2, own, level_out, low_out, co, r, b):
    q0 = even_mask((24, 128))
    _, lane = iotas((8, 128))
    keep = low_rows((8, 128))
    zero = jnp.zeros((8, 128), F32)
    clear_guards(r, b, 16)

    def part(tile, p):
        return jnp.where(lane < 64, pltpu.roll(tile, 64, 1) if p % 2 else tile, 0.0)

    def planes(p, a):
        t = p // 2
        c, h1, w1 = part(mine[t, a], p), part(high1[t, a], p), part(low1[t, a], p)
        inner = 0 < t < 7
        h2 = part(high2[t - 1, a], p) if inner else zero
        w2 = part(low2[t - 1, a], p) if inner else zero
        e0 = [jnp.where(keep, c, half(h1)), jnp.where(keep, h2, 0.0), jnp.where(keep, w2, half(w1))]
        e1 = [jnp.where(keep, half(c), h1), jnp.where(keep, half(h2), 0.0), jnp.where(keep, half(w2), w1)]
        return jnp.concatenate(e0, 0), jnp.concatenate(e1, 0)

    bx0, bx1 = planes(0, 2)
    for p in range(16):
        co[S_R, p], co[S_B, p] = halves(q0, *planes(p, 0))
        co[I_R, p], co[I_B, p] = halves(q0, *planes(p, 1))
        n0, n1 = planes(p + 1, 2) if p < 15 else (jnp.zeros_like(bx0), bx1)
        put_faces(co, p, q0, (bx0, bx1, n0), planes(p, 3), planes(p, 4))
        bx0, bx1 = n0, n1
        if 4 <= p < 12:
            d = part(own[p // 2 - 2, 0], p)
            d = jnp.concatenate([d, d, d], 0), jnp.concatenate([half(d)] * 3, 0)
            co[D_R, p], co[D_B, p] = halves(q0, *d)
    smooth_cone(co, r, b, 8, 4, q0)
    sums = jnp.zeros((32, 128), F32)
    bz_z = zero
    for k in range(8):
        p = k + 4
        red, black = residual(co, r, b, p, q0)
        level_out[0, k] = r[p + 1][:8]
        level_out[1, k] = b[p + 1][:8]
        mid = [part(mine[p // 2, a], p) for a in (2, 3, 4)]
        stack = jnp.concatenate([(red + black)[:8], part(own[p // 2 - 2, 1], p), mid[0], mid[1]], 0)
        sums += exact_dot(stack, one_hot((128, 128), lambda i, j: ((i >> 1) == j - 16 * k + 8) & ((j >> 4) == k)))
        bz_z += exact_dot(mid[2], one_hot((128, 128), lambda i, j: (i == 2 * (j - 16 * k + 8)) & ((j >> 4) == k)))

    def rows(out_row, test):
        return one_hot((16, 8), lambda i, j: ((i >> 1) == out_row) & test(i & 1, j))

    total = exact_dot(rows(0, lambda i, j: (j < 4) & ((j >> 1) == i)), sums[0:8]) * 0.125
    total += exact_dot(rows(1, lambda i, j: ((j & 3) >> 1) == i), sums[8:16]) * 0.125
    total += exact_dot(rows(2, lambda i, j: (j < 4) & ((j >> 1) == i)), sums[16:24]) * 0.0625
    total += exact_dot(rows(3, lambda i, j: (j & 3) == 2 * i), sums[24:32]) * 0.0625
    total += exact_dot(rows(4, lambda i, j: ((j & 3) >> 1) == i), bz_z) * 0.0625
    for j in range(low_out.shape[0]):
        low_out[j] = total


def whole_y_kernel(gathered, out):
    flat = gathered[...].reshape(256, 128)

    def test(i, j):
        k, y = i >> 5, i & 31
        return j == (y >> 1) * 16 + 2 * k + (y & 1)

    out[...] = exact_dot(one_hot((160, 256), test), flat)


def copies_kernel(left, own, right, out):
    for g in range(out.shape[0]):
        for s, ref in enumerate((left, own, right)):
            out[g, s] = ref[...]


def coarse_kernel(sweeps, gathered, level, fine, out, co, r, b):
    shape = (32, 128)
    q0 = even_mask(shape)
    row, lane = iotas(shape)
    r[...] = jnp.zeros_like(r)
    b[...] = jnp.zeros_like(b)

    def plane(a, i):
        total = jnp.zeros(shape, F32)
        for side in range(2):
            x = i + 16 * side
            for s in range(3):
                target = 64 * side + 16 * s
                block = gathered[x // 8, s, 32 * a : 32 * a + 32]
                shift = (target - 16 * (x % 8)) % 128
                moved = pltpu.roll(block, shift, 1) if shift else block
                total = jnp.where((lane >> 4) == target // 16, moved, total)
        return total

    first_bx = plane(2, 0)
    bx0 = first_bx
    for p in range(8):
        x = 2 * p
        co[S_R, p], co[S_B, p] = halves(q0, plane(0, x), plane(0, x + 1))
        bx1 = plane(2, x + 1)
        bx2 = plane(2, x + 2) if p < 7 else jnp.where(lane < 64, pltpu.roll(first_bx, 64, 1), 0.0)
        by, bz = (plane(3, x), plane(3, x + 1)), (plane(4, x), plane(4, x + 1))
        fx, fy, fyp, fz = put_faces(co, p, q0, (bx0, bx1, bx2), by, bz)
        bx0 = bx2
        yp_r, yp_b = jnp.where(row == 31, 0.0, fyp[0]), jnp.where(row == 31, 0.0, fyp[1])
        co[YP_R, p], co[YP_B, p] = yp_r, yp_b
        co[YM_R, p], co[YM_B, p] = jnp.where(row == 0, 0.0, fy[0]), jnp.where(row == 0, 0.0, fy[1])
        a_r, a_b = halves(q0, plane(1, x), plane(1, x + 1))
        d_r = a_r + ((fx[0] + fz[0]) + (fy[0] + yp_r))
        d_b = a_b + ((fx[1] + fz[1]) + (fy[1] + yp_b))
        co[I_R, p], co[I_B, p] = inverse_of(d_r, a_r), inverse_of(d_b, a_b)

    def join(ref):
        ref[0] = jnp.where(lane < 64, 0.0, pltpu.roll(ref[8], 64, 1))
        ref[9] = jnp.where(lane < 64, pltpu.roll(ref[1], 64, 1), 0.0)

    def sweep(step, carry):
        relax(co, r, b, range(8), True, q0)
        join(r)
        relax(co, b, r, range(8), False, q0)
        join(b)
        return carry

    lax.fori_loop(0, sweeps, sweep, 0)

    gy, gx = lax.axis_index("gy"), lax.axis_index("gx")
    ring, place = gx // RING, lax.rem(gx, RING)
    side, base = ring // 2, 4 * lax.rem(ring, 2)
    own = []
    for k in range(8):
        red, black = r[base + k // 2 + 1], b[base + k // 2 + 1]
        value = jnp.where(q0, red, black) if k % 2 == 0 else jnp.where(q0, black, red)
        value = pltpu.roll(value, lax.rem(32 - 2 * gy, 32), 0)
        own.append(pltpu.roll(value, 64 * side, 1)[:8])
    q0 = even_mask((8, 128))
    row, lane = iotas((8, 128))
    up = exact_dot(jnp.concatenate(own, 0), one_hot((128, 128), lambda i, j: (j >> 1) + 8 == i))
    spread = one_hot((64, 64), lambda i, j: ((i >> 3) == (j >> 3)) & (((i & 3) >> 1) == (j & 7)))
    up = exact_dot(spread, up)
    mid = []
    for k in range(8):
        add = up[8 * k : 8 * k + 8]
        mid.extend(halves(q0, level[0, k] + add, level[1, k] + add))
        mine = pltpu.roll(own[k], lax.rem(16 * place + 112, 128), 1)
        out[k, 2] = jnp.where(((lane >> 4) == place) & (row < 2), mine, 0.0)
    wide = exact_dot(jnp.concatenate(mid, 0), one_hot((128, 128), lambda i, j: (j >> 1) == i))
    spread = one_hot((128, 128), lambda i, j: ((i >> 3) == (j >> 3)) & (((i & 7) >> 1) == (j & 7)))
    wide = exact_dot(spread, wide)
    for j in range(16):
        add = wide[8 * j : 8 * j + 8]
        e0, e1 = halves(q0, fine[0, j] + add, fine[1, j] + add)
        out[j // 2, j % 2] = jnp.where(lane < 64, pltpu.roll(e0, 96, 1), pltpu.roll(e1, 32, 1))


def finish_kernel(pieces, fine_out, coarse_out):
    _, lane = iotas((8, 128))
    for t in range(2):
        for c in range(4):
            a, b = pieces[2 * c, t], pieces[2 * c + 1, t]
            span = slice(128 * c, 128 * c + 128)
            fine_out[2 * t, :, span] = jnp.where(lane < 64, a, pltpu.roll(b, 64, 1))
            fine_out[2 * t + 1, :, span] = jnp.where(lane < 64, pltpu.roll(a, 64, 1), b)
    total = pieces[0, 2]
    for j in range(1, RING):
        total = total + pieces[j, 2]
    coarse_out[0] = total[:2]


def in_rings(values, steps):
    count = lax.axis_size("gx")
    pairs = [(i, i + steps) for i in range(count) if 0 <= i % RING + steps < RING]
    return lax.ppermute(values, "gx", pairs)


def on_device(rhs, alpha, beta_x, beta_y, beta_z):
    count_x, count_y = lax.axis_size("gx"), lax.axis_size("gy")
    groups = count_x // RING
    rings = [[RING * i + j for j in range(RING)] for i in range(groups)]
    across = [list(c) for c in zip(*rings)]

    (own,) = call(to_windows_kernel, [(RING, 5, 4, 8, 128)], copied=True)(rhs, alpha, beta_x, beta_y, beta_z)
    own = lax.all_to_all(own, "gx", 0, 0, tiled=True, axis_index_groups=rings)
    to_low, to_high, first_by = call(
        x_messages_kernel, [(41, 8, 128), (40, 8, 128), (32, 128)]
    )(own)
    y_low, y_high = shifted(own, 1, "gy", 1), shifted(own, 1, "gy", -1)
    x_low, x_high = shifted(to_high, 1, "gx", RING), shifted(to_low, 1, "gx", -RING)
    beyond_y = shifted(first_by, 0, "gy", -2)
    to_low, to_high = call(
        corner_messages_kernel, [(60, 8, 128), (60, 8, 128)]
    )(x_low, x_high)
    corner_low, corner_high = shifted(to_high, 1, "gy", 1), shifted(to_low, 1, "gy", -1)
    fine, mid_first, mid_last, mid_own = call(
        fine_kernel,
        [(2, 16, 8, 128), (2, 5, 8, 128), (2, 5, 8, 128), (4, 2, 8, 128)],
        [(17, 24, 24, 128), (26, 24, 128), (26, 24, 128)],
    )(own, x_low, x_high, y_low, y_high, corner_low, corner_high, beyond_y)

    low, high = shifted(mid_last, 0, "gx", RING), shifted(mid_first, 0, "gx", -RING)
    near, far = call(
        mid_message_kernel, [(8, 5, 8, 128), (6, 5, 8, 128)]
    )(low, mid_first, mid_last, high)
    level, low = call(
        mid_kernel,
        [(2, 8, 8, 128), (count_y, 16, 128)],
        [(17, 16, 24, 128), (18, 24, 128), (18, 24, 128)],
    )(
        near, shifted(near, 0, "gy", 1), shifted(near, 0, "gy", -1),
        shifted(far, 0, "gy", 2), shifted(far, 0, "gy", -2), mid_own,
    )

    low = lax.all_to_all(low, "gy", 0, 0, tiled=True)
    (low,) = call(whole_y_kernel, [(160, 128)])(low)
    (low,) = call(copies_kernel, [(groups, 3, 160, 128)])(in_rings(low, 1), low, in_rings(low, -1))
    low = lax.all_to_all(low, "gx", 0, 0, tiled=True, axis_index_groups=across)
    (pieces,) = call(
        lambda *refs: coarse_kernel(8, *refs),
        [(RING, 3, 8, 128)],
        [(17, 8, 32, 128), (10, 32, 128), (10, 32, 128)],
    )(low, level, fine)
    pieces = lax.all_to_all(pieces, "gx", 0, 0, tiled=True, axis_index_groups=rings)
    fine_solution, coarse = call(finish_kernel, [rhs.shape, (1, 2, 128)])(pieces)
    return fine_solution, coarse


def solution(mesh):
    placed = P("gx", "gy", None)
    return jax.shard_map(
        on_device,
        mesh=mesh,
        in_specs=(placed,) * 5,
        out_specs=(placed, placed),
        check_vma=False,
    )
```

```python
import jax
import jax.numpy as jnp
import numpy as np
from jax import lax
from jax.experimental import pallas as pl
from jax.experimental.pallas import tpu as pltpu
from jax.sharding import Mesh
from jax.sharding import PartitionSpec as P

F32 = jnp.float32
RHS, ALPHA, BX, BY, BZ = range(5)
VMEM_BYTES = 20 * 2**20
ALL_VMEM = 62 * 2**20
RING = 8


def shifted(values, name, steps):
    count = lax.axis_size(name)
    lead, last = max(0, -steps), min(count, count - steps)
    return lax.ppermute(values, name, [(i, i + steps) for i in range(lead, last)])


def call(kernel, outs, scratch=(), copied=False):
    def run(*args):
        space = pltpu.HBM if copied else pltpu.VMEM
        buffers = [pltpu.VMEM(a.shape, F32) for a in args] if copied else []
        sems = [pltpu.SemaphoreType.DMA] * len(args) if copied else []
        return pl.pallas_call(
            kernel,
            out_shape=[jax.ShapeDtypeStruct(s, F32) for s in outs],
            in_specs=[pl.BlockSpec(memory_space=space)] * len(args),
            out_specs=[pl.BlockSpec(memory_space=pltpu.VMEM)] * len(outs),
            scratch_shapes=[pltpu.VMEM(s, F32) for s in scratch] + buffers + sems,
            compiler_params=pltpu.CompilerParams(vmem_limit_bytes=ALL_VMEM if copied else VMEM_BYTES),
        )(*args)

    return run


def iotas(shape):
    return lax.broadcasted_iota(jnp.int32, shape, 0), lax.broadcasted_iota(jnp.int32, shape, 1)


def even_mask(shape):
    row, lane = iotas(shape)
    return ((row + lane) & 1) == 0


def half(x):
    return pltpu.roll(x, 4, 0)


def prev_row(x):
    return pltpu.roll(x, 1, 0)


def next_row(x):
    return pltpu.roll(x, x.shape[0] - 1, 0)


def prev_lane(x):
    return pltpu.roll(x, 1, 1)


def next_lane(x):
    return pltpu.roll(x, x.shape[1] - 1, 1)


def exact_dot(a, b):
    return jnp.dot(a, b, precision=lax.Precision.HIGHEST, preferred_element_type=F32)


def one_hot(shape, test):
    row, col = iotas(shape)
    return jnp.where(test(row, col), 1.0, 0.0).astype(F32)


def low_rows(shape):
    row, _ = iotas(shape)
    return (row & 7) < 4


def inverse_of(diagonal, cell):
    inside = cell > 0.0
    return jnp.where(inside, 1.0 / jnp.where(inside, diagonal, 1.0), 0.0)


def halves(q0, e0, e1):
    return jnp.where(q0, e0, e1), jnp.where(q0, e1, e0)


def clear_guards(r, b, n):
    for ref in (r, b):
        ref[0] = jnp.zeros_like(ref[0])
        ref[n + 1] = jnp.zeros_like(ref[n + 1])


S_R, S_B, WP, WO_R, WO_B, YM_R, YM_B, YP_R, YP_B, ZM_R, ZM_B, ZP_R, ZP_B, I_R, I_B, D_R, D_B = range(17)


def beside(co, src, p, red, q0):
    v = src[p + 1]
    before, after = src[p], src[p + 2]
    other = jnp.where(q0, before, after) if red else jnp.where(q0, after, before)
    wo, ym, yp, zm, zp = (
        (WO_R, YM_R, YP_R, ZM_R, ZP_R) if red else (WO_B, YM_B, YP_B, ZM_B, ZP_B)
    )
    total = co[WP, p] * v + co[wo, p] * other
    total = total + (co[ym, p] * prev_row(v) + co[yp, p] * next_row(v))
    return total + (co[zm, p] * prev_lane(v) + co[zp, p] * next_lane(v))


def relax(co, dst, src, pairs, red, q0):
    s, inv = (S_R, I_R) if red else (S_B, I_B)
    for p in pairs:
        dst[p + 1] = (co[s, p] + beside(co, src, p, red, q0)) * co[inv, p]


def first_red(co, dst, pairs):
    for p in pairs:
        dst[p + 1] = co[S_R, p] * co[I_R, p]


def residual(co, r, b, p, q0):
    red = co[S_R, p] - (co[D_R, p] * r[p + 1] - beside(co, b, p, True, q0))
    black = co[S_B, p] - (co[D_B, p] * b[p + 1] - beside(co, r, p, False, q0))
    return red, black


def put_faces(co, p, q0, bx, by, bz):
    b0, b1, b2 = bx
    wo_r, wo_b = halves(q0, b0, b2)
    y_r, y_b = halves(q0, *by)
    z_r, z_b = halves(q0, *bz)
    yp_r, yp_b = next_row(y_b), next_row(y_r)
    zp_r, zp_b = next_lane(z_b), next_lane(z_r)
    co[WP, p], co[WO_R, p], co[WO_B, p] = b1, wo_r, wo_b
    co[YM_R, p], co[YM_B, p], co[YP_R, p], co[YP_B, p] = y_r, y_b, yp_r, yp_b
    co[ZM_R, p], co[ZM_B, p], co[ZP_R, p], co[ZP_B, p] = z_r, z_b, zp_r, zp_b
    return (b1 + wo_r, b1 + wo_b), (y_r, y_b), (yp_r, yp_b), (z_r + zp_r, z_b + zp_b)


def smooth_cone(co, r, b, own, halo, q0):
    def pairs(reach):
        extra = min(halo, (reach + 1) // 2)
        return range(halo - extra, halo + own + extra)

    first_red(co, r, pairs(8))
    for step in range(2, 9):
        red = step % 2 == 1
        relax(co, r if red else b, b if red else r, pairs(9 - step), red, q0)


def to_windows_kernel(*refs):
    args, out, buffers, sems = refs[:5], refs[5], refs[6:11], refs[11:]
    copies = [pltpu.make_async_copy(*c) for c in zip(args, buffers, sems)]
    for c in copies:
        c.start()
    _, lane = iotas((8, 128))
    zero = jnp.zeros((8, 128), F32)
    for a, ref in enumerate(buffers):
        copies[a].wait()
        for x in range(4):
            tiles = [ref[x, :, 128 * c : 128 * c + 128] for c in range(4)]
            up = [pltpu.roll(t, 32, 1) for t in tiles]
            down = [pltpu.roll(t, 96, 1) for t in tiles]
            for c in range(4):
                out[2 * c, a, x] = jnp.where(lane < 32, up[c - 1] if c else zero, up[c])
                out[2 * c + 1, a, x] = jnp.where(lane < 96, down[c], down[c + 1] if c < 3 else zero)


def flat(s, a, x):
    return (s * 5 + a) * 4 + x


def x_messages_kernel(own, to_low, to_high, first_by):
    for a in range(5):
        for x in range(4):
            for s in range(2):
                to_low[flat(s, a, x)] = own[s, a, x]
                to_high[flat(s, a, x)] = own[6 + s, a, x]
    to_low[40] = own[2, BX, 0]
    for x in range(32):
        first_by[x : x + 1] = own[x // 4, BY, x % 4][:1]


def corner_messages_kernel(low, high, to_low, to_high):
    keep = low_rows((8, 128))
    for a in range(5):
        for x in range(4):
            for ref in (to_low, to_high):
                ref[flat(0, a, x)] = low[flat(1, a, x)]
                ref[flat(1, a, x)] = high[flat(0, a, x)]
            outer_low, outer_high = low[flat(0, a, x)], high[flat(1, a, x)]
            to_low[flat(2, a, x)] = jnp.where(keep, outer_low, half(outer_high))
            to_high[flat(2, a, x)] = jnp.where(keep, half(outer_low), outer_high)


def fine_kernel(
    own, x_low, x_high, y_low, y_high, corner_low, corner_high, beyond_y,
    fine_out, mid_first, mid_last, own_out, co, r, b,
):
    q0 = even_mask((24, 128))
    row, lane = iotas((24, 128))
    clear_guards(r, b, 24)
    zero = jnp.zeros((8, 128), F32)

    def plane(a, x):
        block, i = x // 4, x % 4
        if 2 <= block < 10:
            tiles = [ref[block - 2, a, i] for ref in (own, y_high, y_low)]
        elif block in (1, 10):
            side = int(block == 10)
            tiles = [(x_high if side else x_low)[flat(1 - side, a, i)]]
            tiles += [ref[flat(side, a, i)] for ref in (corner_high, corner_low)]
        else:
            up, down = corner_high[flat(2, a, i)], corner_low[flat(2, a, i)]
            if block == 0:
                tiles = [x_low[flat(0, a, i)], up, half(down)]
            else:
                tiles = [x_high[flat(1, a, i)], half(up), down]
        return jnp.concatenate(tiles, 0)

    bx0 = plane(BX, 0)
    for p in range(24):
        x = 2 * p
        co[S_R, p], co[S_B, p] = halves(q0, plane(RHS, x), plane(RHS, x + 1))
        bx1 = plane(BX, x + 1)
        bx2 = plane(BX, x + 2) if p < 23 else jnp.concatenate([x_high[40], zero, zero], 0)
        by = plane(BY, x), plane(BY, x + 1)
        bz = plane(BZ, x), plane(BZ, x + 1)
        fx, fy, fyp, fz = put_faces(co, p, q0, (bx0, bx1, bx2), by, bz)
        bx0 = bx2
        yp_r, yp_b = fyp
        if 4 <= p < 20:
            e0, e1 = beyond_y[x - 8 : x - 7], beyond_y[x - 7 : x - 6]
            up_r, up_b = halves(q0[15:16], e0, e1)
            yp_r = jnp.where(row == 15, up_r, yp_r)
            yp_b = jnp.where(row == 15, up_b, yp_b)
            co[YP_R, p], co[YP_B, p] = yp_r, yp_b
        a_r, a_b = halves(q0, plane(ALPHA, x), plane(ALPHA, x + 1))
        d_r = a_r + ((fx[0] + fz[0]) + (fy[0] + yp_r))
        d_b = a_b + ((fx[1] + fz[1]) + (fy[1] + yp_b))
        co[D_R, p], co[D_B, p] = d_r, d_b
        co[I_R, p], co[I_B, p] = inverse_of(d_r, a_r), inverse_of(d_b, a_b)
    smooth_cone(co, r, b, 16, 4, q0)
    sums, alphas, bys, nexts, bxs, bzs = [], [], [], [], [], []
    for j in range(16):
        p = j + 4
        red, black = residual(co, r, b, p, q0)
        sums.append((red + black)[:8])
        fine_out[0, j] = r[p + 1][:8]
        fine_out[1, j] = b[p + 1][:8]
        s, x = j // 2, 2 * (j % 2)
        alphas.append(own[s, ALPHA, x] + own[s, ALPHA, x + 1])
        bys.append(own[s, BY, x] + own[s, BY, x + 1])
        nexts.append(y_high[s, BY, x] + y_high[s, BY, x + 1])
        bzs.append(own[s, BZ, x] + own[s, BZ, x + 1])
        bxs.append(own[s, BX, x])
    bxs.append(x_high[flat(0, BX, 0)])
    z_sum = one_hot((128, 128), lambda i, j: (i >> 1) == j)
    z_even = one_hot((128, 128), lambda i, j: i == 2 * j)
    y_sum = one_hot((64, 128), lambda i, j: (j >> 1) == i)
    y_even = one_hot((64, 128), lambda i, j: j == 2 * i)
    y_next = one_hot((64, 128), lambda i, j: ((i & 3) < 3) & (j == 2 * i + 2))
    y_last = one_hot((64, 128), lambda i, j: ((i & 3) == 3) & (j == 8 * (i >> 2)))
    along = exact_dot(jnp.concatenate(sums + alphas + bys + nexts + bxs, 0), z_sum)
    bz_z = exact_dot(jnp.concatenate(bzs, 0), z_even)
    source = exact_dot(y_sum, along[0:128]) * 0.125
    alpha = exact_dot(y_sum, along[128:256]) * 0.125
    y_lower = exact_dot(y_even, along[256:384]) * 0.0625
    y_upper = (exact_dot(y_next, along[256:384]) + exact_dot(y_last, along[384:512])) * 0.0625
    x_lower = exact_dot(y_sum, along[512:640]) * 0.0625
    x_upper = exact_dot(y_sum, along[520:648]) * 0.0625
    z_lower = exact_dot(y_sum, bz_z) * 0.0625
    z_upper = next_lane(z_lower)
    diagonal = alpha + ((x_lower + x_upper) + (y_lower + y_upper) + (z_lower + z_upper))
    arrays = (source, inverse_of(diagonal, alpha), x_lower, y_lower, z_lower)
    _, lane = iotas((8, 128))

    def tile(value, t):
        return jnp.where(lane < 64, value[16 * t : 16 * t + 8], pltpu.roll(value[16 * t + 8 : 16 * t + 16], 64, 1))

    for t in range(4):
        for a, value in enumerate(arrays):
            (mid_first if t < 2 else mid_last)[t % 2, a] = tile(value, t)
        own_out[t, 0] = tile(diagonal, t)
        own_out[t, 1] = tile(alpha, t)


def mid_message_kernel(low, first, last, high, near, far):
    tiles = [ref[s] for ref in (low, first, last, high) for s in range(2)]
    for s in range(8):
        near[s] = tiles[s]
        if 0 < s < 7:
            far[s - 1] = tiles[s]


def mid_kernel(mine, low1, high1, low2, high2, own, level_out, low_out, co, r, b):
    q0 = even_mask((24, 128))
    _, lane = iotas((8, 128))
    keep = low_rows((8, 128))
    zero = jnp.zeros((8, 128), F32)
    clear_guards(r, b, 16)

    def part(tile, p):
        return jnp.where(lane < 64, pltpu.roll(tile, 64, 1) if p % 2 else tile, 0.0)

    def planes(p, a):
        t = p // 2
        c, h1, w1 = part(mine[t, a], p), part(high1[t, a], p), part(low1[t, a], p)
        inner = 0 < t < 7
        h2 = part(high2[t - 1, a], p) if inner else zero
        w2 = part(low2[t - 1, a], p) if inner else zero
        e0 = [jnp.where(keep, c, half(h1)), jnp.where(keep, h2, 0.0), jnp.where(keep, w2, half(w1))]
        e1 = [jnp.where(keep, half(c), h1), jnp.where(keep, half(h2), 0.0), jnp.where(keep, half(w2), w1)]
        return jnp.concatenate(e0, 0), jnp.concatenate(e1, 0)

    bx0, bx1 = planes(0, 2)
    for p in range(16):
        co[S_R, p], co[S_B, p] = halves(q0, *planes(p, 0))
        co[I_R, p], co[I_B, p] = halves(q0, *planes(p, 1))
        n0, n1 = planes(p + 1, 2) if p < 15 else (jnp.zeros_like(bx0), bx1)
        put_faces(co, p, q0, (bx0, bx1, n0), planes(p, 3), planes(p, 4))
        bx0, bx1 = n0, n1
        if 4 <= p < 12:
            d = part(own[p // 2 - 2, 0], p)
            d = jnp.concatenate([d, d, d], 0), jnp.concatenate([half(d)] * 3, 0)
            co[D_R, p], co[D_B, p] = halves(q0, *d)
    smooth_cone(co, r, b, 8, 4, q0)
    sums = jnp.zeros((32, 128), F32)
    bz_z = zero
    for k in range(8):
        p = k + 4
        red, black = residual(co, r, b, p, q0)
        level_out[0, k] = r[p + 1][:8]
        level_out[1, k] = b[p + 1][:8]
        mid = [part(mine[p // 2, a], p) for a in (2, 3, 4)]
        stack = jnp.concatenate([(red + black)[:8], part(own[p // 2 - 2, 1], p), mid[0], mid[1]], 0)
        sums += exact_dot(stack, one_hot((128, 128), lambda i, j: ((i >> 1) == j - 16 * k + 8) & ((j >> 4) == k)))
        bz_z += exact_dot(mid[2], one_hot((128, 128), lambda i, j: (i == 2 * (j - 16 * k + 8)) & ((j >> 4) == k)))

    def rows(out_row, test):
        return one_hot((16, 8), lambda i, j: ((i >> 1) == out_row) & test(i & 1, j))

    total = exact_dot(rows(0, lambda i, j: (j < 4) & ((j >> 1) == i)), sums[0:8]) * 0.125
    total += exact_dot(rows(1, lambda i, j: ((j & 3) >> 1) == i), sums[8:16]) * 0.125
    total += exact_dot(rows(2, lambda i, j: (j < 4) & ((j >> 1) == i)), sums[16:24]) * 0.0625
    total += exact_dot(rows(3, lambda i, j: (j & 3) == 2 * i), sums[24:32]) * 0.0625
    total += exact_dot(rows(4, lambda i, j: ((j & 3) >> 1) == i), bz_z) * 0.0625
    for k in range(5):
        mine = total[2 * k : 2 * k + 2]
        for j in range(low_out.shape[0]):
            low_out[j, k] = mine


def whole_y_kernel(gathered, out):
    for g in range(out.shape[0]):
        for j in range(16):
            for k in range(5):
                out[g, 32 * k + 2 * j : 32 * k + 2 * j + 2] = gathered[16 * g + j, k]


def coarse_kernel(sweeps, low, own, high, level, fine, out, co, r, b):
    shape = (32, 128)
    q0 = even_mask(shape)
    row, lane = iotas(shape)
    r[...] = jnp.zeros_like(r)
    b[...] = jnp.zeros_like(b)

    def plane(a, i):
        total = jnp.zeros(shape, F32)
        for side in range(2):
            x = i + 16 * side
            for s in range(3):
                target = 64 * side + 16 * s
                block = (low, own, high)[s][x // 8, 32 * a : 32 * a + 32]
                shift = (target - 16 * (x % 8)) % 128
                moved = pltpu.roll(block, shift, 1) if shift else block
                total = jnp.where((lane >> 4) == target // 16, moved, total)
        return total

    first_bx = plane(2, 0)
    bx0 = first_bx
    for p in range(8):
        x = 2 * p
        co[S_R, p], co[S_B, p] = halves(q0, plane(0, x), plane(0, x + 1))
        bx1 = plane(2, x + 1)
        bx2 = plane(2, x + 2) if p < 7 else jnp.where(lane < 64, pltpu.roll(first_bx, 64, 1), 0.0)
        by, bz = (plane(3, x), plane(3, x + 1)), (plane(4, x), plane(4, x + 1))
        fx, fy, fyp, fz = put_faces(co, p, q0, (bx0, bx1, bx2), by, bz)
        bx0 = bx2
        yp_r, yp_b = jnp.where(row == 31, 0.0, fyp[0]), jnp.where(row == 31, 0.0, fyp[1])
        co[YP_R, p], co[YP_B, p] = yp_r, yp_b
        co[YM_R, p], co[YM_B, p] = jnp.where(row == 0, 0.0, fy[0]), jnp.where(row == 0, 0.0, fy[1])
        a_r, a_b = halves(q0, plane(1, x), plane(1, x + 1))
        d_r = a_r + ((fx[0] + fz[0]) + (fy[0] + yp_r))
        d_b = a_b + ((fx[1] + fz[1]) + (fy[1] + yp_b))
        co[I_R, p], co[I_B, p] = inverse_of(d_r, a_r), inverse_of(d_b, a_b)

    def join(ref):
        ref[0] = jnp.where(lane < 64, 0.0, pltpu.roll(ref[8], 64, 1))
        ref[9] = jnp.where(lane < 64, pltpu.roll(ref[1], 64, 1), 0.0)

    def sweep(step, carry):
        relax(co, r, b, range(8), True, q0)
        join(r)
        relax(co, b, r, range(8), False, q0)
        join(b)
        return carry

    lax.fori_loop(0, sweeps, sweep, 0)

    gy, ring, place = (lax.axis_index(name) for name in ("gy", "ring", "place"))
    side, base = ring // 2, 4 * lax.rem(ring, 2)
    parts = []
    for k in range(8):
        red, black = r[base + k // 2 + 1], b[base + k // 2 + 1]
        value = jnp.where(q0, red, black) if k % 2 == 0 else jnp.where(q0, black, red)
        value = pltpu.roll(value, lax.rem(32 - 2 * gy, 32), 0)
        parts.append(pltpu.roll(value, 64 * side, 1)[:8])
    q0 = even_mask((8, 128))
    row, lane = iotas((8, 128))
    up = exact_dot(jnp.concatenate(parts, 0), one_hot((128, 128), lambda i, j: (j >> 1) + 8 == i))
    spread = one_hot((64, 64), lambda i, j: ((i >> 3) == (j >> 3)) & (((i & 3) >> 1) == (j & 7)))
    up = exact_dot(spread, up)
    mid = []
    for k in range(8):
        add = up[8 * k : 8 * k + 8]
        mid.extend(halves(q0, level[0, k] + add, level[1, k] + add))
        mine = pltpu.roll(parts[k], lax.rem(16 * place + 112, 128), 1)
        out[k, 2] = jnp.where(((lane >> 4) == place) & (row < 2), mine, 0.0)
    wide = exact_dot(jnp.concatenate(mid, 0), one_hot((128, 128), lambda i, j: (j >> 1) == i))
    spread = one_hot((128, 128), lambda i, j: ((i >> 3) == (j >> 3)) & (((i & 7) >> 1) == (j & 7)))
    wide = exact_dot(spread, wide)
    for j in range(16):
        add = wide[8 * j : 8 * j + 8]
        e0, e1 = halves(q0, fine[0, j] + add, fine[1, j] + add)
        out[j // 2, j % 2] = jnp.where(lane < 64, pltpu.roll(e0, 96, 1), pltpu.roll(e1, 32, 1))


def finish_kernel(pieces, fine_out, coarse_out):
    _, lane = iotas((8, 128))
    for t in range(2):
        for c in range(4):
            a, b = pieces[2 * c, t], pieces[2 * c + 1, t]
            span = slice(128 * c, 128 * c + 128)
            fine_out[2 * t, :, span] = jnp.where(lane < 64, a, pltpu.roll(b, 64, 1))
            fine_out[2 * t + 1, :, span] = jnp.where(lane < 64, pltpu.roll(a, 64, 1), b)
    total = pieces[0, 2]
    for j in range(1, RING):
        total = total + pieces[j, 2]
    coarse_out[0] = total[:2]


def cycle(rhs, alpha, beta_x, beta_y, beta_z):
    rings, count_y = lax.axis_size("ring"), lax.axis_size("gy")

    (own,) = call(to_windows_kernel, [(RING, 5, 4, 8, 128)], copied=True)(rhs, alpha, beta_x, beta_y, beta_z)
    own = lax.all_to_all(own, "place", 0, 0, tiled=True)
    to_low, to_high, first_by = call(
        x_messages_kernel, [(41, 8, 128), (40, 8, 128), (32, 128)]
    )(own)
    x_low, x_high = shifted(to_high, "ring", 1), shifted(to_low, "ring", -1)
    y_low, y_high = shifted(own, "gy", 1), shifted(own, "gy", -1)
    beyond_y = shifted(first_by, "gy", -2)
    to_low, to_high = call(
        corner_messages_kernel, [(60, 8, 128), (60, 8, 128)]
    )(x_low, x_high)
    corner_low = shifted(to_high, "gy", 1)
    corner_high = shifted(to_low, "gy", -1)
    fine, mid_first, mid_last, mid_own = call(
        fine_kernel,
        [(2, 16, 8, 128), (2, 5, 8, 128), (2, 5, 8, 128), (4, 2, 8, 128)],
        [(17, 24, 24, 128), (26, 24, 128), (26, 24, 128)],
    )(own, x_low, x_high, y_low, y_high, corner_low, corner_high, beyond_y)

    low, high = shifted(mid_last, "ring", 1), shifted(mid_first, "ring", -1)
    near, far = call(
        mid_message_kernel, [(8, 5, 8, 128), (6, 5, 8, 128)]
    )(low, mid_first, mid_last, high)
    level, low = call(
        mid_kernel,
        [(2, 8, 8, 128), (rings * count_y, 5, 2, 128)],
        [(17, 16, 24, 128), (18, 24, 128), (18, 24, 128)],
    )(
        near, shifted(near, "gy", 1), shifted(near, "gy", -1),
        shifted(far, "gy", 2), shifted(far, "gy", -2), mid_own,
    )

    low = lax.all_to_all(low, ("ring", "gy"), 0, 0, tiled=True)
    (own,) = call(whole_y_kernel, [(rings, 160, 128)])(low)
    (pieces,) = call(
        lambda *refs: coarse_kernel(8, *refs),
        [(RING, 3, 8, 128)],
        [(17, 8, 32, 128), (10, 32, 128), (10, 32, 128)],
    )(shifted(own, "place", 1), own, shifted(own, "place", -1), level, fine)
    pieces = lax.all_to_all(pieces, "place", 0, 0, tiled=True)
    fine_solution, coarse = call(finish_kernel, [rhs.shape, (1, 2, 128)])(pieces)
    return fine_solution, coarse


def solution(mesh):
    count_x, count_y = mesh.devices.shape
    devices = np.array(mesh.devices).reshape(count_x // RING, RING, count_y)
    split = Mesh(devices, ("ring", "place", "gy"))
    placed = P(("ring", "place"), "gy", None)
    return jax.shard_map(
        cycle,
        mesh=split,
        in_specs=(placed,) * 5,
        out_specs=(placed, placed),
        check_vma=False,
    )
```

```python
import jax
import jax.numpy as jnp
import numpy as np
from jax import lax
from jax.experimental import pallas as pl
from jax.experimental.pallas import tpu as pltpu
from jax.sharding import Mesh
from jax.sharding import PartitionSpec as P

F32 = jnp.float32
RHS, ALPHA, BX, BY, BZ = range(5)
VMEM_BYTES = 20 * 2**20
ALL_VMEM = 62 * 2**20
RING = 8


def shifted(values, name, steps):
    count = lax.axis_size(name)
    lead, last = max(0, -steps), min(count, count - steps)
    return lax.ppermute(values, name, [(i, i + steps) for i in range(lead, last)])


def call(kernel, outs, scratch=(), copied=False):
    def run(*args):
        space = pltpu.HBM if copied else pltpu.VMEM
        buffers = [pltpu.VMEM(a.shape, F32) for a in args] if copied else []
        sems = [pltpu.SemaphoreType.DMA] * len(args) if copied else []
        return pl.pallas_call(
            kernel,
            out_shape=[jax.ShapeDtypeStruct(s, F32) for s in outs],
            in_specs=[pl.BlockSpec(memory_space=space)] * len(args),
            out_specs=[pl.BlockSpec(memory_space=pltpu.VMEM)] * len(outs),
            scratch_shapes=[pltpu.VMEM(s, F32) for s in scratch] + buffers + sems,
            compiler_params=pltpu.CompilerParams(vmem_limit_bytes=ALL_VMEM if copied else VMEM_BYTES),
        )(*args)

    return run


def iotas(shape):
    return lax.broadcasted_iota(jnp.int32, shape, 0), lax.broadcasted_iota(jnp.int32, shape, 1)


def even_mask(shape):
    row, lane = iotas(shape)
    return ((row + lane) & 1) == 0


def half(x):
    return pltpu.roll(x, 4, 0)


def prev_row(x):
    return pltpu.roll(x, 1, 0)


def next_row(x):
    return pltpu.roll(x, x.shape[0] - 1, 0)


def prev_lane(x):
    return pltpu.roll(x, 1, 1)


def next_lane(x):
    return pltpu.roll(x, x.shape[1] - 1, 1)


def exact_dot(a, b):
    return jnp.dot(a, b, precision=lax.Precision.HIGHEST, preferred_element_type=F32)


def one_hot(shape, test):
    row, col = iotas(shape)
    return jnp.where(test(row, col), 1.0, 0.0).astype(F32)


def low_rows(shape):
    row, _ = iotas(shape)
    return (row & 7) < 4


def inverse_of(diagonal, cell):
    inside = cell > 0.0
    return jnp.where(inside, 1.0 / jnp.where(inside, diagonal, 1.0), 0.0)


def halves(q0, e0, e1):
    return jnp.where(q0, e0, e1), jnp.where(q0, e1, e0)


def clear_guards(r, b, n):
    for ref in (r, b):
        ref[0] = jnp.zeros_like(ref[0])
        ref[n + 1] = jnp.zeros_like(ref[n + 1])


S_R, S_B, WP, WO_R, WO_B, YM_R, YM_B, YP_R, YP_B, ZM_R, ZM_B, ZP_R, ZP_B, I_R, I_B, D_R, D_B = range(17)


def beside(co, src, p, red, q0):
    v = src[p + 1]
    before, after = src[p], src[p + 2]
    other = jnp.where(q0, before, after) if red else jnp.where(q0, after, before)
    wo, ym, yp, zm, zp = (
        (WO_R, YM_R, YP_R, ZM_R, ZP_R) if red else (WO_B, YM_B, YP_B, ZM_B, ZP_B)
    )
    total = co[WP, p] * v + co[wo, p] * other
    total = total + (co[ym, p] * prev_row(v) + co[yp, p] * next_row(v))
    return total + (co[zm, p] * prev_lane(v) + co[zp, p] * next_lane(v))


def relax(co, dst, src, pairs, red, q0):
    s, inv = (S_R, I_R) if red else (S_B, I_B)
    for p in pairs:
        dst[p + 1] = (co[s, p] + beside(co, src, p, red, q0)) * co[inv, p]


def first_red(co, dst, pairs):
    for p in pairs:
        dst[p + 1] = co[S_R, p] * co[I_R, p]


def residual(co, r, b, p, q0):
    red = co[S_R, p] - (co[D_R, p] * r[p + 1] - beside(co, b, p, True, q0))
    black = co[S_B, p] - (co[D_B, p] * b[p + 1] - beside(co, r, p, False, q0))
    return red, black


def put_faces(co, p, q0, bx, by, bz):
    b0, b1, b2 = bx
    wo_r, wo_b = halves(q0, b0, b2)
    y_r, y_b = halves(q0, *by)
    z_r, z_b = halves(q0, *bz)
    yp_r, yp_b = next_row(y_b), next_row(y_r)
    zp_r, zp_b = next_lane(z_b), next_lane(z_r)
    co[WP, p], co[WO_R, p], co[WO_B, p] = b1, wo_r, wo_b
    co[YM_R, p], co[YM_B, p], co[YP_R, p], co[YP_B, p] = y_r, y_b, yp_r, yp_b
    co[ZM_R, p], co[ZM_B, p], co[ZP_R, p], co[ZP_B, p] = z_r, z_b, zp_r, zp_b
    return (b1 + wo_r, b1 + wo_b), (y_r, y_b), (yp_r, yp_b), (z_r + zp_r, z_b + zp_b)


def smooth_cone(co, r, b, own, halo, q0):
    def pairs(reach):
        extra = min(halo, (reach + 1) // 2)
        return range(halo - extra, halo + own + extra)

    first_red(co, r, pairs(8))
    for step in range(2, 9):
        red = step % 2 == 1
        relax(co, r if red else b, b if red else r, pairs(9 - step), red, q0)


def to_windows_kernel(*refs):
    args, out, buffers, sems = refs[:5], refs[5], refs[6:11], refs[11:]
    copies = [pltpu.make_async_copy(*c) for c in zip(args, buffers, sems)]
    for c in copies:
        c.start()
    _, lane = iotas((8, 128))
    zero = jnp.zeros((8, 128), F32)
    for a, ref in enumerate(buffers):
        copies[a].wait()
        for x in range(4):
            tiles = [ref[x, :, 128 * c : 128 * c + 128] for c in range(4)]
            up = [pltpu.roll(t, 32, 1) for t in tiles]
            down = [pltpu.roll(t, 96, 1) for t in tiles]
            for c in range(4):
                out[2 * c, a, x] = jnp.where(lane < 32, up[c - 1] if c else zero, up[c])
                out[2 * c + 1, a, x] = jnp.where(lane < 96, down[c], down[c + 1] if c < 3 else zero)


def flat(s, a, x):
    return (s * 5 + a) * 4 + x


def x_messages_kernel(own, to_low, to_high, first_by):
    for a in range(5):
        for x in range(4):
            for s in range(2):
                to_low[flat(s, a, x)] = own[s, a, x]
                to_high[flat(s, a, x)] = own[6 + s, a, x]
    to_low[40] = own[2, BX, 0]
    for x in range(32):
        first_by[x : x + 1] = own[x // 4, BY, x % 4][:1]


def corner_messages_kernel(low, high, to_low, to_high):
    keep = low_rows((8, 128))
    for a in range(5):
        for x in range(4):
            for ref in (to_low, to_high):
                ref[flat(0, a, x)] = low[flat(1, a, x)]
                ref[flat(1, a, x)] = high[flat(0, a, x)]
            outer_low, outer_high = low[flat(0, a, x)], high[flat(1, a, x)]
            to_low[flat(2, a, x)] = jnp.where(keep, outer_low, half(outer_high))
            to_high[flat(2, a, x)] = jnp.where(keep, half(outer_low), outer_high)


def fine_kernel(
    own, x_low, x_high, y_low, y_high, corner_low, corner_high, beyond_y,
    fine_out, mid_out, mid_first, mid_last, own_out, co, r, b,
):
    q0 = even_mask((24, 128))
    row, lane = iotas((24, 128))
    clear_guards(r, b, 24)
    zero = jnp.zeros((8, 128), F32)

    def plane(a, x):
        block, i = x // 4, x % 4
        if 2 <= block < 10:
            tiles = [ref[block - 2, a, i] for ref in (own, y_high, y_low)]
        elif block in (1, 10):
            side = int(block == 10)
            tiles = [(x_high if side else x_low)[flat(1 - side, a, i)]]
            tiles += [ref[flat(side, a, i)] for ref in (corner_high, corner_low)]
        else:
            up, down = corner_high[flat(2, a, i)], corner_low[flat(2, a, i)]
            if block == 0:
                tiles = [x_low[flat(0, a, i)], up, half(down)]
            else:
                tiles = [x_high[flat(1, a, i)], half(up), down]
        return jnp.concatenate(tiles, 0)

    bx0 = plane(BX, 0)
    for p in range(24):
        x = 2 * p
        co[S_R, p], co[S_B, p] = halves(q0, plane(RHS, x), plane(RHS, x + 1))
        bx1 = plane(BX, x + 1)
        bx2 = plane(BX, x + 2) if p < 23 else jnp.concatenate([x_high[40], zero, zero], 0)
        by = plane(BY, x), plane(BY, x + 1)
        bz = plane(BZ, x), plane(BZ, x + 1)
        fx, fy, fyp, fz = put_faces(co, p, q0, (bx0, bx1, bx2), by, bz)
        bx0 = bx2
        yp_r, yp_b = fyp
        if 4 <= p < 20:
            e0, e1 = beyond_y[x - 8 : x - 7], beyond_y[x - 7 : x - 6]
            up_r, up_b = halves(q0[15:16], e0, e1)
            yp_r = jnp.where(row == 15, up_r, yp_r)
            yp_b = jnp.where(row == 15, up_b, yp_b)
            co[YP_R, p], co[YP_B, p] = yp_r, yp_b
        a_r, a_b = halves(q0, plane(ALPHA, x), plane(ALPHA, x + 1))
        d_r = a_r + ((fx[0] + fz[0]) + (fy[0] + yp_r))
        d_b = a_b + ((fx[1] + fz[1]) + (fy[1] + yp_b))
        co[D_R, p], co[D_B, p] = d_r, d_b
        co[I_R, p], co[I_B, p] = inverse_of(d_r, a_r), inverse_of(d_b, a_b)
    smooth_cone(co, r, b, 16, 4, q0)
    sums, alphas, bys, nexts, bxs, bzs = [], [], [], [], [], []
    for j in range(16):
        p = j + 4
        red, black = residual(co, r, b, p, q0)
        sums.append((red + black)[:8])
        fine_out[0, j] = r[p + 1][:8]
        fine_out[1, j] = b[p + 1][:8]
        s, x = j // 2, 2 * (j % 2)
        alphas.append(own[s, ALPHA, x] + own[s, ALPHA, x + 1])
        bys.append(own[s, BY, x] + own[s, BY, x + 1])
        nexts.append(y_high[s, BY, x] + y_high[s, BY, x + 1])
        bzs.append(own[s, BZ, x] + own[s, BZ, x + 1])
        bxs.append(own[s, BX, x])
    bxs.append(x_high[flat(0, BX, 0)])
    z_sum = one_hot((128, 128), lambda i, j: (i >> 1) == j)
    z_even = one_hot((128, 128), lambda i, j: i == 2 * j)
    y_sum = one_hot((64, 128), lambda i, j: (j >> 1) == i)
    y_even = one_hot((64, 128), lambda i, j: j == 2 * i)
    y_next = one_hot((64, 128), lambda i, j: ((i & 3) < 3) & (j == 2 * i + 2))
    y_last = one_hot((64, 128), lambda i, j: ((i & 3) == 3) & (j == 8 * (i >> 2)))
    along = exact_dot(jnp.concatenate(sums + alphas + bys + nexts + bxs, 0), z_sum)
    bz_z = exact_dot(jnp.concatenate(bzs, 0), z_even)
    source = exact_dot(y_sum, along[0:128]) * 0.125
    alpha = exact_dot(y_sum, along[128:256]) * 0.125
    y_lower = exact_dot(y_even, along[256:384]) * 0.0625
    y_upper = (exact_dot(y_next, along[256:384]) + exact_dot(y_last, along[384:512])) * 0.0625
    x_lower = exact_dot(y_sum, along[512:640]) * 0.0625
    x_upper = exact_dot(y_sum, along[520:648]) * 0.0625
    z_lower = exact_dot(y_sum, bz_z) * 0.0625
    z_upper = next_lane(z_lower)
    diagonal = alpha + ((x_lower + x_upper) + (y_lower + y_upper) + (z_lower + z_upper))
    arrays = (source, inverse_of(diagonal, alpha), x_lower, y_lower, z_lower)
    _, lane = iotas((8, 128))

    def tile(value, t):
        return jnp.where(lane < 64, value[16 * t : 16 * t + 8], pltpu.roll(value[16 * t + 8 : 16 * t + 16], 64, 1))

    for t in range(4):
        for a, value in enumerate(arrays):
            mid_out[t, a] = tile(value, t)
            (mid_first if t < 2 else mid_last)[t % 2, a] = mid_out[t, a]
        own_out[t, 0] = tile(diagonal, t)
        own_out[t, 1] = tile(alpha, t)


def mid_corners_kernel(low1, high1, low2, high2, to_low, to_high):
    for out, first, inner in ((to_low, 0, 0), (to_high, 2, 3)):
        for t in range(2):
            out[t] = high1[first + t]
            out[2 + t] = low1[first + t]
        out[4] = high2[inner]
        out[5] = low2[inner]


def mid_kernel(
    mine, x_low, x_high, low1, high1, low2, high2, corner_low, corner_high, own,
    level_out, low_out, co, r, b,
):
    q0 = even_mask((24, 128))
    _, lane = iotas((8, 128))
    keep = low_rows((8, 128))
    zero = jnp.zeros((8, 128), F32)
    clear_guards(r, b, 16)

    def part(tile, p):
        return jnp.where(lane < 64, pltpu.roll(tile, 64, 1) if p % 2 else tile, 0.0)

    def tiles(t, a):
        if 2 <= t < 6:
            return [ref[t - 2, a] for ref in (mine, high1, low1, high2, low2)]
        x, corner, s = (x_low, corner_low, t) if t < 2 else (x_high, corner_high, t - 6)
        far = [corner[4, a], corner[5, a]] if t in (1, 6) else [zero, zero]
        return [x[s, a], corner[s, a], corner[2 + s, a]] + far

    def planes(p, a):
        c, h1, w1, h2, w2 = (part(value, p) for value in tiles(p // 2, a))
        e0 = [jnp.where(keep, c, half(h1)), jnp.where(keep, h2, 0.0), jnp.where(keep, w2, half(w1))]
        e1 = [jnp.where(keep, half(c), h1), jnp.where(keep, half(h2), 0.0), jnp.where(keep, half(w2), w1)]
        return jnp.concatenate(e0, 0), jnp.concatenate(e1, 0)

    bx0, bx1 = planes(0, 2)
    for p in range(16):
        co[S_R, p], co[S_B, p] = halves(q0, *planes(p, 0))
        co[I_R, p], co[I_B, p] = halves(q0, *planes(p, 1))
        n0, n1 = planes(p + 1, 2) if p < 15 else (jnp.zeros_like(bx0), bx1)
        put_faces(co, p, q0, (bx0, bx1, n0), planes(p, 3), planes(p, 4))
        bx0, bx1 = n0, n1
        if 4 <= p < 12:
            d = part(own[p // 2 - 2, 0], p)
            d = jnp.concatenate([d, d, d], 0), jnp.concatenate([half(d)] * 3, 0)
            co[D_R, p], co[D_B, p] = halves(q0, *d)
    smooth_cone(co, r, b, 8, 4, q0)
    sums = jnp.zeros((32, 128), F32)
    bz_z = zero
    for k in range(8):
        p = k + 4
        red, black = residual(co, r, b, p, q0)
        level_out[0, k] = r[p + 1][:8]
        level_out[1, k] = b[p + 1][:8]
        mid = [part(mine[p // 2 - 2, a], p) for a in (2, 3, 4)]
        stack = jnp.concatenate([(red + black)[:8], part(own[p // 2 - 2, 1], p), mid[0], mid[1]], 0)
        sums += exact_dot(stack, one_hot((128, 128), lambda i, j: ((i >> 1) == j - 16 * k + 8) & ((j >> 4) == k)))
        bz_z += exact_dot(mid[2], one_hot((128, 128), lambda i, j: (i == 2 * (j - 16 * k + 8)) & ((j >> 4) == k)))

    def rows(out_row, test):
        return one_hot((16, 8), lambda i, j: ((i >> 1) == out_row) & test(i & 1, j))

    total = exact_dot(rows(0, lambda i, j: (j < 4) & ((j >> 1) == i)), sums[0:8]) * 0.125
    total += exact_dot(rows(1, lambda i, j: ((j & 3) >> 1) == i), sums[8:16]) * 0.125
    total += exact_dot(rows(2, lambda i, j: (j < 4) & ((j >> 1) == i)), sums[16:24]) * 0.0625
    total += exact_dot(rows(3, lambda i, j: (j & 3) == 2 * i), sums[24:32]) * 0.0625
    total += exact_dot(rows(4, lambda i, j: ((j & 3) >> 1) == i), bz_z) * 0.0625
    for k in range(5):
        mine = total[2 * k : 2 * k + 2]
        for j in range(low_out.shape[0]):
            low_out[j, k] = mine


def whole_y_kernel(gathered, out):
    for g in range(out.shape[0]):
        for j in range(16):
            for k in range(5):
                out[g, 32 * k + 2 * j : 32 * k + 2 * j + 2] = gathered[16 * g + j, k]


def coarse_kernel(sweeps, low, own, high, level, fine, out, co, r, b, planes):
    shape = (32, 128)
    q0 = even_mask(shape)
    row, lane = iotas(shape)
    r[...] = jnp.zeros_like(r)
    b[...] = jnp.zeros_like(b)

    place_of = lane >> 4
    for a in range(5):
        for g in range(2):
            pieces = []
            for side in range(2):
                for s, ref in enumerate((low, own, high)):
                    block = ref[g + 2 * side, 32 * a : 32 * a + 32]
                    offset = 4 * side + s
                    pieces.append((offset, pltpu.roll(block, 16 * offset, 1) if offset else block))
            for k in range(8):
                total = jnp.zeros(shape, F32)
                for offset, piece in pieces:
                    total = jnp.where(place_of == (k + offset) % 8, piece, total)
                planes[a, 8 * g + k] = pltpu.roll(total, 128 - 16 * k, 1) if k else total

    def plane(a, i):
        return planes[a, i]

    first_bx = plane(2, 0)
    bx0 = first_bx
    for p in range(8):
        x = 2 * p
        co[S_R, p], co[S_B, p] = halves(q0, plane(0, x), plane(0, x + 1))
        bx1 = plane(2, x + 1)
        bx2 = plane(2, x + 2) if p < 7 else jnp.where(lane < 64, pltpu.roll(first_bx, 64, 1), 0.0)
        by, bz = (plane(3, x), plane(3, x + 1)), (plane(4, x), plane(4, x + 1))
        fx, fy, fyp, fz = put_faces(co, p, q0, (bx0, bx1, bx2), by, bz)
        bx0 = bx2
        yp_r, yp_b = jnp.where(row == 31, 0.0, fyp[0]), jnp.where(row == 31, 0.0, fyp[1])
        co[YP_R, p], co[YP_B, p] = yp_r, yp_b
        co[YM_R, p], co[YM_B, p] = jnp.where(row == 0, 0.0, fy[0]), jnp.where(row == 0, 0.0, fy[1])
        a_r, a_b = halves(q0, plane(1, x), plane(1, x + 1))
        d_r = a_r + ((fx[0] + fz[0]) + (fy[0] + yp_r))
        d_b = a_b + ((fx[1] + fz[1]) + (fy[1] + yp_b))
        co[I_R, p], co[I_B, p] = inverse_of(d_r, a_r), inverse_of(d_b, a_b)

    def join(ref):
        ref[0] = jnp.where(lane < 64, 0.0, pltpu.roll(ref[8], 64, 1))
        ref[9] = jnp.where(lane < 64, pltpu.roll(ref[1], 64, 1), 0.0)

    def sweep(step, carry):
        relax(co, r, b, range(8), True, q0)
        join(r)
        relax(co, b, r, range(8), False, q0)
        join(b)
        return carry

    lax.fori_loop(0, sweeps, sweep, 0)

    gy, ring, place = (lax.axis_index(name) for name in ("gy", "ring", "place"))
    side, base = ring // 2, 4 * lax.rem(ring, 2)
    parts = []
    for k in range(8):
        red, black = r[base + k // 2 + 1], b[base + k // 2 + 1]
        value = jnp.where(q0, red, black) if k % 2 == 0 else jnp.where(q0, black, red)
        value = pltpu.roll(value, lax.rem(32 - 2 * gy, 32), 0)
        parts.append(pltpu.roll(value, 64 * side, 1)[:8])
    q0 = even_mask((8, 128))
    row, lane = iotas((8, 128))
    up = exact_dot(jnp.concatenate(parts, 0), one_hot((128, 128), lambda i, j: (j >> 1) + 8 == i))
    spread = one_hot((64, 64), lambda i, j: ((i >> 3) == (j >> 3)) & (((i & 3) >> 1) == (j & 7)))
    up = exact_dot(spread, up)
    mid = []
    for k in range(8):
        add = up[8 * k : 8 * k + 8]
        mid.extend(halves(q0, level[0, k] + add, level[1, k] + add))
        mine = pltpu.roll(parts[k], lax.rem(16 * place + 112, 128), 1)
        out[k, 2] = jnp.where(((lane >> 4) == place) & (row < 2), mine, 0.0)
    wide = exact_dot(jnp.concatenate(mid, 0), one_hot((128, 128), lambda i, j: (j >> 1) == i))
    spread = one_hot((128, 128), lambda i, j: ((i >> 3) == (j >> 3)) & (((i & 7) >> 1) == (j & 7)))
    wide = exact_dot(spread, wide)
    for j in range(16):
        add = wide[8 * j : 8 * j + 8]
        e0, e1 = halves(q0, fine[0, j] + add, fine[1, j] + add)
        out[j // 2, j % 2] = jnp.where(lane < 64, pltpu.roll(e0, 96, 1), pltpu.roll(e1, 32, 1))


def finish_kernel(pieces, fine_out, coarse_out):
    _, lane = iotas((8, 128))
    for t in range(2):
        for c in range(4):
            a, b = pieces[2 * c, t], pieces[2 * c + 1, t]
            span = slice(128 * c, 128 * c + 128)
            fine_out[2 * t, :, span] = jnp.where(lane < 64, a, pltpu.roll(b, 64, 1))
            fine_out[2 * t + 1, :, span] = jnp.where(lane < 64, pltpu.roll(a, 64, 1), b)
    total = pieces[0, 2]
    for j in range(1, RING):
        total = total + pieces[j, 2]
    coarse_out[0] = total[:2]


def cycle(rhs, alpha, beta_x, beta_y, beta_z):
    rings, count_y = lax.axis_size("ring"), lax.axis_size("gy")

    (own,) = call(to_windows_kernel, [(RING, 5, 4, 8, 128)], copied=True)(rhs, alpha, beta_x, beta_y, beta_z)
    own = lax.all_to_all(own, "place", 0, 0, tiled=True)
    to_low, to_high, first_by = call(
        x_messages_kernel, [(41, 8, 128), (40, 8, 128), (32, 128)]
    )(own)
    x_low, x_high = shifted(to_high, "ring", 1), shifted(to_low, "ring", -1)
    y_low, y_high = shifted(own, "gy", 1), shifted(own, "gy", -1)
    beyond_y = shifted(first_by, "gy", -2)
    to_low, to_high = call(
        corner_messages_kernel, [(60, 8, 128), (60, 8, 128)]
    )(x_low, x_high)
    corner_low = shifted(to_high, "gy", 1)
    corner_high = shifted(to_low, "gy", -1)
    fine, mid, mid_first, mid_last, mid_own = call(
        fine_kernel,
        [(2, 16, 8, 128), (4, 5, 8, 128), (2, 5, 8, 128), (2, 5, 8, 128), (4, 2, 8, 128)],
        [(17, 24, 24, 128), (26, 24, 128), (26, 24, 128)],
    )(own, x_low, x_high, y_low, y_high, corner_low, corner_high, beyond_y)

    rows = [shifted(mid, "gy", steps) for steps in (1, -1, 2, -2)]
    x_low = shifted(mid_last, "ring", 1)
    x_high = shifted(mid_first, "ring", -1)
    to_low, to_high = call(mid_corners_kernel, [(6, 5, 8, 128), (6, 5, 8, 128)])(*rows)
    corner_low = shifted(to_high, "ring", 1)
    corner_high = shifted(to_low, "ring", -1)
    level, low = call(
        mid_kernel,
        [(2, 8, 8, 128), (rings * count_y, 5, 2, 128)],
        [(17, 16, 24, 128), (18, 24, 128), (18, 24, 128)],
    )(mid, x_low, x_high, *rows, corner_low, corner_high, mid_own)

    low = lax.all_to_all(low, ("ring", "gy"), 0, 0, tiled=True)
    (own,) = call(whole_y_kernel, [(rings, 160, 128)])(low)
    (pieces,) = call(
        lambda *refs: coarse_kernel(8, *refs),
        [(RING, 3, 8, 128)],
        [(17, 8, 32, 128), (10, 32, 128), (10, 32, 128), (5, 16, 32, 128)],
    )(shifted(own, "place", 1), own, shifted(own, "place", -1), level, fine)
    pieces = lax.all_to_all(pieces, "place", 0, 0, tiled=True)
    fine_solution, coarse = call(finish_kernel, [rhs.shape, (1, 2, 128)])(pieces)
    return fine_solution, coarse


def solution(mesh):
    count_x, count_y = mesh.devices.shape
    devices = np.array(mesh.devices).reshape(count_x // RING, RING, count_y)
    split = Mesh(devices, ("ring", "place", "gy"))
    placed = P(("ring", "place"), "gy", None)
    return jax.shard_map(
        cycle,
        mesh=split,
        in_specs=(placed,) * 5,
        out_specs=(placed, placed),
        check_vma=False,
    )
```

```python
import jax
import jax.numpy as jnp
import numpy as np
from jax import lax
from jax.experimental import pallas as pl
from jax.experimental.pallas import tpu as pltpu
from jax.sharding import Mesh
from jax.sharding import PartitionSpec as P

F32 = jnp.float32
RHS, ALPHA, BX, BY, BZ = range(5)
VMEM_BYTES = 20 * 2**20
ALL_VMEM = 62 * 2**20
RING = 8


def shifted(values, name, steps):
    count = lax.axis_size(name)
    lead, last = max(0, -steps), min(count, count - steps)
    return lax.ppermute(values, name, [(i, i + steps) for i in range(lead, last)])


def call(kernel, outs, scratch=(), copied=False):
    def run(*args):
        space = pltpu.HBM if copied else pltpu.VMEM
        buffers = [pltpu.VMEM(a.shape, F32) for a in args] if copied else []
        sems = [pltpu.SemaphoreType.DMA] * len(args) if copied else []
        return pl.pallas_call(
            kernel,
            out_shape=[jax.ShapeDtypeStruct(s, F32) for s in outs],
            in_specs=[pl.BlockSpec(memory_space=space)] * len(args),
            out_specs=[pl.BlockSpec(memory_space=pltpu.VMEM)] * len(outs),
            scratch_shapes=[pltpu.VMEM(s, F32) for s in scratch] + buffers + sems,
            compiler_params=pltpu.CompilerParams(vmem_limit_bytes=ALL_VMEM if copied else VMEM_BYTES),
        )(*args)

    return run


def iotas(shape):
    return lax.broadcasted_iota(jnp.int32, shape, 0), lax.broadcasted_iota(jnp.int32, shape, 1)


def even_mask(shape):
    row, lane = iotas(shape)
    return ((row + lane) & 1) == 0


def half(x):
    return pltpu.roll(x, 4, 0)


def prev_row(x):
    return pltpu.roll(x, 1, 0)


def next_row(x):
    return pltpu.roll(x, x.shape[0] - 1, 0)


def prev_lane(x):
    return pltpu.roll(x, 1, 1)


def next_lane(x):
    return pltpu.roll(x, x.shape[1] - 1, 1)


def exact_dot(a, b):
    return jnp.dot(a, b, precision=lax.Precision.HIGHEST, preferred_element_type=F32)


def one_hot(shape, test):
    row, col = iotas(shape)
    return jnp.where(test(row, col), 1.0, 0.0).astype(F32)


def low_rows(shape):
    row, _ = iotas(shape)
    return (row & 7) < 4


def inverse_of(diagonal, cell):
    inside = cell > 0.0
    return jnp.where(inside, 1.0 / jnp.where(inside, diagonal, 1.0), 0.0)


def halves(q0, e0, e1):
    return jnp.where(q0, e0, e1), jnp.where(q0, e1, e0)


def clear_guards(r, b, n):
    for ref in (r, b):
        ref[0] = jnp.zeros_like(ref[0])
        ref[n + 1] = jnp.zeros_like(ref[n + 1])


S_R, S_B, WP, WO_R, WO_B, YM_R, YM_B, YP_R, YP_B, ZM_R, ZM_B, ZP_R, ZP_B, I_R, I_B, D_R, D_B = range(17)


def beside(co, src, p, red, q0):
    v = src[p + 1]
    before, after = src[p], src[p + 2]
    other = jnp.where(q0, before, after) if red else jnp.where(q0, after, before)
    wo, ym, yp, zm, zp = (
        (WO_R, YM_R, YP_R, ZM_R, ZP_R) if red else (WO_B, YM_B, YP_B, ZM_B, ZP_B)
    )
    total = co[WP, p] * v + co[wo, p] * other
    total = total + (co[ym, p] * prev_row(v) + co[yp, p] * next_row(v))
    return total + (co[zm, p] * prev_lane(v) + co[zp, p] * next_lane(v))


def relax(co, dst, src, pairs, red, q0):
    s, inv = (S_R, I_R) if red else (S_B, I_B)
    for p in pairs:
        dst[p + 1] = (co[s, p] + beside(co, src, p, red, q0)) * co[inv, p]


def first_red(co, dst, pairs):
    for p in pairs:
        dst[p + 1] = co[S_R, p] * co[I_R, p]


def residual(co, r, b, p, q0):
    red = co[S_R, p] - (co[D_R, p] * r[p + 1] - beside(co, b, p, True, q0))
    black = co[S_B, p] - (co[D_B, p] * b[p + 1] - beside(co, r, p, False, q0))
    return red, black


def put_faces(co, p, q0, bx, by, bz):
    b0, b1, b2 = bx
    wo_r, wo_b = halves(q0, b0, b2)
    y_r, y_b = halves(q0, *by)
    z_r, z_b = halves(q0, *bz)
    yp_r, yp_b = next_row(y_b), next_row(y_r)
    zp_r, zp_b = next_lane(z_b), next_lane(z_r)
    co[WP, p], co[WO_R, p], co[WO_B, p] = b1, wo_r, wo_b
    co[YM_R, p], co[YM_B, p], co[YP_R, p], co[YP_B, p] = y_r, y_b, yp_r, yp_b
    co[ZM_R, p], co[ZM_B, p], co[ZP_R, p], co[ZP_B, p] = z_r, z_b, zp_r, zp_b
    return (b1 + wo_r, b1 + wo_b), (y_r, y_b), (yp_r, yp_b), (z_r + zp_r, z_b + zp_b)


def smooth_cone(co, r, b, own, halo, q0):
    def pairs(reach):
        extra = min(halo, (reach + 1) // 2)
        return range(halo - extra, halo + own + extra)

    first_red(co, r, pairs(8))
    for step in range(2, 9):
        red = step % 2 == 1
        relax(co, r if red else b, b if red else r, pairs(9 - step), red, q0)


def to_windows_kernel(*refs):
    args, out, buffers, sems = refs[:5], refs[5], refs[6:11], refs[11:]
    copies = [pltpu.make_async_copy(*c) for c in zip(args, buffers, sems)]
    for c in copies:
        c.start()
    _, lane = iotas((8, 128))
    zero = jnp.zeros((8, 128), F32)
    for a, ref in enumerate(buffers):
        copies[a].wait()
        for x in range(4):
            tiles = [ref[x, :, 128 * c : 128 * c + 128] for c in range(4)]
            up = [pltpu.roll(t, 32, 1) for t in tiles]
            down = [pltpu.roll(t, 96, 1) for t in tiles]
            for c in range(4):
                out[2 * c, a, x] = jnp.where(lane < 32, up[c - 1] if c else zero, up[c])
                out[2 * c + 1, a, x] = jnp.where(lane < 96, down[c], down[c + 1] if c < 3 else zero)


def flat(s, a, x):
    return (s * 5 + a) * 4 + x


def x_messages_kernel(own, to_low, to_high, first_by):
    for a in range(5):
        for x in range(4):
            for s in range(2):
                to_low[flat(s, a, x)] = own[s, a, x]
                to_high[flat(s, a, x)] = own[6 + s, a, x]
    to_low[40] = own[2, BX, 0]
    for x in range(32):
        first_by[x : x + 1] = own[x // 4, BY, x % 4][:1]


def corner_messages_kernel(low, high, to_low, to_high):
    keep = low_rows((8, 128))
    for a in range(5):
        for x in range(4):
            for ref in (to_low, to_high):
                ref[flat(0, a, x)] = low[flat(1, a, x)]
                ref[flat(1, a, x)] = high[flat(0, a, x)]
            outer_low, outer_high = low[flat(0, a, x)], high[flat(1, a, x)]
            to_low[flat(2, a, x)] = jnp.where(keep, outer_low, half(outer_high))
            to_high[flat(2, a, x)] = jnp.where(keep, half(outer_low), outer_high)


def fine_kernel(
    own, x_low, x_high, y_low, y_high, corner_low, corner_high, beyond_y,
    fine_out, mid_first, mid_last, own_out, co, r, b,
):
    q0 = even_mask((24, 128))
    row, lane = iotas((24, 128))
    clear_guards(r, b, 24)
    zero = jnp.zeros((8, 128), F32)

    def plane(a, x):
        block, i = x // 4, x % 4
        if 2 <= block < 10:
            tiles = [ref[block - 2, a, i] for ref in (own, y_high, y_low)]
        elif block in (1, 10):
            side = int(block == 10)
            tiles = [(x_high if side else x_low)[flat(1 - side, a, i)]]
            tiles += [ref[flat(side, a, i)] for ref in (corner_high, corner_low)]
        else:
            up, down = corner_high[flat(2, a, i)], corner_low[flat(2, a, i)]
            if block == 0:
                tiles = [x_low[flat(0, a, i)], up, half(down)]
            else:
                tiles = [x_high[flat(1, a, i)], half(up), down]
        return jnp.concatenate(tiles, 0)

    bx0 = plane(BX, 0)
    for p in range(24):
        x = 2 * p
        co[S_R, p], co[S_B, p] = halves(q0, plane(RHS, x), plane(RHS, x + 1))
        bx1 = plane(BX, x + 1)
        bx2 = plane(BX, x + 2) if p < 23 else jnp.concatenate([x_high[40], zero, zero], 0)
        by = plane(BY, x), plane(BY, x + 1)
        bz = plane(BZ, x), plane(BZ, x + 1)
        fx, fy, fyp, fz = put_faces(co, p, q0, (bx0, bx1, bx2), by, bz)
        bx0 = bx2
        yp_r, yp_b = fyp
        if 4 <= p < 20:
            e0, e1 = beyond_y[x - 8 : x - 7], beyond_y[x - 7 : x - 6]
            up_r, up_b = halves(q0[15:16], e0, e1)
            yp_r = jnp.where(row == 15, up_r, yp_r)
            yp_b = jnp.where(row == 15, up_b, yp_b)
            co[YP_R, p], co[YP_B, p] = yp_r, yp_b
        a_r, a_b = halves(q0, plane(ALPHA, x), plane(ALPHA, x + 1))
        d_r = a_r + ((fx[0] + fz[0]) + (fy[0] + yp_r))
        d_b = a_b + ((fx[1] + fz[1]) + (fy[1] + yp_b))
        co[D_R, p], co[D_B, p] = d_r, d_b
        co[I_R, p], co[I_B, p] = inverse_of(d_r, a_r), inverse_of(d_b, a_b)
    smooth_cone(co, r, b, 16, 4, q0)
    sums, alphas, bys, nexts, bxs, bzs = [], [], [], [], [], []
    for j in range(16):
        p = j + 4
        red, black = residual(co, r, b, p, q0)
        sums.append((red + black)[:8])
        fine_out[0, j] = r[p + 1][:8]
        fine_out[1, j] = b[p + 1][:8]
        s, x = j // 2, 2 * (j % 2)
        alphas.append(own[s, ALPHA, x] + own[s, ALPHA, x + 1])
        bys.append(own[s, BY, x] + own[s, BY, x + 1])
        nexts.append(y_high[s, BY, x] + y_high[s, BY, x + 1])
        bzs.append(own[s, BZ, x] + own[s, BZ, x + 1])
        bxs.append(own[s, BX, x])
    bxs.append(x_high[flat(0, BX, 0)])
    z_sum = one_hot((128, 128), lambda i, j: (i >> 1) == j)
    z_even = one_hot((128, 128), lambda i, j: i == 2 * j)
    y_sum = one_hot((64, 128), lambda i, j: (j >> 1) == i)
    y_even = one_hot((64, 128), lambda i, j: j == 2 * i)
    y_next = one_hot((64, 128), lambda i, j: ((i & 3) < 3) & (j == 2 * i + 2))
    y_last = one_hot((64, 128), lambda i, j: ((i & 3) == 3) & (j == 8 * (i >> 2)))
    along = exact_dot(jnp.concatenate(sums + alphas + bys + nexts + bxs, 0), z_sum)
    bz_z = exact_dot(jnp.concatenate(bzs, 0), z_even)
    source = exact_dot(y_sum, along[0:128]) * 0.125
    alpha = exact_dot(y_sum, along[128:256]) * 0.125
    y_lower = exact_dot(y_even, along[256:384]) * 0.0625
    y_upper = (exact_dot(y_next, along[256:384]) + exact_dot(y_last, along[384:512])) * 0.0625
    x_lower = exact_dot(y_sum, along[512:640]) * 0.0625
    x_upper = exact_dot(y_sum, along[520:648]) * 0.0625
    z_lower = exact_dot(y_sum, bz_z) * 0.0625
    z_upper = next_lane(z_lower)
    diagonal = alpha + ((x_lower + x_upper) + (y_lower + y_upper) + (z_lower + z_upper))
    arrays = (source, inverse_of(diagonal, alpha), x_lower, y_lower, z_lower)
    _, lane = iotas((8, 128))

    def tile(value, t):
        return jnp.where(lane < 64, value[16 * t : 16 * t + 8], pltpu.roll(value[16 * t + 8 : 16 * t + 16], 64, 1))

    for t in range(4):
        for a, value in enumerate(arrays):
            (mid_first if t < 2 else mid_last)[t % 2, a] = tile(value, t)
        own_out[t, 0] = tile(diagonal, t)
        own_out[t, 1] = tile(alpha, t)


def mid_message_kernel(low, first, last, high, near, far):
    tiles = [ref[s] for ref in (low, first, last, high) for s in range(2)]
    for s in range(8):
        near[s] = tiles[s]
        if 0 < s < 7:
            far[s - 1] = tiles[s]


def mid_kernel(mine, low1, high1, low2, high2, own, level_out, low_out, co, r, b):
    q0 = even_mask((24, 128))
    _, lane = iotas((8, 128))
    keep = low_rows((8, 128))
    zero = jnp.zeros((8, 128), F32)
    clear_guards(r, b, 16)

    def part(tile, p):
        return jnp.where(lane < 64, pltpu.roll(tile, 64, 1) if p % 2 else tile, 0.0)

    def planes(p, a):
        t = p // 2
        c, h1, w1 = part(mine[t, a], p), part(high1[t, a], p), part(low1[t, a], p)
        inner = 0 < t < 7
        h2 = part(high2[t - 1, a], p) if inner else zero
        w2 = part(low2[t - 1, a], p) if inner else zero
        e0 = [jnp.where(keep, c, half(h1)), jnp.where(keep, h2, 0.0), jnp.where(keep, w2, half(w1))]
        e1 = [jnp.where(keep, half(c), h1), jnp.where(keep, half(h2), 0.0), jnp.where(keep, half(w2), w1)]
        return jnp.concatenate(e0, 0), jnp.concatenate(e1, 0)

    bx0, bx1 = planes(0, 2)
    for p in range(16):
        co[S_R, p], co[S_B, p] = halves(q0, *planes(p, 0))
        co[I_R, p], co[I_B, p] = halves(q0, *planes(p, 1))
        n0, n1 = planes(p + 1, 2) if p < 15 else (jnp.zeros_like(bx0), bx1)
        put_faces(co, p, q0, (bx0, bx1, n0), planes(p, 3), planes(p, 4))
        bx0, bx1 = n0, n1
        if 4 <= p < 12:
            d = part(own[p // 2 - 2, 0], p)
            d = jnp.concatenate([d, d, d], 0), jnp.concatenate([half(d)] * 3, 0)
            co[D_R, p], co[D_B, p] = halves(q0, *d)
    smooth_cone(co, r, b, 8, 4, q0)
    sums = jnp.zeros((32, 128), F32)
    bz_z = zero
    for k in range(8):
        p = k + 4
        red, black = residual(co, r, b, p, q0)
        level_out[0, k] = r[p + 1][:8]
        level_out[1, k] = b[p + 1][:8]
        mid = [part(mine[p // 2, a], p) for a in (2, 3, 4)]
        stack = jnp.concatenate([(red + black)[:8], part(own[p // 2 - 2, 1], p), mid[0], mid[1]], 0)
        sums += exact_dot(stack, one_hot((128, 128), lambda i, j: ((i >> 1) == j - 16 * k + 8) & ((j >> 4) == k)))
        bz_z += exact_dot(mid[2], one_hot((128, 128), lambda i, j: (i == 2 * (j - 16 * k + 8)) & ((j >> 4) == k)))

    def rows(out_row, test):
        return one_hot((16, 8), lambda i, j: ((i >> 1) == out_row) & test(i & 1, j))

    total = exact_dot(rows(0, lambda i, j: (j < 4) & ((j >> 1) == i)), sums[0:8]) * 0.125
    total += exact_dot(rows(1, lambda i, j: ((j & 3) >> 1) == i), sums[8:16]) * 0.125
    total += exact_dot(rows(2, lambda i, j: (j < 4) & ((j >> 1) == i)), sums[16:24]) * 0.0625
    total += exact_dot(rows(3, lambda i, j: (j & 3) == 2 * i), sums[24:32]) * 0.0625
    total += exact_dot(rows(4, lambda i, j: ((j & 3) >> 1) == i), bz_z) * 0.0625
    for k in range(5):
        mine = total[2 * k : 2 * k + 2]
        for j in range(low_out.shape[0]):
            low_out[j, k] = mine


def whole_y_kernel(gathered, out):
    for g in range(out.shape[0]):
        for j in range(16):
            for k in range(5):
                out[g, 32 * k + 2 * j : 32 * k + 2 * j + 2] = gathered[16 * g + j, k]


def coarse_kernel(sweeps, low, own, high, level, fine, out, co, r, b, planes):
    shape = (32, 128)
    q0 = even_mask(shape)
    row, lane = iotas(shape)
    r[...] = jnp.zeros_like(r)
    b[...] = jnp.zeros_like(b)

    place_of = lane >> 4
    for a in range(5):
        for g in range(2):
            pieces = []
            for side in range(2):
                for s, ref in enumerate((low, own, high)):
                    block = ref[g + 2 * side, 32 * a : 32 * a + 32]
                    offset = 4 * side + s
                    pieces.append((offset, pltpu.roll(block, 16 * offset, 1) if offset else block))
            for k in range(8):
                total = jnp.zeros(shape, F32)
                for offset, piece in pieces:
                    total = jnp.where(place_of == (k + offset) % 8, piece, total)
                planes[a, 8 * g + k] = pltpu.roll(total, 128 - 16 * k, 1) if k else total

    def plane(a, i):
        return planes[a, i]

    first_bx = plane(2, 0)
    bx0 = first_bx
    for p in range(8):
        x = 2 * p
        co[S_R, p], co[S_B, p] = halves(q0, plane(0, x), plane(0, x + 1))
        bx1 = plane(2, x + 1)
        bx2 = plane(2, x + 2) if p < 7 else jnp.where(lane < 64, pltpu.roll(first_bx, 64, 1), 0.0)
        by, bz = (plane(3, x), plane(3, x + 1)), (plane(4, x), plane(4, x + 1))
        fx, fy, fyp, fz = put_faces(co, p, q0, (bx0, bx1, bx2), by, bz)
        bx0 = bx2
        yp_r, yp_b = jnp.where(row == 31, 0.0, fyp[0]), jnp.where(row == 31, 0.0, fyp[1])
        co[YP_R, p], co[YP_B, p] = yp_r, yp_b
        co[YM_R, p], co[YM_B, p] = jnp.where(row == 0, 0.0, fy[0]), jnp.where(row == 0, 0.0, fy[1])
        a_r, a_b = halves(q0, plane(1, x), plane(1, x + 1))
        d_r = a_r + ((fx[0] + fz[0]) + (fy[0] + yp_r))
        d_b = a_b + ((fx[1] + fz[1]) + (fy[1] + yp_b))
        co[I_R, p], co[I_B, p] = inverse_of(d_r, a_r), inverse_of(d_b, a_b)

    def join(ref):
        ref[0] = jnp.where(lane < 64, 0.0, pltpu.roll(ref[8], 64, 1))
        ref[9] = jnp.where(lane < 64, pltpu.roll(ref[1], 64, 1), 0.0)

    def sweep(step, carry):
        relax(co, r, b, range(8), True, q0)
        join(r)
        relax(co, b, r, range(8), False, q0)
        join(b)
        return carry

    lax.fori_loop(0, sweeps, sweep, 0)

    gy, ring, place = (lax.axis_index(name) for name in ("gy", "ring", "place"))
    side, base = ring // 2, 4 * lax.rem(ring, 2)
    parts = []
    for k in range(8):
        red, black = r[base + k // 2 + 1], b[base + k // 2 + 1]
        value = jnp.where(q0, red, black) if k % 2 == 0 else jnp.where(q0, black, red)
        value = pltpu.roll(value, lax.rem(32 - 2 * gy, 32), 0)
        parts.append(pltpu.roll(value, 64 * side, 1)[:8])
    q0 = even_mask((8, 128))
    row, lane = iotas((8, 128))
    up = exact_dot(jnp.concatenate(parts, 0), one_hot((128, 128), lambda i, j: (j >> 1) + 8 == i))
    spread = one_hot((64, 64), lambda i, j: ((i >> 3) == (j >> 3)) & (((i & 3) >> 1) == (j & 7)))
    up = exact_dot(spread, up)
    mid = []
    for k in range(8):
        add = up[8 * k : 8 * k + 8]
        mid.extend(halves(q0, level[0, k] + add, level[1, k] + add))
        mine = pltpu.roll(parts[k], lax.rem(16 * place + 112, 128), 1)
        out[k, 2] = jnp.where(((lane >> 4) == place) & (row < 2), mine, 0.0)
    wide = exact_dot(jnp.concatenate(mid, 0), one_hot((128, 128), lambda i, j: (j >> 1) == i))
    spread = one_hot((128, 128), lambda i, j: ((i >> 3) == (j >> 3)) & (((i & 7) >> 1) == (j & 7)))
    wide = exact_dot(spread, wide)
    for j in range(16):
        add = wide[8 * j : 8 * j + 8]
        e0, e1 = halves(q0, fine[0, j] + add, fine[1, j] + add)
        out[j // 2, j % 2] = jnp.where(lane < 64, pltpu.roll(e0, 96, 1), pltpu.roll(e1, 32, 1))


def finish_kernel(pieces, fine_out, coarse_out):
    _, lane = iotas((8, 128))
    for t in range(2):
        for c in range(4):
            a, b = pieces[2 * c, t], pieces[2 * c + 1, t]
            span = slice(128 * c, 128 * c + 128)
            fine_out[2 * t, :, span] = jnp.where(lane < 64, a, pltpu.roll(b, 64, 1))
            fine_out[2 * t + 1, :, span] = jnp.where(lane < 64, pltpu.roll(a, 64, 1), b)
    total = pieces[0, 2]
    for j in range(1, RING):
        total = total + pieces[j, 2]
    coarse_out[0] = total[:2]


def cycle(rhs, alpha, beta_x, beta_y, beta_z):
    rings, count_y = lax.axis_size("ring"), lax.axis_size("gy")

    (own,) = call(to_windows_kernel, [(RING, 5, 4, 8, 128)], copied=True)(rhs, alpha, beta_x, beta_y, beta_z)
    own = lax.all_to_all(own, "place", 0, 0, tiled=True)
    to_low, to_high, first_by = call(
        x_messages_kernel, [(41, 8, 128), (40, 8, 128), (32, 128)]
    )(own)
    x_low, x_high = shifted(to_high, "ring", 1), shifted(to_low, "ring", -1)
    y_low, y_high = shifted(own, "gy", 1), shifted(own, "gy", -1)
    beyond_y = shifted(first_by, "gy", -2)
    to_low, to_high = call(
        corner_messages_kernel, [(60, 8, 128), (60, 8, 128)]
    )(x_low, x_high)
    corner_low = shifted(to_high, "gy", 1)
    corner_high = shifted(to_low, "gy", -1)
    fine, mid_first, mid_last, mid_own = call(
        fine_kernel,
        [(2, 16, 8, 128), (2, 5, 8, 128), (2, 5, 8, 128), (4, 2, 8, 128)],
        [(17, 24, 24, 128), (26, 24, 128), (26, 24, 128)],
    )(own, x_low, x_high, y_low, y_high, corner_low, corner_high, beyond_y)

    low, high = shifted(mid_last, "ring", 1), shifted(mid_first, "ring", -1)
    near, far = call(
        mid_message_kernel, [(8, 5, 8, 128), (6, 5, 8, 128)]
    )(low, mid_first, mid_last, high)
    level, low = call(
        mid_kernel,
        [(2, 8, 8, 128), (rings * count_y, 5, 2, 128)],
        [(17, 16, 24, 128), (18, 24, 128), (18, 24, 128)],
    )(
        near, shifted(near, "gy", 1), shifted(near, "gy", -1),
        shifted(far, "gy", 2), shifted(far, "gy", -2), mid_own,
    )

    low = lax.all_to_all(low, ("ring", "gy"), 0, 0, tiled=True)
    (own,) = call(whole_y_kernel, [(rings, 160, 128)])(low)
    (pieces,) = call(
        lambda *refs: coarse_kernel(8, *refs),
        [(RING, 3, 8, 128)],
        [(17, 8, 32, 128), (10, 32, 128), (10, 32, 128), (5, 16, 32, 128)],
    )(shifted(own, "place", 1), own, shifted(own, "place", -1), level, fine)
    pieces = lax.all_to_all(pieces, "place", 0, 0, tiled=True)
    fine_solution, coarse = call(finish_kernel, [rhs.shape, (1, 2, 128)])(pieces)
    return fine_solution, coarse


def solution(mesh):
    count_x, count_y = mesh.devices.shape
    devices = np.array(mesh.devices).reshape(count_x // RING, RING, count_y)
    split = Mesh(devices, ("ring", "place", "gy"))
    placed = P(("ring", "place"), "gy", None)
    return jax.shard_map(
        cycle,
        mesh=split,
        in_specs=(placed,) * 5,
        out_specs=(placed, placed),
        check_vma=False,
    )
```

```python
import jax
import jax.numpy as jnp
import numpy as np
from jax import lax
from jax.experimental import pallas as pl
from jax.experimental.pallas import tpu as pltpu
from jax.sharding import Mesh
from jax.sharding import PartitionSpec as P

F32 = jnp.float32
RHS, ALPHA, BX, BY, BZ = range(5)
VMEM_BYTES = 20 * 2**20
ALL_VMEM = 62 * 2**20
RING = 8


def shifted(values, name, steps):
    count = lax.axis_size(name)
    lead, last = max(0, -steps), min(count, count - steps)
    return lax.ppermute(values, name, [(i, i + steps) for i in range(lead, last)])


def call(kernel, outs, scratch=(), copied=False):
    def run(*args):
        space = pltpu.HBM if copied else pltpu.VMEM
        buffers = [pltpu.VMEM(a.shape, F32) for a in args] if copied else []
        sems = [pltpu.SemaphoreType.DMA] * len(args) if copied else []
        return pl.pallas_call(
            kernel,
            out_shape=[jax.ShapeDtypeStruct(s, F32) for s in outs],
            in_specs=[pl.BlockSpec(memory_space=space)] * len(args),
            out_specs=[pl.BlockSpec(memory_space=pltpu.VMEM)] * len(outs),
            scratch_shapes=[pltpu.VMEM(s, F32) for s in scratch] + buffers + sems,
            compiler_params=pltpu.CompilerParams(vmem_limit_bytes=ALL_VMEM if copied else VMEM_BYTES),
        )(*args)

    return run


def iotas(shape):
    return lax.broadcasted_iota(jnp.int32, shape, 0), lax.broadcasted_iota(jnp.int32, shape, 1)


def even_mask(shape):
    row, lane = iotas(shape)
    return ((row + lane) & 1) == 0


def half(x):
    return pltpu.roll(x, 4, 0)


def prev_row(x):
    return pltpu.roll(x, 1, 0)


def next_row(x):
    return pltpu.roll(x, x.shape[0] - 1, 0)


def prev_lane(x):
    return pltpu.roll(x, 1, 1)


def next_lane(x):
    return pltpu.roll(x, x.shape[1] - 1, 1)


def pick(values, chooser):
    parts, rest = [], values
    for _ in range(3):
        part = rest.astype(jnp.bfloat16)
        parts.append(part)
        rest = rest - part.astype(F32)
    total = jnp.dot(jnp.concatenate(parts, 0), chooser, preferred_element_type=F32)
    n = values.shape[0]
    return (total[2 * n :] + total[n : 2 * n]) + total[:n]


def pick_rows(chooser, values):
    parts, rest = [], values
    for _ in range(3):
        part = rest.astype(jnp.bfloat16)
        parts.append(jnp.dot(chooser, part, preferred_element_type=F32))
        rest = rest - part.astype(F32)
    return (parts[2] + parts[1]) + parts[0]


def one_hot(shape, test):
    row, col = iotas(shape)
    return jnp.where(test(row, col), 1.0, 0.0).astype(jnp.bfloat16)


def low_rows(shape):
    row, _ = iotas(shape)
    return (row & 7) < 4


def inverse_of(diagonal, cell):
    inside = cell > 0.0
    return jnp.where(inside, 1.0 / jnp.where(inside, diagonal, 1.0), 0.0)


def halves(q0, e0, e1):
    return jnp.where(q0, e0, e1), jnp.where(q0, e1, e0)


def clear_guards(r, b, n):
    for ref in (r, b):
        ref[0] = jnp.zeros_like(ref[0])
        ref[n + 1] = jnp.zeros_like(ref[n + 1])


S_R, S_B, WP, WO_R, WO_B, YM_R, YM_B, YP_R, YP_B, ZM_R, ZM_B, ZP_R, ZP_B, I_R, I_B, D_R, D_B = range(17)


def beside(co, src, p, red, q0):
    v = src[p + 1]
    before, after = src[p], src[p + 2]
    other = jnp.where(q0, before, after) if red else jnp.where(q0, after, before)
    wo, ym, yp, zm, zp = (
        (WO_R, YM_R, YP_R, ZM_R, ZP_R) if red else (WO_B, YM_B, YP_B, ZM_B, ZP_B)
    )
    total = co[WP, p] * v + co[wo, p] * other
    total = total + (co[ym, p] * prev_row(v) + co[yp, p] * next_row(v))
    return total + (co[zm, p] * prev_lane(v) + co[zp, p] * next_lane(v))


def relax(co, dst, src, pairs, red, q0):
    s, inv = (S_R, I_R) if red else (S_B, I_B)
    for p in pairs:
        dst[p + 1] = (co[s, p] + beside(co, src, p, red, q0)) * co[inv, p]


def first_red(co, dst, pairs):
    for p in pairs:
        dst[p + 1] = co[S_R, p] * co[I_R, p]


def residual(co, r, b, p, q0):
    red = co[S_R, p] - (co[D_R, p] * r[p + 1] - beside(co, b, p, True, q0))
    black = co[S_B, p] - (co[D_B, p] * b[p + 1] - beside(co, r, p, False, q0))
    return red, black


def put_faces(co, p, q0, bx, by, bz):
    b0, b1, b2 = bx
    wo_r, wo_b = halves(q0, b0, b2)
    y_r, y_b = halves(q0, *by)
    z_r, z_b = halves(q0, *bz)
    yp_r, yp_b = next_row(y_b), next_row(y_r)
    zp_r, zp_b = next_lane(z_b), next_lane(z_r)
    co[WP, p], co[WO_R, p], co[WO_B, p] = b1, wo_r, wo_b
    co[YM_R, p], co[YM_B, p], co[YP_R, p], co[YP_B, p] = y_r, y_b, yp_r, yp_b
    co[ZM_R, p], co[ZM_B, p], co[ZP_R, p], co[ZP_B, p] = z_r, z_b, zp_r, zp_b
    return (b1 + wo_r, b1 + wo_b), (y_r, y_b), (yp_r, yp_b), (z_r + zp_r, z_b + zp_b)


def smooth_cone(co, r, b, own, halo, q0):
    def pairs(reach):
        extra = min(halo, (reach + 1) // 2)
        return range(halo - extra, halo + own + extra)

    first_red(co, r, pairs(8))
    for step in range(2, 9):
        red = step % 2 == 1
        relax(co, r if red else b, b if red else r, pairs(9 - step), red, q0)


def to_windows_kernel(*refs):
    args, out, buffers, sems = refs[:5], refs[5], refs[6:11], refs[11:]
    copies = [pltpu.make_async_copy(*c) for c in zip(args, buffers, sems)]
    for c in copies:
        c.start()
    _, lane = iotas((8, 128))
    zero = jnp.zeros((8, 128), F32)
    for a, ref in enumerate(buffers):
        copies[a].wait()
        for x in range(4):
            tiles = [ref[x, :, 128 * c : 128 * c + 128] for c in range(4)]
            up = [pltpu.roll(t, 32, 1) for t in tiles]
            down = [pltpu.roll(t, 96, 1) for t in tiles]
            for c in range(4):
                out[2 * c, a, x] = jnp.where(lane < 32, up[c - 1] if c else zero, up[c])
                out[2 * c + 1, a, x] = jnp.where(lane < 96, down[c], down[c + 1] if c < 3 else zero)


def flat(s, a, x):
    return (s * 5 + a) * 4 + x


def x_messages_kernel(own, to_low, to_high, first_by):
    for a in range(5):
        for x in range(4):
            for s in range(2):
                to_low[flat(s, a, x)] = own[s, a, x]
                to_high[flat(s, a, x)] = own[6 + s, a, x]
    to_low[40] = own[2, BX, 0]
    for x in range(32):
        first_by[x : x + 1] = own[x // 4, BY, x % 4][:1]


def corner_messages_kernel(low, high, to_low, to_high):
    keep = low_rows((8, 128))
    for a in range(5):
        for x in range(4):
            for ref in (to_low, to_high):
                ref[flat(0, a, x)] = low[flat(1, a, x)]
                ref[flat(1, a, x)] = high[flat(0, a, x)]
            outer_low, outer_high = low[flat(0, a, x)], high[flat(1, a, x)]
            to_low[flat(2, a, x)] = jnp.where(keep, outer_low, half(outer_high))
            to_high[flat(2, a, x)] = jnp.where(keep, half(outer_low), outer_high)


def fine_kernel(
    own, x_low, x_high, y_low, y_high, corner_low, corner_high, beyond_y, mid_coefs,
    fine_out, mid_first, mid_last, co, r, b,
):
    q0 = even_mask((24, 128))
    row, _ = iotas((24, 128))
    clear_guards(r, b, 24)
    zero = jnp.zeros((8, 128), F32)

    def plane(a, x):
        block, i = x // 4, x % 4
        if 2 <= block < 10:
            tiles = [ref[block - 2, a, i] for ref in (own, y_high, y_low)]
        elif block in (1, 10):
            side = int(block == 10)
            tiles = [(x_high if side else x_low)[flat(1 - side, a, i)]]
            tiles += [ref[flat(side, a, i)] for ref in (corner_high, corner_low)]
        else:
            up, down = corner_high[flat(2, a, i)], corner_low[flat(2, a, i)]
            if block == 0:
                tiles = [x_low[flat(0, a, i)], up, half(down)]
            else:
                tiles = [x_high[flat(1, a, i)], half(up), down]
        return jnp.concatenate(tiles, 0)

    bx0 = plane(BX, 0)
    for p in range(24):
        x = 2 * p
        co[S_R, p], co[S_B, p] = halves(q0, plane(RHS, x), plane(RHS, x + 1))
        bx1 = plane(BX, x + 1)
        bx2 = plane(BX, x + 2) if p < 23 else jnp.concatenate([x_high[40], zero, zero], 0)
        by = plane(BY, x), plane(BY, x + 1)
        bz = plane(BZ, x), plane(BZ, x + 1)
        fx, fy, fyp, fz = put_faces(co, p, q0, (bx0, bx1, bx2), by, bz)
        bx0 = bx2
        yp_r, yp_b = fyp
        if 4 <= p < 20:
            e0, e1 = beyond_y[x - 8 : x - 7], beyond_y[x - 7 : x - 6]
            up_r, up_b = halves(q0[15:16], e0, e1)
            yp_r = jnp.where(row == 15, up_r, yp_r)
            yp_b = jnp.where(row == 15, up_b, yp_b)
            co[YP_R, p], co[YP_B, p] = yp_r, yp_b
        a_r, a_b = halves(q0, plane(ALPHA, x), plane(ALPHA, x + 1))
        d_r = a_r + ((fx[0] + fz[0]) + (fy[0] + yp_r))
        d_b = a_b + ((fx[1] + fz[1]) + (fy[1] + yp_b))
        co[D_R, p], co[D_B, p] = d_r, d_b
        co[I_R, p], co[I_B, p] = inverse_of(d_r, a_r), inverse_of(d_b, a_b)
    smooth_cone(co, r, b, 16, 4, q0)
    sums = []
    for j in range(16):
        p = j + 4
        red, black = residual(co, r, b, p, q0)
        sums.append((red + black)[:8])
        fine_out[0, j] = r[p + 1][:8]
        fine_out[1, j] = b[p + 1][:8]
    along = pick(jnp.concatenate(sums, 0), one_hot((128, 128), lambda i, j: (i >> 1) == j))
    source = pick_rows(one_hot((64, 128), lambda i, j: (j >> 1) == i), along) * 0.125
    for t in range(4):
        out = mid_first if t < 2 else mid_last
        out[t % 2, 0] = mid_tile(source, t)
        for a in range(4):
            out[t % 2, a + 1] = mid_coefs[t, a]


def mid_tile(value, t):
    _, lane = iotas((8, 128))
    return jnp.where(lane < 64, value[16 * t : 16 * t + 8], pltpu.roll(value[16 * t + 8 : 16 * t + 16], 64, 1))


def low_rows_of(out_row, test):
    return one_hot((16, 8), lambda i, j: ((i >> 1) == out_row) & test(i & 1, j))


def coefficients_kernel(own, x_high, y_high, mid_coefs, mid_own, low_out):
    alphas, bys, nexts, bxs, bzs = [], [], [], [], []
    for j in range(16):
        s, x = j // 2, 2 * (j % 2)
        alphas.append(own[s, ALPHA, x] + own[s, ALPHA, x + 1])
        bys.append(own[s, BY, x] + own[s, BY, x + 1])
        nexts.append(y_high[s, BY, x] + y_high[s, BY, x + 1])
        bzs.append(own[s, BZ, x] + own[s, BZ, x + 1])
        bxs.append(own[s, BX, x])
    bxs.append(x_high[flat(0, BX, 0)])
    along = pick(
        jnp.concatenate(alphas + bys + nexts + bxs, 0), one_hot((128, 128), lambda i, j: (i >> 1) == j)
    )
    bz_z = pick(jnp.concatenate(bzs, 0), one_hot((128, 128), lambda i, j: i == 2 * j))
    y_sum = one_hot((64, 128), lambda i, j: (j >> 1) == i)
    y_even = one_hot((64, 128), lambda i, j: j == 2 * i)
    y_next = one_hot((64, 128), lambda i, j: ((i & 3) < 3) & (j == 2 * i + 2))
    y_last = one_hot((64, 128), lambda i, j: ((i & 3) == 3) & (j == 8 * (i >> 2)))
    alpha = pick_rows(y_sum, along[0:128]) * 0.125
    y_lower = pick_rows(y_even, along[128:256]) * 0.0625
    y_upper = (pick_rows(y_next, along[128:256]) + pick_rows(y_last, along[256:384])) * 0.0625
    x_lower = pick_rows(y_sum, along[384:512]) * 0.0625
    x_upper = pick_rows(y_sum, along[392:520]) * 0.0625
    z_lower = pick_rows(y_sum, bz_z) * 0.0625
    diagonal = alpha + ((x_lower + x_upper) + (y_lower + y_upper) + (z_lower + next_lane(z_lower)))
    sums = jnp.zeros((24, 128), F32)
    low_bz = jnp.zeros((8, 128), F32)
    for t in range(4):
        for a, value in enumerate((inverse_of(diagonal, alpha), x_lower, y_lower, z_lower)):
            mid_coefs[t, a] = mid_tile(value, t)
        mid_own[t] = mid_tile(diagonal, t)
        stack = jnp.concatenate([mid_tile(alpha, t), mid_coefs[t, 1], mid_coefs[t, 2]], 0)

        def chooser(test):
            def to(i, j):
                k = 2 * t + (i >> 6)
                return ((j >> 4) == k) & test(i & 63, j - 16 * k + 8)

            return one_hot((128, 128), to)

        sums += pick(stack, chooser(lambda i, j: (i >> 1) == j))
        low_bz += pick(mid_coefs[t, 3], chooser(lambda i, j: i == 2 * j))
    total = pick_rows(low_rows_of(0, lambda i, j: ((j & 3) >> 1) == i), sums[0:8]) * 0.125
    total += pick_rows(low_rows_of(1, lambda i, j: (j < 4) & ((j >> 1) == i)), sums[8:16]) * 0.0625
    total += pick_rows(low_rows_of(2, lambda i, j: (j & 3) == 2 * i), sums[16:24]) * 0.0625
    total += pick_rows(low_rows_of(3, lambda i, j: ((j & 3) >> 1) == i), low_bz) * 0.0625
    for k in range(4):
        low_out[k] = total[2 * k : 2 * k + 2]


def mid_message_kernel(low, first, last, high, near, far):
    tiles = [ref[s] for ref in (low, first, last, high) for s in range(2)]
    for s in range(8):
        near[s] = tiles[s]
        if 0 < s < 7:
            far[s - 1] = tiles[s]


def mid_kernel(mine, low1, high1, low2, high2, own, low_coefs, level_out, low_out, co, r, b):
    q0 = even_mask((24, 128))
    _, lane = iotas((8, 128))
    keep = low_rows((8, 128))
    zero = jnp.zeros((8, 128), F32)
    clear_guards(r, b, 16)

    def part(tile, p):
        return jnp.where(lane < 64, pltpu.roll(tile, 64, 1) if p % 2 else tile, 0.0)

    def planes(p, a):
        t = p // 2
        c, h1, w1 = part(mine[t, a], p), part(high1[t, a], p), part(low1[t, a], p)
        inner = 0 < t < 7
        h2 = part(high2[t - 1, a], p) if inner else zero
        w2 = part(low2[t - 1, a], p) if inner else zero
        e0 = [jnp.where(keep, c, half(h1)), jnp.where(keep, h2, 0.0), jnp.where(keep, w2, half(w1))]
        e1 = [jnp.where(keep, half(c), h1), jnp.where(keep, half(h2), 0.0), jnp.where(keep, half(w2), w1)]
        return jnp.concatenate(e0, 0), jnp.concatenate(e1, 0)

    bx0, bx1 = planes(0, 2)
    for p in range(16):
        co[S_R, p], co[S_B, p] = halves(q0, *planes(p, 0))
        co[I_R, p], co[I_B, p] = halves(q0, *planes(p, 1))
        n0, n1 = planes(p + 1, 2) if p < 15 else (jnp.zeros_like(bx0), bx1)
        put_faces(co, p, q0, (bx0, bx1, n0), planes(p, 3), planes(p, 4))
        bx0, bx1 = n0, n1
        if 4 <= p < 12:
            d = part(own[p // 2 - 2], p)
            d = jnp.concatenate([d, d, d], 0), jnp.concatenate([half(d)] * 3, 0)
            co[D_R, p], co[D_B, p] = halves(q0, *d)
    smooth_cone(co, r, b, 8, 4, q0)
    sums = []
    for k in range(8):
        red, black = residual(co, r, b, k + 4, q0)
        level_out[0, k] = r[k + 5][:8]
        level_out[1, k] = b[k + 5][:8]
        sums.append((red + black)[:8])
    along = pick(jnp.concatenate(sums, 0), one_hot((128, 128), lambda i, j: (i >> 1) == j))
    total = zero
    for k in range(8):
        moved = pltpu.roll(along[8 * k : 8 * k + 8], (16 * k - 8) % 128, 1)
        total = jnp.where((lane >> 4) == k, moved, total)
    source = pick_rows(low_rows_of(0, lambda i, j: (j < 4) & ((j >> 1) == i)), total)[:2] * 0.125
    coefs = [low_coefs[k] for k in range(4)]
    for j in range(low_out.shape[0]):
        low_out[j, 0] = source
        for k in range(4):
            low_out[j, k + 1] = coefs[k]


def whole_y_kernel(gathered, out):
    for g in range(out.shape[0]):
        for j in range(16):
            for k in range(5):
                out[g, 32 * k + 2 * j : 32 * k + 2 * j + 2] = gathered[16 * g + j, k]


def coarse_kernel(sweeps, low, own, high, level, fine, out, co, r, b, planes):
    shape = (32, 128)
    q0 = even_mask(shape)
    row, lane = iotas(shape)
    r[...] = jnp.zeros_like(r)
    b[...] = jnp.zeros_like(b)

    place_of = lane >> 4
    for a in range(5):
        for g in range(2):
            pieces = []
            for side in range(2):
                for s, ref in enumerate((low, own, high)):
                    block = ref[g + 2 * side, 32 * a : 32 * a + 32]
                    offset = 4 * side + s
                    pieces.append((offset, pltpu.roll(block, 16 * offset, 1) if offset else block))
            for k in range(8):
                total = jnp.zeros(shape, F32)
                for offset, piece in pieces:
                    total = jnp.where(place_of == (k + offset) % 8, piece, total)
                planes[a, 8 * g + k] = pltpu.roll(total, 128 - 16 * k, 1) if k else total

    def plane(a, i):
        return planes[a, i]

    first_bx = plane(2, 0)
    bx0 = first_bx
    for p in range(8):
        x = 2 * p
        co[S_R, p], co[S_B, p] = halves(q0, plane(0, x), plane(0, x + 1))
        bx1 = plane(2, x + 1)
        bx2 = plane(2, x + 2) if p < 7 else jnp.where(lane < 64, pltpu.roll(first_bx, 64, 1), 0.0)
        by, bz = (plane(3, x), plane(3, x + 1)), (plane(4, x), plane(4, x + 1))
        fx, fy, fyp, fz = put_faces(co, p, q0, (bx0, bx1, bx2), by, bz)
        bx0 = bx2
        yp_r, yp_b = jnp.where(row == 31, 0.0, fyp[0]), jnp.where(row == 31, 0.0, fyp[1])
        co[YP_R, p], co[YP_B, p] = yp_r, yp_b
        co[YM_R, p], co[YM_B, p] = jnp.where(row == 0, 0.0, fy[0]), jnp.where(row == 0, 0.0, fy[1])
        a_r, a_b = halves(q0, plane(1, x), plane(1, x + 1))
        d_r = a_r + ((fx[0] + fz[0]) + (fy[0] + yp_r))
        d_b = a_b + ((fx[1] + fz[1]) + (fy[1] + yp_b))
        co[I_R, p], co[I_B, p] = inverse_of(d_r, a_r), inverse_of(d_b, a_b)

    def join(ref):
        ref[0] = jnp.where(lane < 64, 0.0, pltpu.roll(ref[8], 64, 1))
        ref[9] = jnp.where(lane < 64, pltpu.roll(ref[1], 64, 1), 0.0)

    def sweep(step, carry):
        relax(co, r, b, range(8), True, q0)
        join(r)
        relax(co, b, r, range(8), False, q0)
        join(b)
        return carry

    lax.fori_loop(0, sweeps, sweep, 0)

    gy, ring, place = (lax.axis_index(name) for name in ("gy", "ring", "place"))
    side, base = ring // 2, 4 * lax.rem(ring, 2)
    parts = []
    for k in range(8):
        red, black = r[base + k // 2 + 1], b[base + k // 2 + 1]
        value = jnp.where(q0, red, black) if k % 2 == 0 else jnp.where(q0, black, red)
        value = pltpu.roll(value, lax.rem(32 - 2 * gy, 32), 0)
        parts.append(pltpu.roll(value, 64 * side, 1)[:8])
    q0 = even_mask((8, 128))
    row, lane = iotas((8, 128))
    up = pick(jnp.concatenate(parts, 0), one_hot((128, 128), lambda i, j: (j >> 1) + 8 == i))
    spread = one_hot((64, 64), lambda i, j: ((i >> 3) == (j >> 3)) & (((i & 3) >> 1) == (j & 7)))
    up = pick_rows(spread, up)
    mid = []
    for k in range(8):
        add = up[8 * k : 8 * k + 8]
        mid.extend(halves(q0, level[0, k] + add, level[1, k] + add))
        mine = pltpu.roll(parts[k], lax.rem(16 * place + 112, 128), 1)
        out[k, 2] = jnp.where(((lane >> 4) == place) & (row < 2), mine, 0.0)
    wide = pick(jnp.concatenate(mid, 0), one_hot((128, 128), lambda i, j: (j >> 1) == i))
    spread = one_hot((128, 128), lambda i, j: ((i >> 3) == (j >> 3)) & (((i & 7) >> 1) == (j & 7)))
    wide = pick_rows(spread, wide)
    for j in range(16):
        add = wide[8 * j : 8 * j + 8]
        e0, e1 = halves(q0, fine[0, j] + add, fine[1, j] + add)
        out[j // 2, j % 2] = jnp.where(lane < 64, pltpu.roll(e0, 96, 1), pltpu.roll(e1, 32, 1))


def finish_kernel(pieces, fine_out, coarse_out):
    _, lane = iotas((8, 128))
    for t in range(2):
        for c in range(4):
            a, b = pieces[2 * c, t], pieces[2 * c + 1, t]
            span = slice(128 * c, 128 * c + 128)
            fine_out[2 * t, :, span] = jnp.where(lane < 64, a, pltpu.roll(b, 64, 1))
            fine_out[2 * t + 1, :, span] = jnp.where(lane < 64, pltpu.roll(a, 64, 1), b)
    total = pieces[0, 2]
    for j in range(1, RING):
        total = total + pieces[j, 2]
    coarse_out[0] = total[:2]


def cycle(rhs, alpha, beta_x, beta_y, beta_z):
    rings, count_y = lax.axis_size("ring"), lax.axis_size("gy")

    (own,) = call(to_windows_kernel, [(RING, 5, 4, 8, 128)], copied=True)(rhs, alpha, beta_x, beta_y, beta_z)
    own = lax.all_to_all(own, "place", 0, 0, tiled=True)
    to_low, to_high, first_by = call(
        x_messages_kernel, [(41, 8, 128), (40, 8, 128), (32, 128)]
    )(own)
    x_low, x_high = shifted(to_high, "ring", 1), shifted(to_low, "ring", -1)
    y_low, y_high = shifted(own, "gy", 1), shifted(own, "gy", -1)
    beyond_y = shifted(first_by, "gy", -2)
    to_low, to_high = call(
        corner_messages_kernel, [(60, 8, 128), (60, 8, 128)]
    )(x_low, x_high)
    corner_low = shifted(to_high, "gy", 1)
    corner_high = shifted(to_low, "gy", -1)
    mid_coefs, mid_own, low_coefs = call(
        coefficients_kernel, [(4, 4, 8, 128), (4, 8, 128), (4, 2, 128)]
    )(own, x_high, y_high)
    fine, mid_first, mid_last = call(
        fine_kernel,
        [(2, 16, 8, 128), (2, 5, 8, 128), (2, 5, 8, 128)],
        [(17, 24, 24, 128), (26, 24, 128), (26, 24, 128)],
    )(own, x_low, x_high, y_low, y_high, corner_low, corner_high, beyond_y, mid_coefs)

    low, high = shifted(mid_last, "ring", 1), shifted(mid_first, "ring", -1)
    near, far = call(
        mid_message_kernel, [(8, 5, 8, 128), (6, 5, 8, 128)]
    )(low, mid_first, mid_last, high)
    level, low = call(
        mid_kernel,
        [(2, 8, 8, 128), (rings * count_y, 5, 2, 128)],
        [(17, 16, 24, 128), (18, 24, 128), (18, 24, 128)],
    )(
        near, shifted(near, "gy", 1), shifted(near, "gy", -1),
        shifted(far, "gy", 2), shifted(far, "gy", -2), mid_own, low_coefs,
    )

    low = lax.all_to_all(low, ("ring", "gy"), 0, 0, tiled=True)
    (own,) = call(whole_y_kernel, [(rings, 160, 128)])(low)
    (pieces,) = call(
        lambda *refs: coarse_kernel(8, *refs),
        [(RING, 3, 8, 128)],
        [(17, 8, 32, 128), (10, 32, 128), (10, 32, 128), (5, 16, 32, 128)],
    )(shifted(own, "place", 1), own, shifted(own, "place", -1), level, fine)
    pieces = lax.all_to_all(pieces, "place", 0, 0, tiled=True)
    fine_solution, coarse = call(finish_kernel, [rhs.shape, (1, 2, 128)])(pieces)
    return fine_solution, coarse


def solution(mesh):
    count_x, count_y = mesh.devices.shape
    devices = np.array(mesh.devices).reshape(count_x // RING, RING, count_y)
    split = Mesh(devices, ("ring", "place", "gy"))
    placed = P(("ring", "place"), "gy", None)
    return jax.shard_map(
        cycle,
        mesh=split,
        in_specs=(placed,) * 5,
        out_specs=(placed, placed),
        check_vma=False,
    )
```

```python
import jax
import jax.numpy as jnp
import numpy as np
from jax import lax
from jax.experimental import pallas as pl
from jax.experimental.pallas import tpu as pltpu
from jax.sharding import Mesh
from jax.sharding import PartitionSpec as P

F32 = jnp.float32
RHS, ALPHA, BX, BY, BZ = range(5)
VMEM_BYTES = 20 * 2**20
ALL_VMEM = 62 * 2**20
RING = 8


def shifted(values, name, steps):
    count = lax.axis_size(name)
    lead, last = max(0, -steps), min(count, count - steps)
    return lax.ppermute(values, name, [(i, i + steps) for i in range(lead, last)])


def call(kernel, outs, scratch=(), copied=False):
    def run(*args):
        space = pltpu.HBM if copied else pltpu.VMEM
        buffers = [pltpu.VMEM(a.shape, F32) for a in args] if copied else []
        sems = [pltpu.SemaphoreType.DMA] * len(args) if copied else []
        return pl.pallas_call(
            kernel,
            out_shape=[jax.ShapeDtypeStruct(s, F32) for s in outs],
            in_specs=[pl.BlockSpec(memory_space=space)] * len(args),
            out_specs=[pl.BlockSpec(memory_space=pltpu.VMEM)] * len(outs),
            scratch_shapes=[pltpu.VMEM(s, F32) for s in scratch] + buffers + sems,
            compiler_params=pltpu.CompilerParams(vmem_limit_bytes=ALL_VMEM if copied else VMEM_BYTES),
        )(*args)

    return run


def iotas(shape):
    return lax.broadcasted_iota(jnp.int32, shape, 0), lax.broadcasted_iota(jnp.int32, shape, 1)


def even_mask(shape):
    row, lane = iotas(shape)
    return ((row + lane) & 1) == 0


def half(x):
    return pltpu.roll(x, 4, 0)


def prev_row(x):
    return pltpu.roll(x, 1, 0)


def next_row(x):
    return pltpu.roll(x, x.shape[0] - 1, 0)


def prev_lane(x):
    return pltpu.roll(x, 1, 1)


def next_lane(x):
    return pltpu.roll(x, x.shape[1] - 1, 1)


def pick(values, chooser):
    parts, rest = [], values
    for _ in range(3):
        part = rest.astype(jnp.bfloat16)
        parts.append(part)
        rest = rest - part.astype(F32)
    total = jnp.dot(jnp.concatenate(parts, 0), chooser, preferred_element_type=F32)
    n = values.shape[0]
    return (total[2 * n :] + total[n : 2 * n]) + total[:n]


def pick_rows(chooser, values):
    parts, rest = [], values
    for _ in range(3):
        part = rest.astype(jnp.bfloat16)
        parts.append(jnp.dot(chooser, part, preferred_element_type=F32))
        rest = rest - part.astype(F32)
    return (parts[2] + parts[1]) + parts[0]


def one_hot(shape, test):
    row, col = iotas(shape)
    return jnp.where(test(row, col), 1.0, 0.0).astype(jnp.bfloat16)


def low_rows(shape):
    row, _ = iotas(shape)
    return (row & 7) < 4


def inverse_of(diagonal, cell):
    inside = cell > 0.0
    return jnp.where(inside, 1.0 / jnp.where(inside, diagonal, 1.0), 0.0)


def halves(q0, e0, e1):
    return jnp.where(q0, e0, e1), jnp.where(q0, e1, e0)


def clear_guards(r, b, n):
    for ref in (r, b):
        ref[0] = jnp.zeros_like(ref[0])
        ref[n + 1] = jnp.zeros_like(ref[n + 1])


S_R, S_B, WP, WO_R, WO_B, YM_R, YM_B, YP_R, YP_B, ZM_R, ZM_B, ZP_R, ZP_B, I_R, I_B, D_R, D_B = range(17)


def beside(co, src, p, red, q0):
    v = src[p + 1]
    before, after = src[p], src[p + 2]
    other = jnp.where(q0, before, after) if red else jnp.where(q0, after, before)
    wo, ym, yp, zm, zp = (
        (WO_R, YM_R, YP_R, ZM_R, ZP_R) if red else (WO_B, YM_B, YP_B, ZM_B, ZP_B)
    )
    total = co[WP, p] * v + co[wo, p] * other
    total = total + (co[ym, p] * prev_row(v) + co[yp, p] * next_row(v))
    return total + (co[zm, p] * prev_lane(v) + co[zp, p] * next_lane(v))


def relax(co, dst, src, pairs, red, q0):
    s, inv = (S_R, I_R) if red else (S_B, I_B)
    for p in pairs:
        dst[p + 1] = (co[s, p] + beside(co, src, p, red, q0)) * co[inv, p]


def first_red(co, dst, pairs):
    for p in pairs:
        dst[p + 1] = co[S_R, p] * co[I_R, p]


def residual(co, r, b, p, q0):
    red = co[S_R, p] - (co[D_R, p] * r[p + 1] - beside(co, b, p, True, q0))
    black = co[S_B, p] - (co[D_B, p] * b[p + 1] - beside(co, r, p, False, q0))
    return red, black


def put_faces(co, p, q0, bx, by, bz):
    b0, b1, b2 = bx
    wo_r, wo_b = halves(q0, b0, b2)
    y_r, y_b = halves(q0, *by)
    z_r, z_b = halves(q0, *bz)
    yp_r, yp_b = next_row(y_b), next_row(y_r)
    zp_r, zp_b = next_lane(z_b), next_lane(z_r)
    co[WP, p], co[WO_R, p], co[WO_B, p] = b1, wo_r, wo_b
    co[YM_R, p], co[YM_B, p], co[YP_R, p], co[YP_B, p] = y_r, y_b, yp_r, yp_b
    co[ZM_R, p], co[ZM_B, p], co[ZP_R, p], co[ZP_B, p] = z_r, z_b, zp_r, zp_b
    return (b1 + wo_r, b1 + wo_b), (y_r, y_b), (yp_r, yp_b), (z_r + zp_r, z_b + zp_b)


def smooth_cone(co, r, b, own, halo, q0):
    def pairs(reach):
        extra = min(halo, (reach + 1) // 2)
        return range(halo - extra, halo + own + extra)

    first_red(co, r, pairs(8))
    for step in range(2, 9):
        red = step % 2 == 1
        relax(co, r if red else b, b if red else r, pairs(9 - step), red, q0)


def to_windows_kernel(*refs):
    args, out, buffers, sems = refs[:5], refs[5], refs[6:11], refs[11:]
    copies = [pltpu.make_async_copy(*c) for c in zip(args, buffers, sems)]
    for c in copies:
        c.start()
    _, lane = iotas((8, 128))
    zero = jnp.zeros((8, 128), F32)
    for a, ref in enumerate(buffers):
        copies[a].wait()
        for x in range(4):
            tiles = [ref[x, :, 128 * c : 128 * c + 128] for c in range(4)]
            up = [pltpu.roll(t, 32, 1) for t in tiles]
            down = [pltpu.roll(t, 96, 1) for t in tiles]
            for c in range(4):
                out[2 * c, a, x] = jnp.where(lane < 32, up[c - 1] if c else zero, up[c])
                out[2 * c + 1, a, x] = jnp.where(lane < 96, down[c], down[c + 1] if c < 3 else zero)


def flat(s, a, x):
    return (s * 5 + a) * 4 + x


def x_messages_kernel(own, to_low, to_high, first_by):
    for a in range(5):
        for x in range(4):
            for s in range(2):
                to_low[flat(s, a, x)] = own[s, a, x]
                to_high[flat(s, a, x)] = own[6 + s, a, x]
    to_low[40] = own[2, BX, 0]
    for x in range(32):
        first_by[x : x + 1] = own[x // 4, BY, x % 4][:1]


def corner_messages_kernel(low, high, to_low, to_high):
    keep = low_rows((8, 128))
    for a in range(5):
        for x in range(4):
            for ref in (to_low, to_high):
                ref[flat(0, a, x)] = low[flat(1, a, x)]
                ref[flat(1, a, x)] = high[flat(0, a, x)]
            outer_low, outer_high = low[flat(0, a, x)], high[flat(1, a, x)]
            to_low[flat(2, a, x)] = jnp.where(keep, outer_low, half(outer_high))
            to_high[flat(2, a, x)] = jnp.where(keep, half(outer_low), outer_high)


def fine_kernel(
    own, x_low, x_high, y_low, y_high, corner_low, corner_high, beyond_y, mid_coefs,
    fine_out, mid_first, mid_last, co, r, b,
):
    q0 = even_mask((24, 128))
    row, _ = iotas((24, 128))
    clear_guards(r, b, 24)
    zero = jnp.zeros((8, 128), F32)

    def plane(a, x):
        block, i = x // 4, x % 4
        if 2 <= block < 10:
            tiles = [ref[block - 2, a, i] for ref in (own, y_high, y_low)]
        elif block in (1, 10):
            side = int(block == 10)
            tiles = [(x_high if side else x_low)[flat(1 - side, a, i)]]
            tiles += [ref[flat(side, a, i)] for ref in (corner_high, corner_low)]
        else:
            up, down = corner_high[flat(2, a, i)], corner_low[flat(2, a, i)]
            if block == 0:
                tiles = [x_low[flat(0, a, i)], up, half(down)]
            else:
                tiles = [x_high[flat(1, a, i)], half(up), down]
        return jnp.concatenate(tiles, 0)

    bx0 = plane(BX, 0)
    for p in range(24):
        x = 2 * p
        co[S_R, p], co[S_B, p] = halves(q0, plane(RHS, x), plane(RHS, x + 1))
        bx1 = plane(BX, x + 1)
        bx2 = plane(BX, x + 2) if p < 23 else jnp.concatenate([x_high[40], zero, zero], 0)
        by = plane(BY, x), plane(BY, x + 1)
        bz = plane(BZ, x), plane(BZ, x + 1)
        fx, fy, fyp, fz = put_faces(co, p, q0, (bx0, bx1, bx2), by, bz)
        bx0 = bx2
        yp_r, yp_b = fyp
        if 4 <= p < 20:
            e0, e1 = beyond_y[x - 8 : x - 7], beyond_y[x - 7 : x - 6]
            up_r, up_b = halves(q0[15:16], e0, e1)
            yp_r = jnp.where(row == 15, up_r, yp_r)
            yp_b = jnp.where(row == 15, up_b, yp_b)
            co[YP_R, p], co[YP_B, p] = yp_r, yp_b
        a_r, a_b = halves(q0, plane(ALPHA, x), plane(ALPHA, x + 1))
        d_r = a_r + ((fx[0] + fz[0]) + (fy[0] + yp_r))
        d_b = a_b + ((fx[1] + fz[1]) + (fy[1] + yp_b))
        co[D_R, p], co[D_B, p] = d_r, d_b
        co[I_R, p], co[I_B, p] = inverse_of(d_r, a_r), inverse_of(d_b, a_b)
    smooth_cone(co, r, b, 16, 4, q0)
    sums = []
    for j in range(16):
        p = j + 4
        red, black = residual(co, r, b, p, q0)
        sums.append((red + black)[:8])
        fine_out[0, j] = r[p + 1][:8]
        fine_out[1, j] = b[p + 1][:8]
    along = pick(jnp.concatenate(sums, 0), one_hot((128, 128), lambda i, j: (i >> 1) == j))
    source = pick_rows(one_hot((64, 128), lambda i, j: (j >> 1) == i), along) * 0.125
    for t in range(4):
        out = mid_first if t < 2 else mid_last
        out[t % 2, 0] = mid_tile(source, t)
        for a in range(4):
            out[t % 2, a + 1] = mid_coefs[t, a]


def mid_tile(value, t):
    _, lane = iotas((8, 128))
    return jnp.where(lane < 64, value[16 * t : 16 * t + 8], pltpu.roll(value[16 * t + 8 : 16 * t + 16], 64, 1))


def low_rows_of(out_row, test):
    return one_hot((16, 8), lambda i, j: ((i >> 1) == out_row) & test(i & 1, j))


def coefficients_kernel(own, x_high, y_high, mid_coefs, mid_own, low_out):
    alphas, bys, nexts, bxs, bzs = [], [], [], [], []
    for j in range(16):
        s, x = j // 2, 2 * (j % 2)
        alphas.append(own[s, ALPHA, x] + own[s, ALPHA, x + 1])
        bys.append(own[s, BY, x] + own[s, BY, x + 1])
        nexts.append(y_high[s, BY, x] + y_high[s, BY, x + 1])
        bzs.append(own[s, BZ, x] + own[s, BZ, x + 1])
        bxs.append(own[s, BX, x])
    bxs.append(x_high[flat(0, BX, 0)])
    along = pick(
        jnp.concatenate(alphas + bys + nexts + bxs, 0), one_hot((128, 128), lambda i, j: (i >> 1) == j)
    )
    bz_z = pick(jnp.concatenate(bzs, 0), one_hot((128, 128), lambda i, j: i == 2 * j))
    y_sum = one_hot((64, 128), lambda i, j: (j >> 1) == i)
    y_even = one_hot((64, 128), lambda i, j: j == 2 * i)
    y_next = one_hot((64, 128), lambda i, j: ((i & 3) < 3) & (j == 2 * i + 2))
    y_last = one_hot((64, 128), lambda i, j: ((i & 3) == 3) & (j == 8 * (i >> 2)))
    alpha = pick_rows(y_sum, along[0:128]) * 0.125
    y_lower = pick_rows(y_even, along[128:256]) * 0.0625
    y_upper = (pick_rows(y_next, along[128:256]) + pick_rows(y_last, along[256:384])) * 0.0625
    x_lower = pick_rows(y_sum, along[384:512]) * 0.0625
    x_upper = pick_rows(y_sum, along[392:520]) * 0.0625
    z_lower = pick_rows(y_sum, bz_z) * 0.0625
    diagonal = alpha + ((x_lower + x_upper) + (y_lower + y_upper) + (z_lower + next_lane(z_lower)))
    sums = jnp.zeros((24, 128), F32)
    low_bz = jnp.zeros((8, 128), F32)
    for t in range(4):
        for a, value in enumerate((inverse_of(diagonal, alpha), x_lower, y_lower, z_lower)):
            mid_coefs[t, a] = mid_tile(value, t)
        mid_own[t] = mid_tile(diagonal, t)
        stack = jnp.concatenate([mid_tile(alpha, t), mid_coefs[t, 1], mid_coefs[t, 2]], 0)

        def chooser(test):
            def to(i, j):
                k = 2 * t + (i >> 6)
                return ((j >> 4) == k) & test(i & 63, j - 16 * k + 8)

            return one_hot((128, 128), to)

        sums += pick(stack, chooser(lambda i, j: (i >> 1) == j))
        low_bz += pick(mid_coefs[t, 3], chooser(lambda i, j: i == 2 * j))
    total = pick_rows(low_rows_of(0, lambda i, j: ((j & 3) >> 1) == i), sums[0:8]) * 0.125
    total += pick_rows(low_rows_of(1, lambda i, j: (j < 4) & ((j >> 1) == i)), sums[8:16]) * 0.0625
    total += pick_rows(low_rows_of(2, lambda i, j: (j & 3) == 2 * i), sums[16:24]) * 0.0625
    total += pick_rows(low_rows_of(3, lambda i, j: ((j & 3) >> 1) == i), low_bz) * 0.0625
    for k in range(4):
        low_out[k] = total[2 * k : 2 * k + 2]


def mid_message_kernel(low, first, last, high, out):
    for n, ref in enumerate((low, first, last, high)):
        for s in range(2):
            out[2 * n + s] = ref[s]


def chip_message_kernel(other, own, out):
    for s in range(8):
        out[s] = other[s]
    for s in range(6):
        out[8 + s] = own[s + 1]


def inner_tiles_kernel(values, out):
    for s in range(6):
        out[s] = values[s + 1]


def mid_kernel(mine, beside, across, beyond, own, low_coefs, level_out, low_out, co, r, b):
    upper = lax.rem(lax.axis_index("gy"), 2) == 1
    q0 = even_mask((24, 128))
    _, lane = iotas((8, 128))
    keep = low_rows((8, 128))
    zero = jnp.zeros((8, 128), F32)
    lower_core = lane < jnp.where(upper, 0, 128)
    clear_guards(r, b, 16)

    def part(tile, p):
        return jnp.where(lane < 64, pltpu.roll(tile, 64, 1) if p % 2 else tile, 0.0)

    def planes(p, a):
        t = p // 2
        c = part(mine[t, a], p)
        near = part(beside[t, a], p), part(across[t, a], p)
        h1, w1 = halves(lower_core, *near)
        h2, w2 = zero, zero
        if 0 < t < 7:
            far = part(beyond[t - 1, a], p), part(across[t + 7, a], p)
            h2, w2 = halves(lower_core, *far)
        e0 = [jnp.where(keep, c, half(h1)), jnp.where(keep, h2, 0.0), jnp.where(keep, w2, half(w1))]
        e1 = [jnp.where(keep, half(c), h1), jnp.where(keep, half(h2), 0.0), jnp.where(keep, half(w2), w1)]
        return jnp.concatenate(e0, 0), jnp.concatenate(e1, 0)

    bx0, bx1 = planes(0, 2)
    for p in range(16):
        co[S_R, p], co[S_B, p] = halves(q0, *planes(p, 0))
        co[I_R, p], co[I_B, p] = halves(q0, *planes(p, 1))
        n0, n1 = planes(p + 1, 2) if p < 15 else (jnp.zeros_like(bx0), bx1)
        put_faces(co, p, q0, (bx0, bx1, n0), planes(p, 3), planes(p, 4))
        bx0, bx1 = n0, n1
        if 4 <= p < 12:
            d = part(own[p // 2 - 2], p)
            d = jnp.concatenate([d, d, d], 0), jnp.concatenate([half(d)] * 3, 0)
            co[D_R, p], co[D_B, p] = halves(q0, *d)
    smooth_cone(co, r, b, 8, 4, q0)
    sums = []
    for k in range(8):
        red, black = residual(co, r, b, k + 4, q0)
        level_out[0, k] = r[k + 5][:8]
        level_out[1, k] = b[k + 5][:8]
        sums.append((red + black)[:8])
    along = pick(jnp.concatenate(sums, 0), one_hot((128, 128), lambda i, j: (i >> 1) == j))
    total = zero
    for k in range(8):
        moved = pltpu.roll(along[8 * k : 8 * k + 8], (16 * k - 8) % 128, 1)
        total = jnp.where((lane >> 4) == k, moved, total)
    source = pick_rows(low_rows_of(0, lambda i, j: (j < 4) & ((j >> 1) == i)), total)[:2] * 0.125
    coefs = [low_coefs[k] for k in range(4)]
    for j in range(low_out.shape[0]):
        low_out[j, 0] = source
        for k in range(4):
            low_out[j, k + 1] = coefs[k]


def whole_y_kernel(gathered, out):
    for g in range(out.shape[0]):
        for j in range(16):
            for k in range(5):
                out[g, 32 * k + 2 * j : 32 * k + 2 * j + 2] = gathered[16 * g + j, k]


def coarse_kernel(sweeps, low, own, high, level, fine, out, co, r, b, planes):
    shape = (32, 128)
    q0 = even_mask(shape)
    row, lane = iotas(shape)
    r[...] = jnp.zeros_like(r)
    b[...] = jnp.zeros_like(b)

    place_of = lane >> 4
    for a in range(5):
        for g in range(2):
            pieces = []
            for side in range(2):
                for s, ref in enumerate((low, own, high)):
                    block = ref[g + 2 * side, 32 * a : 32 * a + 32]
                    offset = 4 * side + s
                    pieces.append((offset, pltpu.roll(block, 16 * offset, 1) if offset else block))
            for k in range(8):
                total = jnp.zeros(shape, F32)
                for offset, piece in pieces:
                    total = jnp.where(place_of == (k + offset) % 8, piece, total)
                planes[a, 8 * g + k] = pltpu.roll(total, 128 - 16 * k, 1) if k else total

    def plane(a, i):
        return planes[a, i]

    first_bx = plane(2, 0)
    bx0 = first_bx
    for p in range(8):
        x = 2 * p
        co[S_R, p], co[S_B, p] = halves(q0, plane(0, x), plane(0, x + 1))
        bx1 = plane(2, x + 1)
        bx2 = plane(2, x + 2) if p < 7 else jnp.where(lane < 64, pltpu.roll(first_bx, 64, 1), 0.0)
        by, bz = (plane(3, x), plane(3, x + 1)), (plane(4, x), plane(4, x + 1))
        fx, fy, fyp, fz = put_faces(co, p, q0, (bx0, bx1, bx2), by, bz)
        bx0 = bx2
        yp_r, yp_b = jnp.where(row == 31, 0.0, fyp[0]), jnp.where(row == 31, 0.0, fyp[1])
        co[YP_R, p], co[YP_B, p] = yp_r, yp_b
        co[YM_R, p], co[YM_B, p] = jnp.where(row == 0, 0.0, fy[0]), jnp.where(row == 0, 0.0, fy[1])
        a_r, a_b = halves(q0, plane(1, x), plane(1, x + 1))
        d_r = a_r + ((fx[0] + fz[0]) + (fy[0] + yp_r))
        d_b = a_b + ((fx[1] + fz[1]) + (fy[1] + yp_b))
        co[I_R, p], co[I_B, p] = inverse_of(d_r, a_r), inverse_of(d_b, a_b)

    def join(ref):
        ref[0] = jnp.where(lane < 64, 0.0, pltpu.roll(ref[8], 64, 1))
        ref[9] = jnp.where(lane < 64, pltpu.roll(ref[1], 64, 1), 0.0)

    def sweep(step, carry):
        relax(co, r, b, range(8), True, q0)
        join(r)
        relax(co, b, r, range(8), False, q0)
        join(b)
        return carry

    lax.fori_loop(0, sweeps, sweep, 0)

    gy, ring, place = (lax.axis_index(name) for name in ("gy", "ring", "place"))
    side, base = ring // 2, 4 * lax.rem(ring, 2)
    parts = []
    for k in range(8):
        red, black = r[base + k // 2 + 1], b[base + k // 2 + 1]
        value = jnp.where(q0, red, black) if k % 2 == 0 else jnp.where(q0, black, red)
        value = pltpu.roll(value, lax.rem(32 - 2 * gy, 32), 0)
        parts.append(pltpu.roll(value, 64 * side, 1)[:8])
    q0 = even_mask((8, 128))
    row, lane = iotas((8, 128))
    up = pick(jnp.concatenate(parts, 0), one_hot((128, 128), lambda i, j: (j >> 1) + 8 == i))
    spread = one_hot((64, 64), lambda i, j: ((i >> 3) == (j >> 3)) & (((i & 3) >> 1) == (j & 7)))
    up = pick_rows(spread, up)
    mid = []
    for k in range(8):
        add = up[8 * k : 8 * k + 8]
        mid.extend(halves(q0, level[0, k] + add, level[1, k] + add))
        mine = pltpu.roll(parts[k], lax.rem(16 * place + 112, 128), 1)
        out[k, 2] = jnp.where(((lane >> 4) == place) & (row < 2), mine, 0.0)
    wide = pick(jnp.concatenate(mid, 0), one_hot((128, 128), lambda i, j: (j >> 1) == i))
    spread = one_hot((128, 128), lambda i, j: ((i >> 3) == (j >> 3)) & (((i & 7) >> 1) == (j & 7)))
    wide = pick_rows(spread, wide)
    for j in range(16):
        add = wide[8 * j : 8 * j + 8]
        e0, e1 = halves(q0, fine[0, j] + add, fine[1, j] + add)
        out[j // 2, j % 2] = jnp.where(lane < 64, pltpu.roll(e0, 96, 1), pltpu.roll(e1, 32, 1))


def finish_kernel(pieces, fine_out, coarse_out):
    _, lane = iotas((8, 128))
    for t in range(2):
        for c in range(4):
            a, b = pieces[2 * c, t], pieces[2 * c + 1, t]
            span = slice(128 * c, 128 * c + 128)
            fine_out[2 * t, :, span] = jnp.where(lane < 64, a, pltpu.roll(b, 64, 1))
            fine_out[2 * t + 1, :, span] = jnp.where(lane < 64, pltpu.roll(a, 64, 1), b)
    total = pieces[0, 2]
    for j in range(1, RING):
        total = total + pieces[j, 2]
    coarse_out[0] = total[:2]


def cycle(rhs, alpha, beta_x, beta_y, beta_z):
    rings, count_y = lax.axis_size("ring"), lax.axis_size("gy")

    (own,) = call(to_windows_kernel, [(RING, 5, 4, 8, 128)], copied=True)(rhs, alpha, beta_x, beta_y, beta_z)
    own = lax.all_to_all(own, "place", 0, 0, tiled=True)
    to_low, to_high, first_by = call(
        x_messages_kernel, [(41, 8, 128), (40, 8, 128), (32, 128)]
    )(own)
    x_low, x_high = shifted(to_high, "ring", 1), shifted(to_low, "ring", -1)
    y_low, y_high = shifted(own, "gy", 1), shifted(own, "gy", -1)
    beyond_y = shifted(first_by, "gy", -2)
    to_low, to_high = call(
        corner_messages_kernel, [(60, 8, 128), (60, 8, 128)]
    )(x_low, x_high)
    corner_low = shifted(to_high, "gy", 1)
    corner_high = shifted(to_low, "gy", -1)
    mid_coefs, mid_own, low_coefs = call(
        coefficients_kernel, [(4, 4, 8, 128), (4, 8, 128), (4, 2, 128)]
    )(own, x_high, y_high)
    fine, mid_first, mid_last = call(
        fine_kernel,
        [(2, 16, 8, 128), (2, 5, 8, 128), (2, 5, 8, 128)],
        [(17, 24, 24, 128), (26, 24, 128), (26, 24, 128)],
    )(own, x_low, x_high, y_low, y_high, corner_low, corner_high, beyond_y, mid_coefs)

    low, high = shifted(mid_last, "ring", 1), shifted(mid_first, "ring", -1)
    (mid,) = call(mid_message_kernel, [(8, 5, 8, 128)])(low, mid_first, mid_last, high)
    cores = [(i, i ^ 1) for i in range(count_y)]
    chips = [(i, i + 2 - 4 * (i % 2)) for i in range(count_y) if 0 <= i + 2 - 4 * (i % 2) < count_y]
    beside = lax.ppermute(mid, "gy", cores)
    (message,) = call(chip_message_kernel, [(14, 5, 8, 128)])(beside, mid)
    across = lax.ppermute(message, "gy", chips)
    (inner,) = call(inner_tiles_kernel, [(6, 5, 8, 128)])(across)
    beyond = lax.ppermute(inner, "gy", cores)
    level, low = call(
        mid_kernel,
        [(2, 8, 8, 128), (rings * count_y, 5, 2, 128)],
        [(17, 16, 24, 128), (18, 24, 128), (18, 24, 128)],
    )(mid, beside, across, beyond, mid_own, low_coefs)

    low = lax.all_to_all(low, ("ring", "gy"), 0, 0, tiled=True)
    (own,) = call(whole_y_kernel, [(rings, 160, 128)])(low)
    (pieces,) = call(
        lambda *refs: coarse_kernel(8, *refs),
        [(RING, 3, 8, 128)],
        [(17, 8, 32, 128), (10, 32, 128), (10, 32, 128), (5, 16, 32, 128)],
    )(shifted(own, "place", 1), own, shifted(own, "place", -1), level, fine)
    pieces = lax.all_to_all(pieces, "place", 0, 0, tiled=True)
    fine_solution, coarse = call(finish_kernel, [rhs.shape, (1, 2, 128)])(pieces)
    return fine_solution, coarse


def solution(mesh):
    count_x, count_y = mesh.devices.shape
    devices = np.array(mesh.devices).reshape(count_x // RING, RING, count_y)
    split = Mesh(devices, ("ring", "place", "gy"))
    placed = P(("ring", "place"), "gy", None)
    return jax.shard_map(
        cycle,
        mesh=split,
        in_specs=(placed,) * 5,
        out_specs=(placed, placed),
        check_vma=False,
    )
```

```python
import jax
import jax.numpy as jnp
import numpy as np
from jax import lax
from jax.experimental import pallas as pl
from jax.experimental.pallas import tpu as pltpu
from jax.sharding import Mesh
from jax.sharding import PartitionSpec as P

F32 = jnp.float32
RHS, ALPHA, BX, BY, BZ = range(5)
VMEM_BYTES = 20 * 2**20
ALL_VMEM = 62 * 2**20
RING = 8


def shifted(values, name, steps):
    count = lax.axis_size(name)
    lead, last = max(0, -steps), min(count, count - steps)
    return lax.ppermute(values, name, [(i, i + steps) for i in range(lead, last)])


def call(kernel, outs, scratch=(), copied=False):
    def run(*args):
        space = pltpu.HBM if copied else pltpu.VMEM
        buffers = [pltpu.VMEM(a.shape, F32) for a in args] if copied else []
        sems = [pltpu.SemaphoreType.DMA] * len(args) if copied else []
        return pl.pallas_call(
            kernel,
            out_shape=[jax.ShapeDtypeStruct(s, F32) for s in outs],
            in_specs=[pl.BlockSpec(memory_space=space)] * len(args),
            out_specs=[pl.BlockSpec(memory_space=pltpu.VMEM)] * len(outs),
            scratch_shapes=[pltpu.VMEM(s, F32) for s in scratch] + buffers + sems,
            compiler_params=pltpu.CompilerParams(vmem_limit_bytes=ALL_VMEM if copied else VMEM_BYTES),
        )(*args)

    return run


def iotas(shape):
    return lax.broadcasted_iota(jnp.int32, shape, 0), lax.broadcasted_iota(jnp.int32, shape, 1)


def even_mask(shape):
    row, lane = iotas(shape)
    return ((row + lane) & 1) == 0


def half(x):
    return pltpu.roll(x, 4, 0)


def prev_row(x):
    return pltpu.roll(x, 1, 0)


def next_row(x):
    return pltpu.roll(x, x.shape[0] - 1, 0)


def prev_lane(x):
    return pltpu.roll(x, 1, 1)


def next_lane(x):
    return pltpu.roll(x, x.shape[1] - 1, 1)


def pick(values, chooser):
    parts, rest = [], values
    for _ in range(3):
        part = rest.astype(jnp.bfloat16)
        parts.append(part)
        rest = rest - part.astype(F32)
    total = jnp.dot(jnp.concatenate(parts, 0), chooser, preferred_element_type=F32)
    n = values.shape[0]
    return (total[2 * n :] + total[n : 2 * n]) + total[:n]


def pick_rows(chooser, values):
    parts, rest = [], values
    for _ in range(3):
        part = rest.astype(jnp.bfloat16)
        parts.append(jnp.dot(chooser, part, preferred_element_type=F32))
        rest = rest - part.astype(F32)
    return (parts[2] + parts[1]) + parts[0]


def one_hot(shape, test):
    row, col = iotas(shape)
    return jnp.where(test(row, col), 1.0, 0.0).astype(jnp.bfloat16)


def low_rows(shape):
    row, _ = iotas(shape)
    return (row & 7) < 4


def inverse_of(diagonal, cell):
    inside = cell > 0.0
    return jnp.where(inside, 1.0 / jnp.where(inside, diagonal, 1.0), 0.0)


def halves(q0, e0, e1):
    return jnp.where(q0, e0, e1), jnp.where(q0, e1, e0)


def clear_guards(r, b, n):
    for ref in (r, b):
        ref[0] = jnp.zeros_like(ref[0])
        ref[n + 1] = jnp.zeros_like(ref[n + 1])


S_R, S_B, WP, WO_R, WO_B, YM_R, YM_B, YP_R, YP_B, ZM_R, ZM_B, ZP_R, ZP_B, I_R, I_B, D_R, D_B = range(17)


def beside(co, src, p, red, q0):
    v = src[p + 1]
    before, after = src[p], src[p + 2]
    other = jnp.where(q0, before, after) if red else jnp.where(q0, after, before)
    wo, ym, yp, zm, zp = (
        (WO_R, YM_R, YP_R, ZM_R, ZP_R) if red else (WO_B, YM_B, YP_B, ZM_B, ZP_B)
    )
    total = co[WP, p] * v + co[wo, p] * other
    total = total + (co[ym, p] * prev_row(v) + co[yp, p] * next_row(v))
    return total + (co[zm, p] * prev_lane(v) + co[zp, p] * next_lane(v))


def relax(co, dst, src, pairs, red, q0):
    s, inv = (S_R, I_R) if red else (S_B, I_B)
    for p in pairs:
        dst[p + 1] = (co[s, p] + beside(co, src, p, red, q0)) * co[inv, p]


def first_red(co, dst, pairs):
    for p in pairs:
        dst[p + 1] = co[S_R, p] * co[I_R, p]


def residual(co, r, b, p, q0):
    red = co[S_R, p] - (co[D_R, p] * r[p + 1] - beside(co, b, p, True, q0))
    black = co[S_B, p] - (co[D_B, p] * b[p + 1] - beside(co, r, p, False, q0))
    return red, black


def put_faces(co, p, q0, bx, by, bz):
    b0, b1, b2 = bx
    wo_r, wo_b = halves(q0, b0, b2)
    y_r, y_b = halves(q0, *by)
    z_r, z_b = halves(q0, *bz)
    yp_r, yp_b = next_row(y_b), next_row(y_r)
    zp_r, zp_b = next_lane(z_b), next_lane(z_r)
    co[WP, p], co[WO_R, p], co[WO_B, p] = b1, wo_r, wo_b
    co[YM_R, p], co[YM_B, p], co[YP_R, p], co[YP_B, p] = y_r, y_b, yp_r, yp_b
    co[ZM_R, p], co[ZM_B, p], co[ZP_R, p], co[ZP_B, p] = z_r, z_b, zp_r, zp_b
    return (b1 + wo_r, b1 + wo_b), (y_r, y_b), (yp_r, yp_b), (z_r + zp_r, z_b + zp_b)


def smooth_cone(co, r, b, own, halo, q0):
    def pairs(reach):
        extra = min(halo, (reach + 1) // 2)
        return range(halo - extra, halo + own + extra)

    first_red(co, r, pairs(8))
    for step in range(2, 9):
        red = step % 2 == 1
        relax(co, r if red else b, b if red else r, pairs(9 - step), red, q0)


def to_windows_kernel(*refs):
    args, out, buffers, sems = refs[:5], refs[5], refs[6:11], refs[11:]
    copies = [pltpu.make_async_copy(*c) for c in zip(args, buffers, sems)]
    for c in copies:
        c.start()
    _, lane = iotas((8, 128))
    zero = jnp.zeros((8, 128), F32)
    for a, ref in enumerate(buffers):
        copies[a].wait()
        for x in range(4):
            tiles = [ref[x, :, 128 * c : 128 * c + 128] for c in range(4)]
            up = [pltpu.roll(t, 32, 1) for t in tiles]
            down = [pltpu.roll(t, 96, 1) for t in tiles]
            for c in range(4):
                out[2 * c, a, x] = jnp.where(lane < 32, up[c - 1] if c else zero, up[c])
                out[2 * c + 1, a, x] = jnp.where(lane < 96, down[c], down[c + 1] if c < 3 else zero)


def flat(s, a, x):
    return (s * 5 + a) * 4 + x


def x_messages_kernel(own, to_low, to_high, first_by):
    for a in range(5):
        for x in range(4):
            for s in range(2):
                to_low[flat(s, a, x)] = own[s, a, x]
                to_high[flat(s, a, x)] = own[6 + s, a, x]
    to_low[40] = own[2, BX, 0]
    for x in range(32):
        first_by[x : x + 1] = own[x // 4, BY, x % 4][:1]


def corner_messages_kernel(low, high, to_low, to_high):
    keep = low_rows((8, 128))
    for a in range(5):
        for x in range(4):
            for ref in (to_low, to_high):
                ref[flat(0, a, x)] = low[flat(1, a, x)]
                ref[flat(1, a, x)] = high[flat(0, a, x)]
            outer_low, outer_high = low[flat(0, a, x)], high[flat(1, a, x)]
            to_low[flat(2, a, x)] = jnp.where(keep, outer_low, half(outer_high))
            to_high[flat(2, a, x)] = jnp.where(keep, half(outer_low), outer_high)


def fine_kernel(
    own, x_low, x_high, y_low, y_high, corner_low, corner_high, beyond_y, mid_coefs,
    fine_out, mid_first, mid_last, co, r, b,
):
    q0 = even_mask((24, 128))
    row, _ = iotas((24, 128))
    clear_guards(r, b, 24)
    zero = jnp.zeros((8, 128), F32)

    def plane(a, x):
        block, i = x // 4, x % 4
        if 2 <= block < 10:
            tiles = [ref[block - 2, a, i] for ref in (own, y_high, y_low)]
        elif block in (1, 10):
            side = int(block == 10)
            tiles = [(x_high if side else x_low)[flat(1 - side, a, i)]]
            tiles += [ref[flat(side, a, i)] for ref in (corner_high, corner_low)]
        else:
            up, down = corner_high[flat(2, a, i)], corner_low[flat(2, a, i)]
            if block == 0:
                tiles = [x_low[flat(0, a, i)], up, half(down)]
            else:
                tiles = [x_high[flat(1, a, i)], half(up), down]
        return jnp.concatenate(tiles, 0)

    bx0 = plane(BX, 0)
    for p in range(24):
        x = 2 * p
        co[S_R, p], co[S_B, p] = halves(q0, plane(RHS, x), plane(RHS, x + 1))
        bx1 = plane(BX, x + 1)
        bx2 = plane(BX, x + 2) if p < 23 else jnp.concatenate([x_high[40], zero, zero], 0)
        by = plane(BY, x), plane(BY, x + 1)
        bz = plane(BZ, x), plane(BZ, x + 1)
        fx, fy, fyp, fz = put_faces(co, p, q0, (bx0, bx1, bx2), by, bz)
        bx0 = bx2
        yp_r, yp_b = fyp
        if 4 <= p < 20:
            e0, e1 = beyond_y[x - 8 : x - 7], beyond_y[x - 7 : x - 6]
            up_r, up_b = halves(q0[15:16], e0, e1)
            yp_r = jnp.where(row == 15, up_r, yp_r)
            yp_b = jnp.where(row == 15, up_b, yp_b)
            co[YP_R, p], co[YP_B, p] = yp_r, yp_b
        a_r, a_b = halves(q0, plane(ALPHA, x), plane(ALPHA, x + 1))
        d_r = a_r + ((fx[0] + fz[0]) + (fy[0] + yp_r))
        d_b = a_b + ((fx[1] + fz[1]) + (fy[1] + yp_b))
        co[D_R, p], co[D_B, p] = d_r, d_b
        co[I_R, p], co[I_B, p] = inverse_of(d_r, a_r), inverse_of(d_b, a_b)
    smooth_cone(co, r, b, 16, 4, q0)
    sums = []
    for j in range(16):
        p = j + 4
        red, black = residual(co, r, b, p, q0)
        sums.append((red + black)[:8])
        fine_out[0, j] = r[p + 1][:8]
        fine_out[1, j] = b[p + 1][:8]
    along = pick(jnp.concatenate(sums, 0), one_hot((128, 128), lambda i, j: (i >> 1) == j))
    source = pick_rows(one_hot((64, 128), lambda i, j: (j >> 1) == i), along) * 0.125
    for t in range(4):
        out = mid_first if t < 2 else mid_last
        out[t % 2, 0] = mid_tile(source, t)
        for a in range(4):
            out[t % 2, a + 1] = mid_coefs[t, a]


def mid_tile(value, t):
    _, lane = iotas((8, 128))
    return jnp.where(lane < 64, value[16 * t : 16 * t + 8], pltpu.roll(value[16 * t + 8 : 16 * t + 16], 64, 1))


def low_rows_of(out_row, test):
    return one_hot((16, 8), lambda i, j: ((i >> 1) == out_row) & test(i & 1, j))


def coefficients_kernel(own, x_high, y_high, mid_coefs, mid_own, low_out):
    alphas, bys, nexts, bxs, bzs = [], [], [], [], []
    for j in range(16):
        s, x = j // 2, 2 * (j % 2)
        alphas.append(own[s, ALPHA, x] + own[s, ALPHA, x + 1])
        bys.append(own[s, BY, x] + own[s, BY, x + 1])
        nexts.append(y_high[s, BY, x] + y_high[s, BY, x + 1])
        bzs.append(own[s, BZ, x] + own[s, BZ, x + 1])
        bxs.append(own[s, BX, x])
    bxs.append(x_high[flat(0, BX, 0)])
    along = pick(
        jnp.concatenate(alphas + bys + nexts + bxs, 0), one_hot((128, 128), lambda i, j: (i >> 1) == j)
    )
    bz_z = pick(jnp.concatenate(bzs, 0), one_hot((128, 128), lambda i, j: i == 2 * j))
    y_sum = one_hot((64, 128), lambda i, j: (j >> 1) == i)
    y_even = one_hot((64, 128), lambda i, j: j == 2 * i)
    y_next = one_hot((64, 128), lambda i, j: ((i & 3) < 3) & (j == 2 * i + 2))
    y_last = one_hot((64, 128), lambda i, j: ((i & 3) == 3) & (j == 8 * (i >> 2)))
    alpha = pick_rows(y_sum, along[0:128]) * 0.125
    y_lower = pick_rows(y_even, along[128:256]) * 0.0625
    y_upper = (pick_rows(y_next, along[128:256]) + pick_rows(y_last, along[256:384])) * 0.0625
    x_lower = pick_rows(y_sum, along[384:512]) * 0.0625
    x_upper = pick_rows(y_sum, along[392:520]) * 0.0625
    z_lower = pick_rows(y_sum, bz_z) * 0.0625
    diagonal = alpha + ((x_lower + x_upper) + (y_lower + y_upper) + (z_lower + next_lane(z_lower)))
    sums = jnp.zeros((24, 128), F32)
    low_bz = jnp.zeros((8, 128), F32)
    for t in range(4):
        for a, value in enumerate((inverse_of(diagonal, alpha), x_lower, y_lower, z_lower)):
            mid_coefs[t, a] = mid_tile(value, t)
        mid_own[t] = mid_tile(diagonal, t)
        stack = jnp.concatenate([mid_tile(alpha, t), mid_coefs[t, 1], mid_coefs[t, 2]], 0)

        def chooser(test):
            def to(i, j):
                k = 2 * t + (i >> 6)
                return ((j >> 4) == k) & test(i & 63, j - 16 * k + 8)

            return one_hot((128, 128), to)

        sums += pick(stack, chooser(lambda i, j: (i >> 1) == j))
        low_bz += pick(mid_coefs[t, 3], chooser(lambda i, j: i == 2 * j))
    total = pick_rows(low_rows_of(0, lambda i, j: ((j & 3) >> 1) == i), sums[0:8]) * 0.125
    total += pick_rows(low_rows_of(1, lambda i, j: (j < 4) & ((j >> 1) == i)), sums[8:16]) * 0.0625
    total += pick_rows(low_rows_of(2, lambda i, j: (j & 3) == 2 * i), sums[16:24]) * 0.0625
    total += pick_rows(low_rows_of(3, lambda i, j: ((j & 3) >> 1) == i), low_bz) * 0.0625
    for k in range(4):
        low_out[k] = total[2 * k : 2 * k + 2]


def mid_message_kernel(low, first, last, high, out, inner):
    tiles = [ref[s] for ref in (low, first, last, high) for s in range(2)]
    for s in range(8):
        out[s] = tiles[s]
        if 0 < s < 7:
            inner[s - 1] = tiles[s]


def chip_message_kernel(other, inner, out):
    for s in range(8):
        out[s] = other[s]
    for s in range(6):
        out[8 + s] = inner[s]


def mid_kernel(mine, beside, across, beyond, own, low_coefs, level_out, low_out, co, r, b):
    upper = lax.rem(lax.axis_index("gy"), 2) == 1
    q0 = even_mask((24, 128))
    _, lane = iotas((8, 128))
    keep = low_rows((8, 128))
    zero = jnp.zeros((8, 128), F32)
    lower_core = lane < jnp.where(upper, 0, 128)
    clear_guards(r, b, 16)

    def part(tile, p):
        return jnp.where(lane < 64, pltpu.roll(tile, 64, 1) if p % 2 else tile, 0.0)

    def planes(p, a):
        t = p // 2
        c = part(mine[t, a], p)
        near = part(beside[t, a], p), part(across[t, a], p)
        h1, w1 = halves(lower_core, *near)
        h2, w2 = zero, zero
        if 0 < t < 7:
            far = part(beyond[t - 1, a], p), part(across[t + 7, a], p)
            h2, w2 = halves(lower_core, *far)
        e0 = [jnp.where(keep, c, half(h1)), jnp.where(keep, h2, 0.0), jnp.where(keep, w2, half(w1))]
        e1 = [jnp.where(keep, half(c), h1), jnp.where(keep, half(h2), 0.0), jnp.where(keep, half(w2), w1)]
        return jnp.concatenate(e0, 0), jnp.concatenate(e1, 0)

    bx0, bx1 = planes(0, 2)
    for p in range(16):
        co[S_R, p], co[S_B, p] = halves(q0, *planes(p, 0))
        co[I_R, p], co[I_B, p] = halves(q0, *planes(p, 1))
        n0, n1 = planes(p + 1, 2) if p < 15 else (jnp.zeros_like(bx0), bx1)
        put_faces(co, p, q0, (bx0, bx1, n0), planes(p, 3), planes(p, 4))
        bx0, bx1 = n0, n1
        if 4 <= p < 12:
            d = part(own[p // 2 - 2], p)
            d = jnp.concatenate([d, d, d], 0), jnp.concatenate([half(d)] * 3, 0)
            co[D_R, p], co[D_B, p] = halves(q0, *d)
    smooth_cone(co, r, b, 8, 4, q0)
    sums = []
    for k in range(8):
        red, black = residual(co, r, b, k + 4, q0)
        level_out[0, k] = r[k + 5][:8]
        level_out[1, k] = b[k + 5][:8]
        sums.append((red + black)[:8])
    along = pick(jnp.concatenate(sums, 0), one_hot((128, 128), lambda i, j: (i >> 1) == j))
    total = zero
    for k in range(8):
        moved = pltpu.roll(along[8 * k : 8 * k + 8], (16 * k - 8) % 128, 1)
        total = jnp.where((lane >> 4) == k, moved, total)
    source = pick_rows(low_rows_of(0, lambda i, j: (j < 4) & ((j >> 1) == i)), total)[:2] * 0.125
    coefs = [low_coefs[k] for k in range(4)]
    for j in range(low_out.shape[0]):
        low_out[j, 0] = source
        for k in range(4):
            low_out[j, k + 1] = coefs[k]


def whole_y_kernel(gathered, out):
    for g in range(out.shape[0]):
        for j in range(16):
            for k in range(5):
                out[g, 32 * k + 2 * j : 32 * k + 2 * j + 2] = gathered[16 * g + j, k]


def coarse_kernel(sweeps, low, own, high, level, fine, out, co, r, b, planes):
    shape = (32, 128)
    q0 = even_mask(shape)
    row, lane = iotas(shape)
    r[...] = jnp.zeros_like(r)
    b[...] = jnp.zeros_like(b)

    place_of = lane >> 4
    for a in range(5):
        for g in range(2):
            pieces = []
            for side in range(2):
                for s, ref in enumerate((low, own, high)):
                    block = ref[g + 2 * side, 32 * a : 32 * a + 32]
                    offset = 4 * side + s
                    pieces.append((offset, pltpu.roll(block, 16 * offset, 1) if offset else block))
            for k in range(8):
                total = jnp.zeros(shape, F32)
                for offset, piece in pieces:
                    total = jnp.where(place_of == (k + offset) % 8, piece, total)
                planes[a, 8 * g + k] = pltpu.roll(total, 128 - 16 * k, 1) if k else total

    def plane(a, i):
        return planes[a, i]

    first_bx = plane(2, 0)
    bx0 = first_bx
    for p in range(8):
        x = 2 * p
        co[S_R, p], co[S_B, p] = halves(q0, plane(0, x), plane(0, x + 1))
        bx1 = plane(2, x + 1)
        bx2 = plane(2, x + 2) if p < 7 else jnp.where(lane < 64, pltpu.roll(first_bx, 64, 1), 0.0)
        by, bz = (plane(3, x), plane(3, x + 1)), (plane(4, x), plane(4, x + 1))
        fx, fy, fyp, fz = put_faces(co, p, q0, (bx0, bx1, bx2), by, bz)
        bx0 = bx2
        yp_r, yp_b = jnp.where(row == 31, 0.0, fyp[0]), jnp.where(row == 31, 0.0, fyp[1])
        co[YP_R, p], co[YP_B, p] = yp_r, yp_b
        co[YM_R, p], co[YM_B, p] = jnp.where(row == 0, 0.0, fy[0]), jnp.where(row == 0, 0.0, fy[1])
        a_r, a_b = halves(q0, plane(1, x), plane(1, x + 1))
        d_r = a_r + ((fx[0] + fz[0]) + (fy[0] + yp_r))
        d_b = a_b + ((fx[1] + fz[1]) + (fy[1] + yp_b))
        co[I_R, p], co[I_B, p] = inverse_of(d_r, a_r), inverse_of(d_b, a_b)

    def join(ref):
        ref[0] = jnp.where(lane < 64, 0.0, pltpu.roll(ref[8], 64, 1))
        ref[9] = jnp.where(lane < 64, pltpu.roll(ref[1], 64, 1), 0.0)

    def sweep(step, carry):
        relax(co, r, b, range(8), True, q0)
        join(r)
        relax(co, b, r, range(8), False, q0)
        join(b)
        return carry

    lax.fori_loop(0, sweeps, sweep, 0)

    gy, ring, place = (lax.axis_index(name) for name in ("gy", "ring", "place"))
    side, base = ring // 2, 4 * lax.rem(ring, 2)
    parts = []
    for k in range(8):
        red, black = r[base + k // 2 + 1], b[base + k // 2 + 1]
        value = jnp.where(q0, red, black) if k % 2 == 0 else jnp.where(q0, black, red)
        value = pltpu.roll(value, lax.rem(32 - 2 * gy, 32), 0)
        parts.append(pltpu.roll(value, 64 * side, 1)[:8])
    q0 = even_mask((8, 128))
    row, lane = iotas((8, 128))
    up = pick(jnp.concatenate(parts, 0), one_hot((128, 128), lambda i, j: (j >> 1) + 8 == i))
    spread = one_hot((64, 64), lambda i, j: ((i >> 3) == (j >> 3)) & (((i & 3) >> 1) == (j & 7)))
    up = pick_rows(spread, up)
    mid = []
    for k in range(8):
        add = up[8 * k : 8 * k + 8]
        mid.extend(halves(q0, level[0, k] + add, level[1, k] + add))
        mine = pltpu.roll(parts[k], lax.rem(16 * place + 112, 128), 1)
        out[k, 2] = jnp.where(((lane >> 4) == place) & (row < 2), mine, 0.0)
    wide = pick(jnp.concatenate(mid, 0), one_hot((128, 128), lambda i, j: (j >> 1) == i))
    spread = one_hot((128, 128), lambda i, j: ((i >> 3) == (j >> 3)) & (((i & 7) >> 1) == (j & 7)))
    wide = pick_rows(spread, wide)
    for j in range(16):
        add = wide[8 * j : 8 * j + 8]
        e0, e1 = halves(q0, fine[0, j] + add, fine[1, j] + add)
        out[j // 2, j % 2] = jnp.where(lane < 64, pltpu.roll(e0, 96, 1), pltpu.roll(e1, 32, 1))


def finish_kernel(pieces, fine_out, coarse_out):
    _, lane = iotas((8, 128))
    for t in range(2):
        for c in range(4):
            a, b = pieces[2 * c, t], pieces[2 * c + 1, t]
            span = slice(128 * c, 128 * c + 128)
            fine_out[2 * t, :, span] = jnp.where(lane < 64, a, pltpu.roll(b, 64, 1))
            fine_out[2 * t + 1, :, span] = jnp.where(lane < 64, pltpu.roll(a, 64, 1), b)
    total = pieces[0, 2]
    for j in range(1, RING):
        total = total + pieces[j, 2]
    coarse_out[0] = total[:2]


def cycle(rhs, alpha, beta_x, beta_y, beta_z):
    rings, count_y = lax.axis_size("ring"), lax.axis_size("gy")

    (own,) = call(to_windows_kernel, [(RING, 5, 4, 8, 128)], copied=True)(rhs, alpha, beta_x, beta_y, beta_z)
    own = lax.all_to_all(own, "place", 0, 0, tiled=True)
    to_low, to_high, first_by = call(
        x_messages_kernel, [(41, 8, 128), (40, 8, 128), (32, 128)]
    )(own)
    x_low, x_high = shifted(to_high, "ring", 1), shifted(to_low, "ring", -1)
    y_low, y_high = shifted(own, "gy", 1), shifted(own, "gy", -1)
    beyond_y = shifted(first_by, "gy", -2)
    to_low, to_high = call(
        corner_messages_kernel, [(60, 8, 128), (60, 8, 128)]
    )(x_low, x_high)
    corner_low = shifted(to_high, "gy", 1)
    corner_high = shifted(to_low, "gy", -1)
    mid_coefs, mid_own, low_coefs = call(
        coefficients_kernel, [(4, 4, 8, 128), (4, 8, 128), (4, 2, 128)]
    )(own, x_high, y_high)
    fine, mid_first, mid_last = call(
        fine_kernel,
        [(2, 16, 8, 128), (2, 5, 8, 128), (2, 5, 8, 128)],
        [(17, 24, 24, 128), (26, 24, 128), (26, 24, 128)],
    )(own, x_low, x_high, y_low, y_high, corner_low, corner_high, beyond_y, mid_coefs)

    low, high = shifted(mid_last, "ring", 1), shifted(mid_first, "ring", -1)
    mid, inner = call(mid_message_kernel, [(8, 5, 8, 128), (6, 5, 8, 128)])(low, mid_first, mid_last, high)
    cores = [(i, i ^ 1) for i in range(count_y)]
    outward = [(i, i + 2 - 4 * (i % 2)) for i in range(count_y)]
    inward = [(j, i) for i, j in outward]
    chips, far = ([(i, j) for i, j in p if min(i, j) >= 0 and max(i, j) < count_y] for p in (outward, inward))
    beside = lax.ppermute(mid, "gy", cores)
    beyond = lax.ppermute(inner, "gy", far)
    (message,) = call(chip_message_kernel, [(14, 5, 8, 128)])(beside, inner)
    across = lax.ppermute(message, "gy", chips)
    level, low = call(
        mid_kernel,
        [(2, 8, 8, 128), (rings * count_y, 5, 2, 128)],
        [(17, 16, 24, 128), (18, 24, 128), (18, 24, 128)],
    )(mid, beside, across, beyond, mid_own, low_coefs)

    low = lax.all_to_all(low, ("ring", "gy"), 0, 0, tiled=True)
    (own,) = call(whole_y_kernel, [(rings, 160, 128)])(low)
    (pieces,) = call(
        lambda *refs: coarse_kernel(8, *refs),
        [(RING, 3, 8, 128)],
        [(17, 8, 32, 128), (10, 32, 128), (10, 32, 128), (5, 16, 32, 128)],
    )(shifted(own, "place", 1), own, shifted(own, "place", -1), level, fine)
    pieces = lax.all_to_all(pieces, "place", 0, 0, tiled=True)
    fine_solution, coarse = call(finish_kernel, [rhs.shape, (1, 2, 128)])(pieces)
    return fine_solution, coarse


def solution(mesh):
    count_x, count_y = mesh.devices.shape
    devices = np.array(mesh.devices).reshape(count_x // RING, RING, count_y)
    split = Mesh(devices, ("ring", "place", "gy"))
    placed = P(("ring", "place"), "gy", None)
    return jax.shard_map(
        cycle,
        mesh=split,
        in_specs=(placed,) * 5,
        out_specs=(placed, placed),
        check_vma=False,
    )
```

```python
import jax
import jax.numpy as jnp
import numpy as np
from jax import lax
from jax.experimental import pallas as pl
from jax.experimental.pallas import tpu as pltpu
from jax.sharding import Mesh
from jax.sharding import PartitionSpec as P

F32 = jnp.float32
RHS, ALPHA, BX, BY, BZ = range(5)
VMEM_BYTES = 20 * 2**20
ALL_VMEM = 62 * 2**20
RING = 8


def shifted(values, name, steps):
    count = lax.axis_size(name)
    lead, last = max(0, -steps), min(count, count - steps)
    return lax.ppermute(values, name, [(i, i + steps) for i in range(lead, last)])


def call(kernel, outs, scratch=(), copied=False):
    def run(*args):
        space = pltpu.HBM if copied else pltpu.VMEM
        buffers = [pltpu.VMEM(a.shape, F32) for a in args] if copied else []
        sems = [pltpu.SemaphoreType.DMA] * (2 * len(args)) if copied else []
        return pl.pallas_call(
            kernel,
            out_shape=[jax.ShapeDtypeStruct(s, F32) for s in outs],
            in_specs=[pl.BlockSpec(memory_space=space)] * len(args),
            out_specs=[pl.BlockSpec(memory_space=space)] * len(outs),
            scratch_shapes=[pltpu.VMEM(s, F32) for s in scratch] + buffers + sems,
            compiler_params=pltpu.CompilerParams(vmem_limit_bytes=ALL_VMEM if copied else VMEM_BYTES),
        )(*args)

    return run


def iotas(shape):
    return lax.broadcasted_iota(jnp.int32, shape, 0), lax.broadcasted_iota(jnp.int32, shape, 1)


def even_mask(shape):
    row, lane = iotas(shape)
    return ((row + lane) & 1) == 0


def half(x):
    return pltpu.roll(x, 4, 0)


def prev_row(x):
    return pltpu.roll(x, 1, 0)


def next_row(x):
    return pltpu.roll(x, x.shape[0] - 1, 0)


def prev_lane(x):
    return pltpu.roll(x, 1, 1)


def next_lane(x):
    return pltpu.roll(x, x.shape[1] - 1, 1)


def pick(values, chooser):
    parts, rest = [], values
    for _ in range(3):
        part = rest.astype(jnp.bfloat16)
        parts.append(part)
        rest = rest - part.astype(F32)
    total = jnp.dot(jnp.concatenate(parts, 0), chooser, preferred_element_type=F32)
    n = values.shape[0]
    return (total[2 * n :] + total[n : 2 * n]) + total[:n]


def pick_rows(chooser, values):
    parts, rest = [], values
    for _ in range(3):
        part = rest.astype(jnp.bfloat16)
        parts.append(jnp.dot(chooser, part, preferred_element_type=F32))
        rest = rest - part.astype(F32)
    return (parts[2] + parts[1]) + parts[0]


def one_hot(shape, test):
    row, col = iotas(shape)
    return jnp.where(test(row, col), 1.0, 0.0).astype(jnp.bfloat16)


def low_rows(shape):
    row, _ = iotas(shape)
    return (row & 7) < 4


def inverse_of(diagonal, cell):
    inside = cell > 0.0
    return jnp.where(inside, 1.0 / jnp.where(inside, diagonal, 1.0), 0.0)


def halves(q0, e0, e1):
    return jnp.where(q0, e0, e1), jnp.where(q0, e1, e0)


def clear_guards(r, b, n):
    for ref in (r, b):
        ref[0] = jnp.zeros_like(ref[0])
        ref[n + 1] = jnp.zeros_like(ref[n + 1])


S_R, S_B, WP, WO_R, WO_B, YM_R, YM_B, YP_R, YP_B, ZM_R, ZM_B, ZP_R, ZP_B, I_R, I_B, D_R, D_B = range(17)


def beside(co, src, p, red, q0):
    v = src[p + 1]
    before, after = src[p], src[p + 2]
    other = jnp.where(q0, before, after) if red else jnp.where(q0, after, before)
    wo, ym, yp, zm, zp = (
        (WO_R, YM_R, YP_R, ZM_R, ZP_R) if red else (WO_B, YM_B, YP_B, ZM_B, ZP_B)
    )
    total = co[WP, p] * v + co[wo, p] * other
    total = total + (co[ym, p] * prev_row(v) + co[yp, p] * next_row(v))
    return total + (co[zm, p] * prev_lane(v) + co[zp, p] * next_lane(v))


def relax(co, dst, src, pairs, red, q0):
    s, inv = (S_R, I_R) if red else (S_B, I_B)
    for p in pairs:
        dst[p + 1] = (co[s, p] + beside(co, src, p, red, q0)) * co[inv, p]


def first_red(co, dst, pairs):
    for p in pairs:
        dst[p + 1] = co[S_R, p] * co[I_R, p]


def residual(co, r, b, p, q0):
    red = co[S_R, p] - (co[D_R, p] * r[p + 1] - beside(co, b, p, True, q0))
    black = co[S_B, p] - (co[D_B, p] * b[p + 1] - beside(co, r, p, False, q0))
    return red, black


def put_faces(co, p, q0, bx, by, bz):
    b0, b1, b2 = bx
    wo_r, wo_b = halves(q0, b0, b2)
    y_r, y_b = halves(q0, *by)
    z_r, z_b = halves(q0, *bz)
    yp_r, yp_b = next_row(y_b), next_row(y_r)
    zp_r, zp_b = next_lane(z_b), next_lane(z_r)
    co[WP, p], co[WO_R, p], co[WO_B, p] = b1, wo_r, wo_b
    co[YM_R, p], co[YM_B, p], co[YP_R, p], co[YP_B, p] = y_r, y_b, yp_r, yp_b
    co[ZM_R, p], co[ZM_B, p], co[ZP_R, p], co[ZP_B, p] = z_r, z_b, zp_r, zp_b
    return (b1 + wo_r, b1 + wo_b), (y_r, y_b), (yp_r, yp_b), (z_r + zp_r, z_b + zp_b)


def smooth_cone(co, r, b, own, halo, q0):
    def pairs(reach):
        extra = min(halo, (reach + 1) // 2)
        return range(halo - extra, halo + own + extra)

    first_red(co, r, pairs(8))
    for step in range(2, 9):
        red = step % 2 == 1
        relax(co, r if red else b, b if red else r, pairs(9 - step), red, q0)


def to_windows_kernel(*refs):
    args, result, out, buffers, sems = refs[:5], refs[5], refs[6], refs[7:12], refs[12:]
    copies = [pltpu.make_async_copy(*c) for c in zip(args, buffers, sems[:5])]
    sends = [pltpu.make_async_copy(out.at[:, a], result.at[:, a], sems[5 + a]) for a in range(5)]
    for c in copies:
        c.start()
    _, lane = iotas((8, 128))
    zero = jnp.zeros((8, 128), F32)
    for a, ref in enumerate(buffers):
        copies[a].wait()
        for x in range(4):
            tiles = [ref[x, :, 128 * c : 128 * c + 128] for c in range(4)]
            up = [pltpu.roll(t, 32, 1) for t in tiles]
            down = [pltpu.roll(t, 96, 1) for t in tiles]
            for c in range(4):
                out[2 * c, a, x] = jnp.where(lane < 32, up[c - 1] if c else zero, up[c])
                out[2 * c + 1, a, x] = jnp.where(lane < 96, down[c], down[c + 1] if c < 3 else zero)
        sends[a].start()
    for c in sends:
        c.wait()


def flat(s, a, x):
    return (s * 5 + a) * 4 + x


def x_messages_kernel(own, to_low, to_high, first_by):
    for a in range(5):
        for x in range(4):
            for s in range(2):
                to_low[flat(s, a, x)] = own[s, a, x]
                to_high[flat(s, a, x)] = own[6 + s, a, x]
    to_low[40] = own[2, BX, 0]
    for x in range(32):
        first_by[x : x + 1] = own[x // 4, BY, x % 4][:1]


def corner_messages_kernel(low, high, to_low, to_high):
    keep = low_rows((8, 128))
    for a in range(5):
        for x in range(4):
            for ref in (to_low, to_high):
                ref[flat(0, a, x)] = low[flat(1, a, x)]
                ref[flat(1, a, x)] = high[flat(0, a, x)]
            outer_low, outer_high = low[flat(0, a, x)], high[flat(1, a, x)]
            to_low[flat(2, a, x)] = jnp.where(keep, outer_low, half(outer_high))
            to_high[flat(2, a, x)] = jnp.where(keep, half(outer_low), outer_high)


def fine_kernel(
    own, x_low, x_high, y_low, y_high, corner_low, corner_high, beyond_y, mid_coefs,
    fine_out, mid_first, mid_last, co, r, b,
):
    q0 = even_mask((24, 128))
    row, _ = iotas((24, 128))
    clear_guards(r, b, 24)
    zero = jnp.zeros((8, 128), F32)

    def plane(a, x):
        block, i = x // 4, x % 4
        if 2 <= block < 10:
            tiles = [ref[block - 2, a, i] for ref in (own, y_high, y_low)]
        elif block in (1, 10):
            side = int(block == 10)
            tiles = [(x_high if side else x_low)[flat(1 - side, a, i)]]
            tiles += [ref[flat(side, a, i)] for ref in (corner_high, corner_low)]
        else:
            up, down = corner_high[flat(2, a, i)], corner_low[flat(2, a, i)]
            if block == 0:
                tiles = [x_low[flat(0, a, i)], up, half(down)]
            else:
                tiles = [x_high[flat(1, a, i)], half(up), down]
        return jnp.concatenate(tiles, 0)

    bx0 = plane(BX, 0)
    for p in range(24):
        x = 2 * p
        co[S_R, p], co[S_B, p] = halves(q0, plane(RHS, x), plane(RHS, x + 1))
        bx1 = plane(BX, x + 1)
        bx2 = plane(BX, x + 2) if p < 23 else jnp.concatenate([x_high[40], zero, zero], 0)
        by = plane(BY, x), plane(BY, x + 1)
        bz = plane(BZ, x), plane(BZ, x + 1)
        fx, fy, fyp, fz = put_faces(co, p, q0, (bx0, bx1, bx2), by, bz)
        bx0 = bx2
        yp_r, yp_b = fyp
        if 4 <= p < 20:
            e0, e1 = beyond_y[x - 8 : x - 7], beyond_y[x - 7 : x - 6]
            up_r, up_b = halves(q0[15:16], e0, e1)
            yp_r = jnp.where(row == 15, up_r, yp_r)
            yp_b = jnp.where(row == 15, up_b, yp_b)
            co[YP_R, p], co[YP_B, p] = yp_r, yp_b
        a_r, a_b = halves(q0, plane(ALPHA, x), plane(ALPHA, x + 1))
        d_r = a_r + ((fx[0] + fz[0]) + (fy[0] + yp_r))
        d_b = a_b + ((fx[1] + fz[1]) + (fy[1] + yp_b))
        co[D_R, p], co[D_B, p] = d_r, d_b
        co[I_R, p], co[I_B, p] = inverse_of(d_r, a_r), inverse_of(d_b, a_b)
    smooth_cone(co, r, b, 16, 4, q0)
    sums = []
    for j in range(16):
        p = j + 4
        red, black = residual(co, r, b, p, q0)
        sums.append((red + black)[:8])
        fine_out[0, j] = r[p + 1][:8]
        fine_out[1, j] = b[p + 1][:8]
    along = pick(jnp.concatenate(sums, 0), one_hot((128, 128), lambda i, j: (i >> 1) == j))
    source = pick_rows(one_hot((64, 128), lambda i, j: (j >> 1) == i), along) * 0.125
    for t in range(4):
        out = mid_first if t < 2 else mid_last
        out[t % 2, 0] = mid_tile(source, t)
        for a in range(4):
            out[t % 2, a + 1] = mid_coefs[t, a]


def mid_tile(value, t):
    _, lane = iotas((8, 128))
    return jnp.where(lane < 64, value[16 * t : 16 * t + 8], pltpu.roll(value[16 * t + 8 : 16 * t + 16], 64, 1))


def low_rows_of(out_row, test):
    return one_hot((16, 8), lambda i, j: ((i >> 1) == out_row) & test(i & 1, j))


def coefficients_kernel(own, x_high, y_high, mid_coefs, mid_own, low_out):
    alphas, bys, nexts, bxs, bzs = [], [], [], [], []
    for j in range(16):
        s, x = j // 2, 2 * (j % 2)
        alphas.append(own[s, ALPHA, x] + own[s, ALPHA, x + 1])
        bys.append(own[s, BY, x] + own[s, BY, x + 1])
        nexts.append(y_high[s, BY, x] + y_high[s, BY, x + 1])
        bzs.append(own[s, BZ, x] + own[s, BZ, x + 1])
        bxs.append(own[s, BX, x])
    bxs.append(x_high[flat(0, BX, 0)])
    along = pick(
        jnp.concatenate(alphas + bys + nexts + bxs, 0), one_hot((128, 128), lambda i, j: (i >> 1) == j)
    )
    bz_z = pick(jnp.concatenate(bzs, 0), one_hot((128, 128), lambda i, j: i == 2 * j))
    y_sum = one_hot((64, 128), lambda i, j: (j >> 1) == i)
    y_even = one_hot((64, 128), lambda i, j: j == 2 * i)
    y_next = one_hot((64, 128), lambda i, j: ((i & 3) < 3) & (j == 2 * i + 2))
    y_last = one_hot((64, 128), lambda i, j: ((i & 3) == 3) & (j == 8 * (i >> 2)))
    alpha = pick_rows(y_sum, along[0:128]) * 0.125
    y_lower = pick_rows(y_even, along[128:256]) * 0.0625
    y_upper = (pick_rows(y_next, along[128:256]) + pick_rows(y_last, along[256:384])) * 0.0625
    x_lower = pick_rows(y_sum, along[384:512]) * 0.0625
    x_upper = pick_rows(y_sum, along[392:520]) * 0.0625
    z_lower = pick_rows(y_sum, bz_z) * 0.0625
    diagonal = alpha + ((x_lower + x_upper) + (y_lower + y_upper) + (z_lower + next_lane(z_lower)))
    sums = jnp.zeros((24, 128), F32)
    low_bz = jnp.zeros((8, 128), F32)
    for t in range(4):
        for a, value in enumerate((inverse_of(diagonal, alpha), x_lower, y_lower, z_lower)):
            mid_coefs[t, a] = mid_tile(value, t)
        mid_own[t] = mid_tile(diagonal, t)
        stack = jnp.concatenate([mid_tile(alpha, t), mid_coefs[t, 1], mid_coefs[t, 2]], 0)

        def chooser(test):
            def to(i, j):
                k = 2 * t + (i >> 6)
                return ((j >> 4) == k) & test(i & 63, j - 16 * k + 8)

            return one_hot((128, 128), to)

        sums += pick(stack, chooser(lambda i, j: (i >> 1) == j))
        low_bz += pick(mid_coefs[t, 3], chooser(lambda i, j: i == 2 * j))
    total = pick_rows(low_rows_of(0, lambda i, j: ((j & 3) >> 1) == i), sums[0:8]) * 0.125
    total += pick_rows(low_rows_of(1, lambda i, j: (j < 4) & ((j >> 1) == i)), sums[8:16]) * 0.0625
    total += pick_rows(low_rows_of(2, lambda i, j: (j & 3) == 2 * i), sums[16:24]) * 0.0625
    total += pick_rows(low_rows_of(3, lambda i, j: ((j & 3) >> 1) == i), low_bz) * 0.0625
    for k in range(4):
        low_out[k] = total[2 * k : 2 * k + 2]


def mid_message_kernel(low, first, last, high, out, inner):
    tiles = [ref[s] for ref in (low, first, last, high) for s in range(2)]
    for s in range(8):
        out[s] = tiles[s]
        if 0 < s < 7:
            inner[s - 1] = tiles[s]


def chip_message_kernel(other, inner, out):
    for s in range(8):
        out[s] = other[s]
    for s in range(6):
        out[8 + s] = inner[s]


def mid_kernel(mine, beside, across, beyond, own, low_coefs, level_out, low_out, co, r, b):
    upper = lax.rem(lax.axis_index("gy"), 2) == 1
    q0 = even_mask((24, 128))
    _, lane = iotas((8, 128))
    keep = low_rows((8, 128))
    zero = jnp.zeros((8, 128), F32)
    lower_core = lane < jnp.where(upper, 0, 128)
    clear_guards(r, b, 16)

    def part(tile, p):
        return jnp.where(lane < 64, pltpu.roll(tile, 64, 1) if p % 2 else tile, 0.0)

    def planes(p, a):
        t = p // 2
        c = part(mine[t, a], p)
        near = part(beside[t, a], p), part(across[t, a], p)
        h1, w1 = halves(lower_core, *near)
        h2, w2 = zero, zero
        if 0 < t < 7:
            far = part(beyond[t - 1, a], p), part(across[t + 7, a], p)
            h2, w2 = halves(lower_core, *far)
        e0 = [jnp.where(keep, c, half(h1)), jnp.where(keep, h2, 0.0), jnp.where(keep, w2, half(w1))]
        e1 = [jnp.where(keep, half(c), h1), jnp.where(keep, half(h2), 0.0), jnp.where(keep, half(w2), w1)]
        return jnp.concatenate(e0, 0), jnp.concatenate(e1, 0)

    bx0, bx1 = planes(0, 2)
    for p in range(16):
        co[S_R, p], co[S_B, p] = halves(q0, *planes(p, 0))
        co[I_R, p], co[I_B, p] = halves(q0, *planes(p, 1))
        n0, n1 = planes(p + 1, 2) if p < 15 else (jnp.zeros_like(bx0), bx1)
        put_faces(co, p, q0, (bx0, bx1, n0), planes(p, 3), planes(p, 4))
        bx0, bx1 = n0, n1
        if 4 <= p < 12:
            d = part(own[p // 2 - 2], p)
            d = jnp.concatenate([d, d, d], 0), jnp.concatenate([half(d)] * 3, 0)
            co[D_R, p], co[D_B, p] = halves(q0, *d)
    smooth_cone(co, r, b, 8, 4, q0)
    sums = []
    for k in range(8):
        red, black = residual(co, r, b, k + 4, q0)
        level_out[0, k] = r[k + 5][:8]
        level_out[1, k] = b[k + 5][:8]
        sums.append((red + black)[:8])
    along = pick(jnp.concatenate(sums, 0), one_hot((128, 128), lambda i, j: (i >> 1) == j))
    total = zero
    for k in range(8):
        moved = pltpu.roll(along[8 * k : 8 * k + 8], (16 * k - 8) % 128, 1)
        total = jnp.where((lane >> 4) == k, moved, total)
    source = pick_rows(low_rows_of(0, lambda i, j: (j < 4) & ((j >> 1) == i)), total)[:2] * 0.125
    coefs = [low_coefs[k] for k in range(4)]
    for j in range(low_out.shape[0]):
        low_out[j, 0] = source
        for k in range(4):
            low_out[j, k + 1] = coefs[k]


def whole_y_kernel(gathered, out):
    for g in range(out.shape[0]):
        for j in range(16):
            for k in range(5):
                out[g, 32 * k + 2 * j : 32 * k + 2 * j + 2] = gathered[16 * g + j, k]


def coarse_kernel(sweeps, low, own, high, level, fine, out, co, r, b, planes):
    shape = (32, 128)
    q0 = even_mask(shape)
    row, lane = iotas(shape)
    r[...] = jnp.zeros_like(r)
    b[...] = jnp.zeros_like(b)

    place_of = lane >> 4
    for a in range(5):
        for g in range(2):
            pieces = []
            for side in range(2):
                for s, ref in enumerate((low, own, high)):
                    block = ref[g + 2 * side, 32 * a : 32 * a + 32]
                    offset = 4 * side + s
                    pieces.append((offset, pltpu.roll(block, 16 * offset, 1) if offset else block))
            for k in range(8):
                total = jnp.zeros(shape, F32)
                for offset, piece in pieces:
                    total = jnp.where(place_of == (k + offset) % 8, piece, total)
                planes[a, 8 * g + k] = pltpu.roll(total, 128 - 16 * k, 1) if k else total

    def plane(a, i):
        return planes[a, i]

    first_bx = plane(2, 0)
    bx0 = first_bx
    for p in range(8):
        x = 2 * p
        co[S_R, p], co[S_B, p] = halves(q0, plane(0, x), plane(0, x + 1))
        bx1 = plane(2, x + 1)
        bx2 = plane(2, x + 2) if p < 7 else jnp.where(lane < 64, pltpu.roll(first_bx, 64, 1), 0.0)
        by, bz = (plane(3, x), plane(3, x + 1)), (plane(4, x), plane(4, x + 1))
        fx, fy, fyp, fz = put_faces(co, p, q0, (bx0, bx1, bx2), by, bz)
        bx0 = bx2
        yp_r, yp_b = jnp.where(row == 31, 0.0, fyp[0]), jnp.where(row == 31, 0.0, fyp[1])
        co[YP_R, p], co[YP_B, p] = yp_r, yp_b
        co[YM_R, p], co[YM_B, p] = jnp.where(row == 0, 0.0, fy[0]), jnp.where(row == 0, 0.0, fy[1])
        a_r, a_b = halves(q0, plane(1, x), plane(1, x + 1))
        d_r = a_r + ((fx[0] + fz[0]) + (fy[0] + yp_r))
        d_b = a_b + ((fx[1] + fz[1]) + (fy[1] + yp_b))
        co[I_R, p], co[I_B, p] = inverse_of(d_r, a_r), inverse_of(d_b, a_b)

    def join(ref):
        ref[0] = jnp.where(lane < 64, 0.0, pltpu.roll(ref[8], 64, 1))
        ref[9] = jnp.where(lane < 64, pltpu.roll(ref[1], 64, 1), 0.0)

    def sweep(step, carry):
        relax(co, b, r, range(8), False, q0)
        join(b)
        relax(co, r, b, range(8), True, q0)
        join(r)
        return carry

    first_red(co, r, range(8))
    join(r)
    lax.fori_loop(1, sweeps, sweep, 0)
    relax(co, b, r, range(8), False, q0)

    gy, ring, place = (lax.axis_index(name) for name in ("gy", "ring", "place"))
    side, base = ring // 2, 4 * lax.rem(ring, 2)
    parts = []
    for k in range(8):
        red, black = r[base + k // 2 + 1], b[base + k // 2 + 1]
        value = jnp.where(q0, red, black) if k % 2 == 0 else jnp.where(q0, black, red)
        value = pltpu.roll(value, lax.rem(32 - 2 * gy, 32), 0)
        parts.append(pltpu.roll(value, 64 * side, 1)[:8])
    q0 = even_mask((8, 128))
    row, lane = iotas((8, 128))
    up = pick(jnp.concatenate(parts, 0), one_hot((128, 128), lambda i, j: (j >> 1) + 8 == i))
    spread = one_hot((64, 64), lambda i, j: ((i >> 3) == (j >> 3)) & (((i & 3) >> 1) == (j & 7)))
    up = pick_rows(spread, up)
    mid = []
    for k in range(8):
        add = up[8 * k : 8 * k + 8]
        mid.extend(halves(q0, level[0, k] + add, level[1, k] + add))
        mine = pltpu.roll(parts[k], lax.rem(16 * place + 112, 128), 1)
        out[k, 2] = jnp.where(((lane >> 4) == place) & (row < 2), mine, 0.0)
    wide = pick(jnp.concatenate(mid, 0), one_hot((128, 128), lambda i, j: (j >> 1) == i))
    spread = one_hot((128, 128), lambda i, j: ((i >> 3) == (j >> 3)) & (((i & 7) >> 1) == (j & 7)))
    wide = pick_rows(spread, wide)
    for j in range(16):
        add = wide[8 * j : 8 * j + 8]
        e0, e1 = halves(q0, fine[0, j] + add, fine[1, j] + add)
        out[j // 2, j % 2] = jnp.where(lane < 64, pltpu.roll(e0, 96, 1), pltpu.roll(e1, 32, 1))


def finish_kernel(pieces, fine_out, coarse_out):
    _, lane = iotas((8, 128))
    for t in range(2):
        for c in range(4):
            a, b = pieces[2 * c, t], pieces[2 * c + 1, t]
            span = slice(128 * c, 128 * c + 128)
            fine_out[2 * t, :, span] = jnp.where(lane < 64, a, pltpu.roll(b, 64, 1))
            fine_out[2 * t + 1, :, span] = jnp.where(lane < 64, pltpu.roll(a, 64, 1), b)
    total = pieces[0, 2]
    for j in range(1, RING):
        total = total + pieces[j, 2]
    coarse_out[0] = total[:2]


def cycle(rhs, alpha, beta_x, beta_y, beta_z):
    rings, count_y = lax.axis_size("ring"), lax.axis_size("gy")

    (own,) = call(to_windows_kernel, [(RING, 5, 4, 8, 128)], [(RING, 5, 4, 8, 128)], copied=True)(rhs, alpha, beta_x, beta_y, beta_z)
    own = lax.all_to_all(own, "place", 0, 0, tiled=True)
    to_low, to_high, first_by = call(
        x_messages_kernel, [(41, 8, 128), (40, 8, 128), (32, 128)]
    )(own)
    x_low, x_high = shifted(to_high, "ring", 1), shifted(to_low, "ring", -1)
    y_low, y_high = shifted(own, "gy", 1), shifted(own, "gy", -1)
    beyond_y = shifted(first_by, "gy", -2)
    to_low, to_high = call(
        corner_messages_kernel, [(60, 8, 128), (60, 8, 128)]
    )(x_low, x_high)
    corner_low = shifted(to_high, "gy", 1)
    corner_high = shifted(to_low, "gy", -1)
    mid_coefs, mid_own, low_coefs = call(
        coefficients_kernel, [(4, 4, 8, 128), (4, 8, 128), (4, 2, 128)]
    )(own, x_high, y_high)
    fine, mid_first, mid_last = call(
        fine_kernel,
        [(2, 16, 8, 128), (2, 5, 8, 128), (2, 5, 8, 128)],
        [(17, 24, 24, 128), (26, 24, 128), (26, 24, 128)],
    )(own, x_low, x_high, y_low, y_high, corner_low, corner_high, beyond_y, mid_coefs)

    low, high = shifted(mid_last, "ring", 1), shifted(mid_first, "ring", -1)
    mid, inner = call(mid_message_kernel, [(8, 5, 8, 128), (6, 5, 8, 128)])(low, mid_first, mid_last, high)
    cores = [(i, i ^ 1) for i in range(count_y)]
    outward = [(i, i + 2 - 4 * (i % 2)) for i in range(count_y)]
    inward = [(j, i) for i, j in outward]
    chips, far = ([(i, j) for i, j in p if min(i, j) >= 0 and max(i, j) < count_y] for p in (outward, inward))
    beside = lax.ppermute(mid, "gy", cores)
    beyond = lax.ppermute(inner, "gy", far)
    (message,) = call(chip_message_kernel, [(14, 5, 8, 128)])(beside, inner)
    across = lax.ppermute(message, "gy", chips)
    level, low = call(
        mid_kernel,
        [(2, 8, 8, 128), (rings * count_y, 5, 2, 128)],
        [(17, 16, 24, 128), (18, 24, 128), (18, 24, 128)],
    )(mid, beside, across, beyond, mid_own, low_coefs)

    low = lax.all_to_all(low, ("ring", "gy"), 0, 0, tiled=True)
    (own,) = call(whole_y_kernel, [(rings, 160, 128)])(low)
    (pieces,) = call(
        lambda *refs: coarse_kernel(8, *refs),
        [(RING, 3, 8, 128)],
        [(17, 8, 32, 128), (10, 32, 128), (10, 32, 128), (5, 16, 32, 128)],
    )(shifted(own, "place", 1), own, shifted(own, "place", -1), level, fine)
    pieces = lax.all_to_all(pieces, "place", 0, 0, tiled=True)
    fine_solution, coarse = call(finish_kernel, [rhs.shape, (1, 2, 128)])(pieces)
    return fine_solution, coarse


def solution(mesh):
    count_x, count_y = mesh.devices.shape
    devices = np.array(mesh.devices).reshape(count_x // RING, RING, count_y)
    split = Mesh(devices, ("ring", "place", "gy"))
    placed = P(("ring", "place"), "gy", None)
    return jax.shard_map(
        cycle,
        mesh=split,
        in_specs=(placed,) * 5,
        out_specs=(placed, placed),
        check_vma=False,
    )
```
